32 devices in a mesh: grp: 2 (over y), row: 4 (over z), col: 2 (over x), sub: 2 (over core).
Axes of the slice: x: 2, y: 2, z: 4, core: 2. Of those that a mesh axis runs over, the one named last changes fastest.
Arguments:
- homolog_activations: bfloat16 [128, 192, 256], P(('grp', 'col', 'sub'), 'row'), parts along dimension 0, may hold values from -6 to 6
- edge_activations: bfloat16 [384, 192, 128], P(('grp', 'row', 'sub'), 'col'), parts along dimension 0, may hold values from -6 to 6
- first_projection_matrix: bfloat16 [256, 32], replicated, may hold values from -0.375 to 0.375
- second_projection_matrix: bfloat16 [256, 32], replicated, may hold values from -0.375 to 0.375
- tensor_product_matrix: bfloat16 [1024, 128], replicated, may hold values from -1.5 to 1.5
- multiplicative_entry_matrix: bfloat16 [128, 640], replicated, may hold values from -0.5 to 0.5
- multiplicative_exit_matrix: bfloat16 [128, 128], replicated, may hold values from -0.5 to 0.5
Outputs:
- pair_out: bfloat16 [384, 192, 128], P(('grp', 'row', 'sub'), 'col'), parts along dimension 0
The draws below stay inside these ranges and needn't reach their ends.
There are 2 independent parts, one for each index of `grp`. The reference program is written for one: setup_inputs(seed, part) draws one part's arguments, and reference() takes and returns one part's arrays. A program takes and returns all parts, laid end to end along the dimension named above; an argument that names none is the same for every part. Nothing has to cross between parts.
All inputs are finite; a program needn't handle non-finite values.
Results may differ from the reference program's by a relative error of at most 0.012.
Values may be sent and summed in bfloat16 or wider, within the bound.
No kernel may reach another device: no remote copies, remote signals or barrier semaphores. Data moves between devices by JAX's collectives and lax.ppermute only.
A program may use at most 128 MiB of HBM per device.

```python
import jax
import jax.numpy as jnp
from jax import lax

HOMOLOG_FEATURES = 256
PROJECTED_DIMS = 32
EDGE_FEATURES = 128
HOMOLOG_TOTAL = 64
WINDOW_AMINOS = 192
N_ROW = 4


def level_of(rng, shape, cuts, least, largest):
    def one(dim, shards_of):
        heights = jax.random.uniform(jax.random.fold_in(jax.random.fold_in(rng, 6), dim), (shards_of,), jnp.float32, least / len(cuts), largest / len(cuts))
        return jnp.repeat(jnp.exp(heights), shape[dim] // shards_of).reshape((-1,) + (1,) * (len(shape) - dim - 1))

    loudness = one(*cuts[0])
    for cut in cuts[1:]:
        loudness = loudness * one(*cut)
    return loudness


def normal_values(stream_key, shape, width, bound, shards=(), held_as=jnp.bfloat16):
    factor_of = level_of(stream_key, shape, shards, -0.22, 0.18) if shards else 1.0
    drawn = jax.random.normal(stream_key, shape, jnp.float32) * width * factor_of
    return jnp.minimum(jnp.maximum(drawn, -bound), bound).astype(held_as)


def setup_inputs(seed: int = 0, part: int = 0) -> dict:
    seeds = jax.random.split(jax.random.key(seed), 8)
    part_splits = jax.random.split(jax.random.fold_in(seeds[7], part), 8)
    homolog_activations = normal_values(part_splits[0], (HOMOLOG_TOTAL, WINDOW_AMINOS, HOMOLOG_FEATURES), 1.0, 6.0, ((0, 4), (1, 4)))
    edge_activations = normal_values(part_splits[1], (WINDOW_AMINOS, WINDOW_AMINOS, EDGE_FEATURES), 1.0, 6.0, ((0, 8), (1, 2)))
    first_projection_matrix = normal_values(seeds[2], (HOMOLOG_FEATURES, PROJECTED_DIMS), HOMOLOG_FEATURES ** -0.5, 0.375)
    second_projection_matrix = normal_values(seeds[3], (HOMOLOG_FEATURES, PROJECTED_DIMS), HOMOLOG_FEATURES ** -0.5, 0.375)
    tensor_product_matrix = normal_values(seeds[4], (PROJECTED_DIMS * PROJECTED_DIMS, EDGE_FEATURES), (max(1, PROJECTED_DIMS * PROJECTED_DIMS // HOMOLOG_TOTAL)) ** -0.5, 1.5)
    multiplicative_entry_matrix = normal_values(seeds[5], (EDGE_FEATURES, 5 * EDGE_FEATURES), EDGE_FEATURES ** -0.5, 0.5)
    multiplicative_exit_matrix = normal_values(seeds[6], (EDGE_FEATURES, EDGE_FEATURES), EDGE_FEATURES ** -0.5, 0.5)
    return dict(homolog_activations=homolog_activations, edge_activations=edge_activations, first_projection_matrix=first_projection_matrix, second_projection_matrix=second_projection_matrix, tensor_product_matrix=tensor_product_matrix, multiplicative_entry_matrix=multiplicative_entry_matrix, multiplicative_exit_matrix=multiplicative_exit_matrix)


EPSILON = 1e-05

def standardize_features(values):
    centred = values - lax.optimization_barrier(jnp.mean(values, axis=-1, keepdims=True))
    spread = lax.optimization_barrier(jnp.mean(centred * centred, axis=-1, keepdims=True))
    return centred * lax.rsqrt(spread + EPSILON)

def reference(homolog_activations, edge_activations, first_projection_matrix, second_projection_matrix, tensor_product_matrix, multiplicative_entry_matrix, multiplicative_exit_matrix):
    standardized_source = standardize_features(homolog_activations.astype(jnp.float32)).astype(jnp.bfloat16).reshape(HOMOLOG_TOTAL * WINDOW_AMINOS, HOMOLOG_FEATURES)
    first_projected_vector = jnp.dot(standardized_source, first_projection_matrix, preferred_element_type=jnp.float32).astype(jnp.bfloat16).reshape(HOMOLOG_TOTAL, WINDOW_AMINOS, PROJECTED_DIMS)
    second_projected_vector = jnp.dot(standardized_source, second_projection_matrix, preferred_element_type=jnp.float32).astype(jnp.bfloat16).reshape(HOMOLOG_TOTAL, WINDOW_AMINOS, PROJECTED_DIMS)
    residue_block = WINDOW_AMINOS // N_ROW
    second_projected_gathered = second_projected_vector.astype(jnp.float32)

    def row_block(index):
        block_offset = index * residue_block
        amino_lines = lax.dynamic_slice_in_dim(first_projected_vector, block_offset, residue_block, 1).astype(jnp.float32)
        contracted_result = jnp.einsum('vnq,vxh->nxqh', amino_lines, second_projected_gathered) / HOMOLOG_TOTAL
        contracted_result = contracted_result.astype(jnp.bfloat16).reshape(residue_block * WINDOW_AMINOS, PROJECTED_DIMS * PROJECTED_DIMS)
        base = lax.dynamic_slice_in_dim(edge_activations, block_offset, residue_block, 0).reshape(residue_block * WINDOW_AMINOS, EDGE_FEATURES).astype(jnp.float32)
        middle = (base + jnp.dot(contracted_result, tensor_product_matrix, preferred_element_type=jnp.float32)).astype(jnp.bfloat16)
        normed_mid = standardize_features(middle.astype(jnp.float32)).astype(jnp.bfloat16)
        projected = jnp.dot(normed_mid, multiplicative_entry_matrix, preferred_element_type=jnp.float32)
        left_tri = (jax.nn.sigmoid(projected[:, EDGE_FEATURES:2 * EDGE_FEATURES]) * projected[:, :EDGE_FEATURES]).astype(jnp.bfloat16)
        right_tri = (jax.nn.sigmoid(projected[:, 3 * EDGE_FEATURES:4 * EDGE_FEATURES]) * projected[:, 2 * EDGE_FEATURES:3 * EDGE_FEATURES]).astype(jnp.bfloat16)
        out_gate = jax.nn.sigmoid(projected[:, 4 * EDGE_FEATURES:])
        return (middle, left_tri, right_tri, out_gate)
    middles, lefts, rights, gates = lax.map(row_block, jnp.arange(WINDOW_AMINOS // residue_block, dtype=jnp.int32))
    lefts = lefts.reshape(WINDOW_AMINOS, WINDOW_AMINOS, EDGE_FEATURES)
    rights = rights.reshape(WINDOW_AMINOS, WINDOW_AMINOS, EDGE_FEATURES)
    tri = jnp.einsum('ikc,jkc->ijc', lefts.astype(jnp.float32), rights.astype(jnp.float32)).astype(jnp.bfloat16)
    tri_normed = standardize_features(tri.astype(jnp.float32)).astype(jnp.bfloat16).reshape(WINDOW_AMINOS * WINDOW_AMINOS, EDGE_FEATURES)
    update = jnp.dot(tri_normed, multiplicative_exit_matrix, preferred_element_type=jnp.float32)
    result = middles.reshape(WINDOW_AMINOS * WINDOW_AMINOS, EDGE_FEATURES).astype(jnp.float32) + gates.reshape(WINDOW_AMINOS * WINDOW_AMINOS, EDGE_FEATURES) * update
    return result.astype(jnp.bfloat16).reshape(WINDOW_AMINOS, WINDOW_AMINOS, EDGE_FEATURES)
```

```python
import functools
import jax, jax.numpy as jnp
from jax import lax
from jax.experimental import pallas as pl
from jax.experimental.pallas import tpu as pltpu
from jax.sharding import PartitionSpec as P
EPSILON = 1e-05
def ln0(x):
    m=jnp.mean(x,axis=0,keepdims=True); d=x-m
    v=jnp.mean(d*d,axis=0,keepdims=True)
    return d*lax.rsqrt(v+EPSILON)


def standardize_features(values):
    centred = values - jnp.mean(values, axis=-1, keepdims=True)
    spread = jnp.mean(centred * centred, axis=-1, keepdims=True)
    return centred * lax.rsqrt(spread + EPSILON)


def prep_kernel(fw, r_ref, rt_ref, sc):
    S, JB = r_ref.shape
    J = JB//fw
    blk = 128
    w = sc.shape[2]
    for u in range(S//w):
        for t in range(JB//blk):
            sc[u, t*blk:(t+1)*blk, :] = r_ref[u*w:(u+1)*w, t*blk:(t+1)*blk].astype(jnp.float32).T
        for b in range(fw):
            rt_ref[b, :, u*w:(u+1)*w] = sc[u, pl.ds(b, J, stride=fw), :].astype(jnp.bfloat16)

def prep(r, fw):
    S, JB = r.shape
    J = JB//fw
    w = min(S, 128)
    return pl.pallas_call(functools.partial(prep_kernel, fw),
      out_shape=jax.ShapeDtypeStruct((fw, J, S), jnp.bfloat16),
      in_specs=[pl.BlockSpec(memory_space=pltpu.VMEM)],
      out_specs=pl.BlockSpec(memory_space=pltpu.VMEM),
      scratch_shapes=[pltpu.VMEM((S//w, JB, w), jnp.float32)],
    )(r)

def a_kernel(cfg, l_ref, rt_ref, wt_ref, e_ref, went_ref, *rest):
    fw, C, TI, J, S = cfg
    mid_ref, gate_ref, lo_ref, ro_ref, lt, ot, lsc, rsc = rest
    g = pl.program_id(0)
    IG = l_ref.shape[1]//fw
    for t in range(IG*fw//128):
        lt[t*128:(t+1)*128,:] = l_ref[:, t*128:(t+1)*128].astype(jnp.float32).T.astype(jnp.bfloat16)
    ltv = lt[...]
    for b in range(fw):
        o = lax.dot_general(ltv, rt_ref[b], (((1,),(1,)),((),())), preferred_element_type=jnp.float32)
        ob = o.astype(jnp.bfloat16)
        for i in range(IG):
            ot[i, b*fw:(b+1)*fw, :] = ob[i*fw:(i+1)*fw, :]
    wt = wt_ref[...]; we = went_ref[...]
    for i in range(IG):
        pt = lax.dot_general(wt, ot[i], (((1,),(0,)),((),())), preferred_element_type=jnp.float32)
        et = e_ref[i].astype(jnp.float32).T
        mid = (et + pt*(1.0/S)).astype(jnp.bfloat16)
        mid_ref[i] = mid
        nt = ln0(mid.astype(jnp.float32)).astype(jnp.bfloat16)
        p = lax.dot_general(we, nt, (((1,),(0,)),((),())), preferred_element_type=jnp.float32)
        lsc[i] = jax.nn.sigmoid(p[C:2*C])*p[:C]
        rsc[i] = jax.nn.sigmoid(p[3*C:4*C])*p[2*C:3*C]
        gate_ref[i] = jax.nn.sigmoid(p[4*C:])
    lo_ref[...] = pltpu.einshape("icj->cij", lsc[...]).astype(jnp.bfloat16)
    ro_ref[...] = pltpu.einshape("icj->cij", rsc[...]).astype(jnp.bfloat16)

def a_call(l, rt, wt, e, went, IG=8):
    S,IA=l.shape; fw,J,_=rt.shape; TI=IA//fw; C=wt.shape[0]
    cfg=(fw,C,TI,J,S)
    f=pl.pallas_call(functools.partial(a_kernel,cfg), grid=(TI//IG,),
      out_shape=(jax.ShapeDtypeStruct((TI,C,J),jnp.bfloat16),jax.ShapeDtypeStruct((TI,C,J),jnp.float32),
                 jax.ShapeDtypeStruct((C,TI,J),jnp.bfloat16),jax.ShapeDtypeStruct((C,TI,J),jnp.bfloat16)),
      in_specs=[pl.BlockSpec((S,IG*fw),lambda g:(0,g)),
        pl.BlockSpec((fw,J,S),lambda g:(0,0,0)),pl.BlockSpec(wt.shape,lambda g:(0,0)),
        pl.BlockSpec((IG,J,C),lambda g:(g,0,0)),pl.BlockSpec(went.shape,lambda g:(0,0))],
      out_specs=(pl.BlockSpec((IG,C,J),lambda g:(g,0,0)),pl.BlockSpec((IG,C,J),lambda g:(g,0,0)),
        pl.BlockSpec((C,IG,J),lambda g:(0,g,0)),pl.BlockSpec((C,IG,J),lambda g:(0,g,0))),
      scratch_shapes=[pltpu.VMEM((IG*fw,S),jnp.bfloat16),pltpu.VMEM((IG,fw*fw,J),jnp.bfloat16),
        pltpu.VMEM((IG,C,J),jnp.float32),pltpu.VMEM((IG,C,J),jnp.float32)],
      compiler_params=pltpu.CompilerParams(vmem_limit_bytes=60*1024*1024),
    )
    return f(l,rt,wt,e,went)


def per_device(
    homolog_activations,
    edge_activations,
    first_projection_matrix,
    second_projection_matrix,
    tensor_product_matrix,
    multiplicative_entry_matrix,
    multiplicative_exit_matrix,
):
    homologs_each_device, aminos_each_device, homolog_column_extent = homolog_activations.shape
    tile_rows, tile_cols, width = edge_activations.shape
    factor_width = first_projection_matrix.shape[1]
    sub_count = lax.axis_size("sub")
    col_count = lax.axis_size("col")
    sub_index = lax.axis_index("sub")
    normalized_alignment = (
        standardize_features(homolog_activations.astype(jnp.float32))
        .astype(jnp.bfloat16)
        .reshape(homologs_each_device * aminos_each_device, homolog_column_extent)
    )
    left_factor_slice = jnp.dot(
        normalized_alignment, first_projection_matrix, preferred_element_type=jnp.float32
    ).astype(jnp.bfloat16)
    left_factor_slice = left_factor_slice.reshape(
        homologs_each_device, aminos_each_device * factor_width
    )
    right_factor_slice = jnp.dot(
        normalized_alignment, second_projection_matrix, preferred_element_type=jnp.float32
    ).astype(jnp.bfloat16)
    right_factor_slice = right_factor_slice.reshape(
        homologs_each_device, aminos_each_device * factor_width
    )
    right_residues = lax.all_gather(right_factor_slice, "row", axis=1, tiled=True)
    column_groups = right_residues.reshape(
        homologs_each_device, col_count, tile_cols * factor_width
    ).transpose(1, 0, 2)
    right_outgoing = jnp.broadcast_to(
        column_groups[:, None],
        (col_count, sub_count, homologs_each_device, tile_cols * factor_width),
    )
    right_outgoing = right_outgoing.reshape(
        col_count * sub_count, homologs_each_device, tile_cols * factor_width
    )
    right_all = lax.all_to_all(
        right_outgoing, ("col", "sub"), split_axis=0, concat_axis=1, tiled=True
    )[0]
    left_all = lax.all_gather(left_factor_slice, ("col", "sub"), axis=0, tiled=True)
    left_rows = lax.dynamic_slice_in_dim(
        left_all, sub_index * (tile_rows * factor_width), tile_rows * factor_width, 1
    )
    right_prepared = prep(right_all, factor_width)
    outer_weight = (
        tensor_product_matrix.reshape(factor_width, factor_width, width)
        .transpose(2, 1, 0)
        .reshape(width, factor_width * factor_width)
    )
    mid_t, gate_t, left_tile, right_tile = a_call(
        left_rows, right_prepared, outer_weight, edge_activations, multiplicative_entry_matrix.T
    )
    pair_mid = mid_t.transpose(0, 2, 1).reshape(tile_rows * tile_cols, width)
    out_gate = gate_t.transpose(0, 2, 1).reshape(tile_rows * tile_cols, width)
    left_chan, right_chan = (
        lax.all_to_all(left_tile, ("row", "sub"), split_axis=0, concat_axis=1, tiled=True),
        lax.all_to_all(right_tile, ("row", "sub"), split_axis=0, concat_axis=1, tiled=True),
    )
    right_block = lax.all_to_all(right_chan, "col", split_axis=1, concat_axis=2, tiled=True)
    channels = jnp.einsum(
        "gik,gjk->gij",
        lax.all_gather(left_chan, "col", axis=2, tiled=True),
        right_block,
        preferred_element_type=jnp.float32,
    ).astype(jnp.bfloat16)
    tiles = lax.all_to_all(channels, ("row", "sub"), split_axis=1, concat_axis=0, tiled=True)
    tri = tiles.transpose(1, 2, 0).reshape(tile_rows * tile_cols, width)
    tri_normed = standardize_features(tri.astype(jnp.float32)).astype(jnp.bfloat16)
    update = jnp.dot(tri_normed, multiplicative_exit_matrix, preferred_element_type=jnp.float32)
    result = (pair_mid.astype(jnp.float32) + out_gate * update).astype(jnp.bfloat16)
    return result.reshape(tile_rows, tile_cols, width)


def solution(mesh):
    in_specs = (
        P(("grp", "col", "sub"), "row", None),
        P(("grp", "row", "sub"), "col", None),
        P(),
        P(),
        P(),
        P(),
        P(),
    )
    out_specs = P(("grp", "row", "sub"), "col", None)
    return jax.shard_map(
        per_device, mesh=mesh, in_specs=in_specs, out_specs=out_specs, check_vma=False
    )
```

```python
import functools

import jax
import jax.numpy as jnp
from jax import lax
from jax.experimental import pallas as pl
from jax.experimental.pallas import tpu as pltpu
from jax.sharding import PartitionSpec as P

EPSILON = 1e-05
LANES = 128
VMEM_LIMIT = 60 * 1024 * 1024


def standardize_features(values):
    centred = values - jnp.mean(values, axis=-1, keepdims=True)
    spread = jnp.mean(centred * centred, axis=-1, keepdims=True)
    return centred * lax.rsqrt(spread + EPSILON)


def standardize_columns(values):
    centred = values - jnp.mean(values, axis=0, keepdims=True)
    spread = jnp.mean(centred * centred, axis=0, keepdims=True)
    return centred * lax.rsqrt(spread + EPSILON)


def vmem():
    return pl.BlockSpec(memory_space=pltpu.VMEM)


def smem():
    return pl.BlockSpec(memory_space=pltpu.SMEM)


def packing(count, cols):
    spare = -cols % LANES
    if spare and cols < LANES and cols % spare == 0:
        parts = cols // spare
        if count % (parts + 1) == 0:
            return parts, count // (parts + 1) * parts
    return 0, count


def lane_index(shape):
    return lax.broadcasted_iota(jnp.int32, shape, len(shape) - 1)


def prep_kernel(fw, own_ref, recv_ref, rt_ref, sc):
    groups, m, seqs, row_lanes = own_ref.shape
    res = row_lanes // fw
    chunk = sc.shape[2]
    pieces = [(ref, g) for ref in (own_ref, recv_ref) for g in range(groups)]
    per = chunk // seqs
    for u in range(len(pieces) // per):
        for mm in range(m):
            for t in range(row_lanes // LANES):
                block = jnp.concatenate(
                    [ref[g, mm, :, t * LANES : (t + 1) * LANES].astype(jnp.float32) for ref, g in pieces[u * per : (u + 1) * per]], axis=0
                )
                start = mm * row_lanes + t * LANES
                sc[u, start : start + LANES, :] = block.T
        for b in range(fw):
            rt_ref[b, :, u * chunk : (u + 1) * chunk] = sc[u, pl.ds(b, m * res, stride=fw), :].astype(jnp.bfloat16)


def prep(own, recv, fw):
    groups, m, seqs, row_lanes = own.shape
    total = 2 * groups * seqs
    chunk = min(total, LANES)
    cols = m * row_lanes // fw
    return pl.pallas_call(
        functools.partial(prep_kernel, fw),
        out_shape=jax.ShapeDtypeStruct((fw, cols, total), jnp.bfloat16),
        in_specs=[vmem(), vmem()],
        out_specs=vmem(),
        scratch_shapes=[pltpu.VMEM((total // chunk, m * row_lanes, chunk), jnp.float32)],
    )(own, recv)


def pair_kernel(cfg, sub_ref, l_ref, rt_ref, wt_ref, e_ref, went_ref, mid_ref, gate_ref, lk_ref, ls_ref, rk_ref, rs_ref, lt, ot, lsc, rsc):
    fw, C, J, S = cfg
    half = lk_ref.shape[0]
    IG = l_ref.shape[1] // fw
    for t in range(IG * fw // LANES):
        lt[t * LANES : (t + 1) * LANES, :] = l_ref[:, t * LANES : (t + 1) * LANES].astype(jnp.float32).T.astype(jnp.bfloat16)
    ltv = lt[...]
    for b in range(fw):
        o = lax.dot_general(ltv, rt_ref[b], (((1,), (1,)), ((), ())), preferred_element_type=jnp.float32).astype(jnp.bfloat16)
        for i in range(IG):
            ot[i, b * fw : (b + 1) * fw, :] = o[i * fw : (i + 1) * fw, :]
    wt = wt_ref[...]
    we = went_ref[...]
    for i in range(IG):
        pt = lax.dot_general(wt, ot[i], (((1,), (0,)), ((), ())), preferred_element_type=jnp.float32)
        et = e_ref[i].astype(jnp.float32).T
        mid = (et + pt * (1.0 / S)).astype(jnp.bfloat16)
        mid_ref[i] = mid
        nt = standardize_columns(mid.astype(jnp.float32)).astype(jnp.bfloat16)
        p = lax.dot_general(we, nt, (((1,), (0,)), ((), ())), preferred_element_type=jnp.float32)
        lsc[pl.ds(i * C, C), :J] = jax.nn.sigmoid(p[C : 2 * C]) * p[:C]
        rsc[pl.ds(i * C, C), :J] = jax.nn.sigmoid(p[3 * C : 4 * C]) * p[2 * C : 3 * C]
        gate_ref[i] = jax.nn.sigmoid(p[4 * C :])
    sub = sub_ref[0]
    parts, main = packing(half, J)
    inside = lane_index((IG, LANES)) < J
    for ref, base in ((lk_ref, sub * half), (ls_ref, (1 - sub) * half)):
        for ch in range(half):
            x = lsc[pl.ds(base + ch, IG, stride=C), :]
            ref[ch] = jnp.where(inside, x, 0.0).astype(jnp.bfloat16)
    for ref, base in ((rk_ref, sub * half), (rs_ref, (1 - sub) * half)):
        if parts == 0:
            for ch in range(half):
                x = rsc[pl.ds(base + ch, IG, stride=C), :]
                ref[ch] = jnp.where(inside, x, 0.0).astype(jnp.bfloat16)
        else:
            tails = half - main
            spare = LANES - J
            for q in range(tails):
                tail = rsc[pl.ds(base + main + q, IG, stride=C), :]
                for t in range(parts):
                    x = rsc[pl.ds(base + t * tails + q, IG, stride=C), :]
                    moved = pltpu.roll(tail, J - spare * t, 1)
                    ref[t * tails + q] = jnp.where(inside, x, moved).astype(jnp.bfloat16)


def pair(sub, l, rt, wt, e, went, IG):
    S, IA = l.shape
    fw, J, _ = rt.shape
    TI = IA // fw
    C = wt.shape[0]
    half = C // 2
    rows = packing(half, J)[1]
    bf = jnp.bfloat16
    f = pl.pallas_call(
        functools.partial(pair_kernel, (fw, C, J, S)),
        grid=(TI // IG,),
        out_shape=(
            jax.ShapeDtypeStruct((TI, C, J), bf),
            jax.ShapeDtypeStruct((TI, C, J), jnp.float32),
            jax.ShapeDtypeStruct((half, TI, LANES), bf),
            jax.ShapeDtypeStruct((half, TI, LANES), bf),
            jax.ShapeDtypeStruct((rows, TI, LANES), bf),
            jax.ShapeDtypeStruct((rows, TI, LANES), bf),
        ),
        in_specs=[
            smem(),
            pl.BlockSpec((S, IG * fw), lambda g: (0, g)),
            pl.BlockSpec((fw, J, S), lambda g: (0, 0, 0)),
            pl.BlockSpec(wt.shape, lambda g: (0, 0)),
            pl.BlockSpec((IG, J, C), lambda g: (g, 0, 0)),
            pl.BlockSpec(went.shape, lambda g: (0, 0)),
        ],
        out_specs=(
            pl.BlockSpec((IG, C, J), lambda g: (g, 0, 0)),
            pl.BlockSpec((IG, C, J), lambda g: (g, 0, 0)),
            pl.BlockSpec((half, IG, LANES), lambda g: (0, g, 0)),
            pl.BlockSpec((half, IG, LANES), lambda g: (0, g, 0)),
            pl.BlockSpec((rows, IG, LANES), lambda g: (0, g, 0)),
            pl.BlockSpec((rows, IG, LANES), lambda g: (0, g, 0)),
        ),
        scratch_shapes=[
            pltpu.VMEM((IG * fw, S), bf),
            pltpu.VMEM((IG, fw * fw, J), bf),
            pltpu.VMEM((IG * C, LANES), jnp.float32),
            pltpu.VMEM((IG * C, LANES), jnp.float32),
        ],
        compiler_params=pltpu.CompilerParams(vmem_limit_bytes=VMEM_LIMIT),
        cost_estimate=pl.CostEstimate(flops=2 * TI * J * (S * fw * fw + fw * fw * C + 5 * C * C), bytes_accessed=4 * TI * J * C * 6, transcendentals=TI * J * C * 3),
    )
    return f(sub, l, rt, wt, e, went)


def tri_kernel(cfg, n_slots, pos_ref, lk_ref, lr_ref, *rest):
    nr, nc, m, J = cfg
    slots = rest[:n_slots]
    outs = rest[n_slots : n_slots + 2 * nc]
    rv, lm, sem = rest[n_slots + 2 * nc :]
    half, TI, _ = lk_ref.shape
    row, col, sub = pos_ref[0], pos_ref[1], pos_ref[2]
    parts, main = packing(half, J)
    tails = half - main
    spare = LANES - J

    def copy(index):
        step, u = index // 2, index % 2
        hop = (step + 1) // 2
        origin = row - hop if step % 2 else row + hop
        return origin, pltpu.make_async_copy(slots[index], rv.at[jnp.clip(origin, 0, nr - 1), sub if u == 0 else 1 - sub], sem.at[index])

    for index in range(n_slots):
        origin, c = copy(index)

        @pl.when((origin >= 0) & (origin < nr))
        def _(c=c):
            c.start()

    inside = lane_index((2 * TI, LANES)) < J
    for ch in range(half):
        x = jnp.concatenate([lk_ref[ch], lr_ref[ch]], axis=0)
        if ch < main:
            lm[ch] = x
        else:
            f = x.astype(jnp.float32)
            for t in range(parts):
                moved = pltpu.roll(f, J - spare * t, 1)
                lm[main + (ch - main) * parts + t] = jnp.where(inside, 0.0, moved).astype(jnp.bfloat16)

    for index in range(n_slots):
        origin, c = copy(index)

        @pl.when((origin >= 0) & (origin < nr))
        def _(c=c):
            c.wait()

    def block(ch, start, pieces):
        right = rv[pl.ds(start, m), :, ch].reshape(m * 2 * TI, LANES)
        return lax.dot_general(lm[pieces], right, (((1,), (1,)), ((), ())), preferred_element_type=jnp.float32)

    for dc in range(nc):
        start = lax.rem(col + dc, nc) * m
        own_ref, other_ref = outs[2 * dc], outs[2 * dc + 1]
        for q in range(tails if parts else 0):
            tail = 0.0
            for t in range(parts):
                tail = tail + block(t * tails + q, start, main + q * parts + t)
            tail = jnp.concatenate([tail, jnp.zeros((2 * TI, spare), jnp.float32)], axis=1)
            for t in range(parts):
                x = block(t * tails + q, start, t * tails + q)
                x = jnp.concatenate([x, jnp.zeros((2 * TI, spare), jnp.float32)], axis=1)
                x = jnp.where(inside, x, pltpu.roll(tail, J - spare * t, 1)).astype(jnp.bfloat16)
                own_ref[t * tails + q] = x[:TI]
                other_ref[t * tails + q] = x[TI:]
        if not parts:
            for ch in range(half):
                x = block(ch, start, ch)
                if spare:
                    x = jnp.concatenate([x, jnp.zeros((2 * TI, spare), jnp.float32)], axis=1)
                x = x.astype(jnp.bfloat16)
                own_ref[ch] = x[:TI]
                other_ref[ch] = x[TI:]


def triangle(pos, lk, lr, slots, nr, nc, m, J):
    half, TI, _ = lk.shape
    parts, main = packing(half, J)
    rows = main
    bf = jnp.bfloat16
    n = len(slots)
    return pl.pallas_call(
        functools.partial(tri_kernel, (nr, nc, m, J), n),
        out_shape=[jax.ShapeDtypeStruct((rows, TI, LANES), bf)] * (2 * nc),
        in_specs=[smem(), vmem(), vmem()] + [pl.BlockSpec(memory_space=pl.ANY)] * n,
        out_specs=[vmem()] * (2 * nc),
        scratch_shapes=[
            pltpu.VMEM((nr, 2, rows, TI, LANES), bf),
            pltpu.VMEM((main + (half - main) * max(parts, 1), 2 * TI, LANES), bf),
            pltpu.SemaphoreType.DMA((n,)),
        ],
        compiler_params=pltpu.CompilerParams(vmem_limit_bytes=VMEM_LIMIT),
    )(pos, lk, lr, *slots)


def final_kernel(cfg, n, sub_ref, *rest):
    C, J = cfg
    own = rest[:n]
    other = rest[n : 2 * n]
    mid_ref, gate_ref, wx_ref, out_ref, sc = rest[2 * n :]
    TI = mid_ref.shape[0]
    half = C // 2
    parts, main = packing(half, J)
    tails = half - main
    spare = LANES - J
    sub = sub_ref[0]
    lanes = lane_index((TI, LANES))
    for refs, base in ((own, sub * half), (other, (1 - sub) * half)):
        def total(ch, refs=refs):
            x = refs[0][ch].astype(jnp.float32)
            for ref in refs[1:]:
                x = x + ref[ch].astype(jnp.float32)
            return x.astype(jnp.bfloat16).astype(jnp.float32)

        for q in range(tails if parts else 0):
            tail = jnp.zeros((TI, LANES), jnp.float32)
            for t in range(parts):
                x = total(t * tails + q)
                sc[pl.ds((base + t * tails + q) * TI, TI), :] = x
                tail = jnp.where((lanes >= spare * t) & (lanes < spare * (t + 1)), pltpu.roll(x, LANES - J + spare * t, 1), tail)
            sc[pl.ds((base + main + q) * TI, TI), :] = tail
        if not parts:
            for ch in range(half):
                sc[pl.ds((base + ch) * TI, TI), :] = total(ch)
    wx = wx_ref[...]
    for i in range(TI):
        tri = sc[pl.ds(i, C, stride=TI), :][:, :J]
        normed = standardize_columns(tri).astype(jnp.bfloat16)
        update = lax.dot_general(wx, normed, (((1,), (0,)), ((), ())), preferred_element_type=jnp.float32)
        res = mid_ref[i].astype(jnp.float32) + gate_ref[i] * update
        out_ref[i] = res.T.astype(jnp.bfloat16)


def final(sub, own, other, mid, gate, wx):
    TI, C, J = mid.shape
    n = len(own)
    return pl.pallas_call(
        functools.partial(final_kernel, (C, J), n),
        out_shape=jax.ShapeDtypeStruct((TI, J, C), jnp.bfloat16),
        in_specs=[smem()] + [vmem()] * (2 * n + 3),
        out_specs=vmem(),
        scratch_shapes=[pltpu.VMEM((C * TI, LANES), jnp.float32)],
        compiler_params=pltpu.CompilerParams(vmem_limit_bytes=VMEM_LIMIT),
    )(sub, *own, *other, mid, gate, wx)


def shift(x, axis, d):
    n = lax.axis_size(axis)
    return lax.ppermute(x, axis, [(i, (i + d) % n) for i in range(n)])


def step_along(x, axis, d):
    n = lax.axis_size(axis)
    return lax.ppermute(x, axis, [(i, i + d) for i in range(n) if 0 <= i + d < n])


def per_device(
    homolog_activations,
    edge_activations,
    first_projection_matrix,
    second_projection_matrix,
    tensor_product_matrix,
    multiplicative_entry_matrix,
    multiplicative_exit_matrix,
):
    seqs, residues, features = homolog_activations.shape
    tile_rows, tile_cols, width = edge_activations.shape
    fw = first_projection_matrix.shape[1]
    nr, nc, ns = (lax.axis_size(a) for a in ("row", "col", "sub"))
    assert ns == 2
    row, col, sub = (lax.axis_index(a) for a in ("row", "col", "sub"))
    pos = jnp.stack([row, col, sub]).astype(jnp.int32)
    sub_id = pos[2:]
    m = tile_cols // residues

    normed = standardize_features(homolog_activations.astype(jnp.float32)).astype(jnp.bfloat16).reshape(seqs * residues, features)

    def project(matrix):
        return jnp.dot(normed, matrix, preferred_element_type=jnp.float32).astype(jnp.bfloat16).reshape(seqs, residues * fw)

    right = project(second_projection_matrix)
    left = project(first_projection_matrix)

    rows = jnp.stack([right] + [shift(right, "row", d) for d in range(1, nr)])

    def rows_of(c):
        return jnp.stack([lax.dynamic_index_in_dim(rows, lax.rem(row - (c * m + t) + nr, nr), 0, keepdims=False) for t in range(m)])

    rights, lefts = [rows_of(col)], [left]
    for d in range(1, nc):
        rights.append(shift(rows_of(lax.rem(col + d, nc)), "col", d))
        lefts.append(shift(left, "col", d))
    rights = jnp.stack(rights)
    lefts = jnp.concatenate(lefts, axis=0)
    rights_other = shift(rights, "sub", 1)
    span = tile_rows * fw
    left_own = lax.dynamic_slice_in_dim(lefts, sub * span, span, 1)
    left_other = shift(lax.dynamic_slice_in_dim(lefts, (1 - sub) * span, span, 1), "sub", 1)
    left_rows = jnp.concatenate([left_own, left_other], axis=0)
    right_t = prep(rights, rights_other, fw)

    outer_weight = tensor_product_matrix.reshape(fw, fw, width).transpose(2, 1, 0).reshape(width, fw * fw)
    mid, gate, lk, ls, rk, rs = pair(sub_id, left_rows, right_t, outer_weight, edge_activations, multiplicative_entry_matrix.T, 8)

    rr = shift(rs, "sub", 1)
    lr = shift(ls, "sub", 1)
    slots = [rk, rr]
    up, down = [rk, rr], [rk, rr]
    for _ in range(1, nr):
        up = [step_along(x, "row", 1) for x in up]
        down = [step_along(x, "row", -1) for x in down]
        slots += up + down
    partial = triangle(pos, lk, lr, slots, nr, nc, m, tile_cols)

    own, other = [partial[0]], [shift(partial[1], "sub", 1)]
    for d in range(1, nc):
        own.append(shift(partial[2 * d], "col", d))
        other.append(lax.ppermute(partial[2 * d + 1], ("col", "sub"), [(c * 2 + s, (c + d) % nc * 2 + 1 - s) for c in range(nc) for s in range(2)]))
    return final(sub_id, own, other, mid, gate, multiplicative_exit_matrix.T)


def solution(mesh):
    in_specs = (
        P(("grp", "col", "sub"), "row", None),
        P(("grp", "row", "sub"), "col", None),
        P(),
        P(),
        P(),
        P(),
        P(),
    )
    out_specs = P(("grp", "row", "sub"), "col", None)
    return jax.shard_map(per_device, mesh=mesh, in_specs=in_specs, out_specs=out_specs, check_vma=False)
```

```python
import functools

import jax
import jax.numpy as jnp
from jax import lax
from jax.experimental import pallas as pl
from jax.experimental.pallas import tpu as pltpu
from jax.sharding import PartitionSpec as P

EPSILON = 1e-05
LANES = 128
VMEM_LIMIT = 60 * 1024 * 1024


def standardize_features(values):
    centred = values - jnp.mean(values, axis=-1, keepdims=True)
    spread = jnp.mean(centred * centred, axis=-1, keepdims=True)
    return centred * lax.rsqrt(spread + EPSILON)


def standardize_columns(values):
    centred = values - jnp.mean(values, axis=0, keepdims=True)
    spread = jnp.mean(centred * centred, axis=0, keepdims=True)
    return centred * lax.rsqrt(spread + EPSILON)


def vmem():
    return pl.BlockSpec(memory_space=pltpu.VMEM)


def smem():
    return pl.BlockSpec(memory_space=pltpu.SMEM)


def packing(count, cols):
    spare = -cols % LANES
    if spare and cols < LANES and cols % spare == 0:
        parts = cols // spare
        if count % (parts + 1) == 0:
            return parts, count // (parts + 1) * parts
    return 0, count


def lane_index(shape):
    return lax.broadcasted_iota(jnp.int32, shape, len(shape) - 1)


def prep_kernel(fw, own_ref, recv_ref, rt_ref, sc):
    groups, m, seqs, row_lanes = own_ref.shape
    res = row_lanes // fw
    chunk = sc.shape[2]
    pieces = [(ref, g) for ref in (own_ref, recv_ref) for g in range(groups)]
    per = chunk // seqs
    for u in range(len(pieces) // per):
        for mm in range(m):
            for t in range(row_lanes // LANES):
                block = jnp.concatenate(
                    [ref[g, mm, :, t * LANES : (t + 1) * LANES].astype(jnp.float32) for ref, g in pieces[u * per : (u + 1) * per]], axis=0
                )
                start = mm * row_lanes + t * LANES
                sc[u, start : start + LANES, :] = block.T
        for b in range(fw):
            rt_ref[b, :, u * chunk : (u + 1) * chunk] = sc[u, pl.ds(b, m * res, stride=fw), :].astype(jnp.bfloat16)


def prep(own, recv, fw):
    groups, m, seqs, row_lanes = own.shape
    total = 2 * groups * seqs
    chunk = min(total, LANES)
    cols = m * row_lanes // fw
    return pl.pallas_call(
        functools.partial(prep_kernel, fw),
        out_shape=jax.ShapeDtypeStruct((fw, cols, total), jnp.bfloat16),
        in_specs=[vmem(), vmem()],
        out_specs=vmem(),
        scratch_shapes=[pltpu.VMEM((total // chunk, m * row_lanes, chunk), jnp.float32)],
    )(own, recv)


def pair_kernel(cfg, sub_ref, l_ref, rt_ref, wt_ref, e_ref, went_ref, *rest):
    fw, C, J, S, full = cfg
    if full:
        mid_ref, gate_ref, lk_ref, ls_ref, rk_ref, rs_ref, lt, ot, nts, lsc, rsc = rest
    else:
        rk_ref, rs_ref, lt, ot, nts, rsc = rest
    half = C // 2
    IG = l_ref.shape[1] // fw
    wide = ot.shape[2] // 2
    for t in range(IG * fw // LANES):
        lt[t * LANES : (t + 1) * LANES, :] = l_ref[:, t * LANES : (t + 1) * LANES].astype(jnp.float32).T.astype(jnp.bfloat16)
    ltv = lt[...]
    for b in range(fw):
        o = lax.dot_general(ltv, rt_ref[b], (((1,), (1,)), ((), ())), preferred_element_type=jnp.float32).astype(jnp.bfloat16)
        for i in range(IG):
            ot[i // 2, b * fw : (b + 1) * fw, i % 2 * wide : i % 2 * wide + J] = o[i * fw : (i + 1) * fw, :]
    wt = wt_ref[...]
    for h in range(IG // 2):
        pt = lax.dot_general(wt, ot[h], (((1,), (0,)), ((), ())), preferred_element_type=jnp.float32)
        for k in range(2):
            i = 2 * h + k
            et = e_ref[i].astype(jnp.float32).T
            mid = (et + pt[:, k * wide : k * wide + J] * (1.0 / S)).astype(jnp.bfloat16)
            if full:
                mid_ref[i] = mid
            nts[h, :, k * wide : k * wide + J] = standardize_columns(mid.astype(jnp.float32)).astype(jnp.bfloat16)

    def project(first, count, h):
        return lax.dot_general(went_ref[first * C : (first + count) * C, :], nts[h], (((1,), (0,)), ((), ())), preferred_element_type=jnp.float32)

    for h in range(IG // 2):
        if full:
            p = project(0, 2, h)
            x = jax.nn.sigmoid(p[C:]) * p[:C]
            for k in range(2):
                lsc[pl.ds((2 * h + k) * C, C), :J] = x[:, k * wide : k * wide + J]
        p = project(2, 2, h)
        x = jax.nn.sigmoid(p[C:]) * p[:C]
        for k in range(2):
            rsc[pl.ds((2 * h + k) * C, C), :J] = x[:, k * wide : k * wide + J]
        if full:
            x = jax.nn.sigmoid(project(4, 1, h)).astype(jnp.bfloat16)
            for k in range(2):
                gate_ref[2 * h + k] = x[:, k * wide : k * wide + J]
    sub = sub_ref[0]
    parts, main = packing(half, J)
    inside = lane_index((IG, LANES)) < J
    if full:
        for ref, base in ((lk_ref, sub * half), (ls_ref, (1 - sub) * half)):
            for ch in range(half):
                x = lsc[pl.ds(base + ch, IG, stride=C), :]
                ref[ch] = jnp.where(inside, x, 0.0).astype(jnp.bfloat16)
    for ref, base in ((rk_ref, sub * half), (rs_ref, (1 - sub) * half)):
        if parts == 0:
            for ch in range(half):
                x = rsc[pl.ds(base + ch, IG, stride=C), :]
                ref[ch] = jnp.where(inside, x, 0.0).astype(jnp.bfloat16)
        else:
            tails = half - main
            spare = LANES - J
            for q in range(tails):
                tail = rsc[pl.ds(base + main + q, IG, stride=C), :]
                for t in range(parts):
                    x = rsc[pl.ds(base + t * tails + q, IG, stride=C), :]
                    moved = pltpu.roll(tail, J - spare * t, 1)
                    ref[t * tails + q] = jnp.where(inside, x, moved).astype(jnp.bfloat16)


def pair(sub, l, rt, wt, e, went, IG, full=True):
    S, IA = l.shape
    fw, J, _ = rt.shape
    TI = IA // fw
    C = wt.shape[0]
    half = C // 2
    rows = packing(half, J)[1]
    wide = -(-J // LANES) * LANES
    bf = jnp.bfloat16
    tile = (jax.ShapeDtypeStruct((TI, C, J), bf), pl.BlockSpec((IG, C, J), lambda g: (g, 0, 0)))
    lefts = (jax.ShapeDtypeStruct((half, TI, LANES), bf), pl.BlockSpec((half, IG, LANES), lambda g: (0, g, 0)))
    rights = (jax.ShapeDtypeStruct((rows, TI, LANES), bf), pl.BlockSpec((rows, IG, LANES), lambda g: (0, g, 0)))
    outs = ([tile] * 2 + [lefts] * 2 if full else []) + [rights] * 2
    gated = pltpu.VMEM((IG * C, LANES), jnp.float32)
    f = pl.pallas_call(
        functools.partial(pair_kernel, (fw, C, J, S, full)),
        grid=(TI // IG,),
        out_shape=[o[0] for o in outs],
        in_specs=[
            smem(),
            pl.BlockSpec((S, IG * fw), lambda g: (0, g)),
            pl.BlockSpec((fw, J, S), lambda g: (0, 0, 0)),
            pl.BlockSpec(wt.shape, lambda g: (0, 0)),
            pl.BlockSpec((IG, J, C), lambda g: (g, 0, 0)),
            pl.BlockSpec(went.shape, lambda g: (0, 0)),
        ],
        out_specs=[o[1] for o in outs],
        scratch_shapes=[
            pltpu.VMEM((IG * fw, S), bf),
            pltpu.VMEM((IG // 2, fw * fw, 2 * wide), bf),
            pltpu.VMEM((IG // 2, C, 2 * wide), bf),
            gated,
        ]
        + ([gated] if full else []),
        compiler_params=pltpu.CompilerParams(vmem_limit_bytes=VMEM_LIMIT),
        cost_estimate=pl.CostEstimate(flops=2 * TI * J * (S * fw * fw + fw * fw * C + 5 * C * C), bytes_accessed=4 * TI * J * C * 6, transcendentals=TI * J * C * 3),
    )
    return f(sub, l, rt, wt, e, went)


def tri_kernel(cfg, n_slots, pos_ref, lk_ref, lr_ref, *rest):
    nr, nc, m, J = cfg
    slots = rest[:n_slots]
    outs = rest[n_slots : n_slots + 2 * nc]
    rv, lm, sem = rest[n_slots + 2 * nc :]
    half, TI, _ = lk_ref.shape
    row, col, sub = pos_ref[0], pos_ref[1], pos_ref[2]
    parts, main = packing(half, J)
    tails = half - main
    spare = LANES - J

    def copy(index):
        step, u = index // 2, index % 2
        hop = (step + 1) // 2
        origin = row - hop if step % 2 else row + hop
        return origin, pltpu.make_async_copy(slots[index], rv.at[jnp.clip(origin, 0, nr - 1), sub if u == 0 else 1 - sub], sem.at[index])

    for index in range(n_slots):
        origin, c = copy(index)

        @pl.when((origin >= 0) & (origin < nr))
        def _(c=c):
            c.start()

    inside = lane_index((2 * TI, LANES)) < J
    for ch in range(half):
        x = jnp.concatenate([lk_ref[ch], lr_ref[ch]], axis=0)
        if ch < main:
            lm[ch] = x
        else:
            f = x.astype(jnp.float32)
            for t in range(parts):
                moved = pltpu.roll(f, J - spare * t, 1)
                lm[main + (ch - main) * parts + t] = jnp.where(inside, 0.0, moved).astype(jnp.bfloat16)

    for index in range(n_slots):
        origin, c = copy(index)

        @pl.when((origin >= 0) & (origin < nr))
        def _(c=c):
            c.wait()

    def block(ch, start, pieces):
        right = rv[pl.ds(start, m), :, ch].reshape(m * 2 * TI, LANES)
        return lax.dot_general(lm[pieces], right, (((1,), (1,)), ((), ())), preferred_element_type=jnp.float32)

    for dc in range(nc):
        start = lax.rem(col + dc, nc) * m
        own_ref, other_ref = outs[2 * dc], outs[2 * dc + 1]
        for q in range(tails if parts else 0):
            tail = 0.0
            for t in range(parts):
                tail = tail + block(t * tails + q, start, main + q * parts + t)
            tail = jnp.concatenate([tail, jnp.zeros((2 * TI, spare), jnp.float32)], axis=1)
            for t in range(parts):
                x = block(t * tails + q, start, t * tails + q)
                x = jnp.concatenate([x, jnp.zeros((2 * TI, spare), jnp.float32)], axis=1)
                x = jnp.where(inside, x, pltpu.roll(tail, J - spare * t, 1)).astype(jnp.bfloat16)
                own_ref[t * tails + q] = x[:TI]
                other_ref[t * tails + q] = x[TI:]
        if not parts:
            for ch in range(half):
                x = block(ch, start, ch)
                if spare:
                    x = jnp.concatenate([x, jnp.zeros((2 * TI, spare), jnp.float32)], axis=1)
                x = x.astype(jnp.bfloat16)
                own_ref[ch] = x[:TI]
                other_ref[ch] = x[TI:]


def triangle(pos, lk, lr, slots, nr, nc, m, J):
    half, TI, _ = lk.shape
    parts, main = packing(half, J)
    rows = main
    bf = jnp.bfloat16
    n = len(slots)
    return pl.pallas_call(
        functools.partial(tri_kernel, (nr, nc, m, J), n),
        out_shape=[jax.ShapeDtypeStruct((rows, TI, LANES), bf)] * (2 * nc),
        in_specs=[smem(), vmem(), vmem()] + [pl.BlockSpec(memory_space=pl.ANY)] * n,
        out_specs=[vmem()] * (2 * nc),
        scratch_shapes=[
            pltpu.VMEM((nr, 2, rows, TI, LANES), bf),
            pltpu.VMEM((main + (half - main) * max(parts, 1), 2 * TI, LANES), bf),
            pltpu.SemaphoreType.DMA((n,)),
        ],
        compiler_params=pltpu.CompilerParams(vmem_limit_bytes=VMEM_LIMIT),
    )(pos, lk, lr, *slots)


def finish(sc, mid_ref, gate_ref, wx_ref, out_ref):
    TI, C, J = mid_ref.shape
    wx = wx_ref[...]
    for i in range(TI):
        tri = sc[pl.ds(i, C, stride=TI), :][:, :J]
        normed = standardize_columns(tri).astype(jnp.bfloat16)
        update = lax.dot_general(wx, normed, (((1,), (0,)), ((), ())), preferred_element_type=jnp.float32)
        res = mid_ref[i].astype(jnp.float32) + gate_ref[i].astype(jnp.float32) * update
        out_ref[i] = res.T.astype(jnp.bfloat16)


def final_kernel(cfg, n, sub_ref, *rest):
    C, J = cfg
    own = rest[:n]
    other = rest[n : 2 * n]
    mid_ref, gate_ref, wx_ref, out_ref, sc = rest[2 * n :]
    TI = mid_ref.shape[0]
    half = C // 2
    parts, main = packing(half, J)
    tails = half - main
    spare = LANES - J
    sub = sub_ref[0]
    lanes = lane_index((TI, LANES))
    for refs, base in ((own, sub * half), (other, (1 - sub) * half)):
        def total(ch, refs=refs):
            x = refs[0][ch].astype(jnp.float32)
            for ref in refs[1:]:
                x = x + ref[ch].astype(jnp.float32)
            return x.astype(jnp.bfloat16).astype(jnp.float32)

        for q in range(tails if parts else 0):
            tail = jnp.zeros((TI, LANES), jnp.float32)
            for t in range(parts):
                x = total(t * tails + q)
                sc[pl.ds((base + t * tails + q) * TI, TI), :] = x
                tail = jnp.where((lanes >= spare * t) & (lanes < spare * (t + 1)), pltpu.roll(x, LANES - J + spare * t, 1), tail)
            sc[pl.ds((base + main + q) * TI, TI), :] = tail
        if not parts:
            for ch in range(half):
                sc[pl.ds((base + ch) * TI, TI), :] = total(ch)
    finish(sc, mid_ref, gate_ref, wx_ref, out_ref)


def final(sub, own, other, mid, gate, wx):
    TI, C, J = mid.shape
    n = len(own)
    return pl.pallas_call(
        functools.partial(final_kernel, (C, J), n),
        out_shape=jax.ShapeDtypeStruct((TI, J, C), jnp.bfloat16),
        in_specs=[smem()] + [vmem()] * (2 * n + 3),
        out_specs=vmem(),
        scratch_shapes=[pltpu.VMEM((C * TI, LANES), jnp.float32)],
        compiler_params=pltpu.CompilerParams(vmem_limit_bytes=VMEM_LIMIT),
    )(sub, *own, *other, mid, gate, wx)


def lane_pack(values, parts, spare, cols):
    if not parts:
        return values
    inside = lane_index(values[0].shape) < cols
    tails = len(values) // (parts + 1)
    main = tails * parts
    return [jnp.where(inside, values[r], pltpu.roll(values[main + r % tails], cols - spare * (r // tails), 1)) for r in range(main)]


def masked_left(lk_ref, lr_ref, lm, J):
    half, TI, _ = lk_ref.shape
    parts, main = packing(half, J)
    spare = LANES - J
    inside = lane_index((2 * TI, LANES)) < J
    for ch in range(half):
        x = jnp.concatenate([lk_ref[ch], lr_ref[ch]], axis=0)
        if ch < main:
            lm[ch] = x
        else:
            f = x.astype(jnp.float32)
            for t in range(parts):
                moved = pltpu.roll(f, J - spare * t, 1)
                lm[main + (ch - main) * parts + t] = jnp.where(inside, 0.0, moved).astype(jnp.bfloat16)


def shard_products(lm, rv, k, J, half, TI, store):
    parts, main = packing(half, J)
    tails = half - main

    def dot(left, row):
        right = rv[k, :, row].reshape(2 * TI, LANES)
        return lax.dot_general(lm[left], right, (((1,), (1,)), ((), ())), preferred_element_type=jnp.float32)

    def channel(ch):
        if ch < main:
            return dot(ch, ch)
        q = ch - main
        x = dot(main + q * parts, q)
        for t in range(1, parts):
            x = x + dot(main + q * parts + t, t * tails + q)
        return x

    pairs = half // 2
    cols = 4 * TI
    pad = jnp.zeros((2 * TI, LANES - cols), jnp.float32)
    p2, m2 = packing(pairs, cols)
    t2 = pairs - m2

    def both(q):
        return jnp.concatenate([channel(q), channel(q + pairs), pad], axis=1)

    inside = lane_index((2 * TI, LANES)) < cols
    spare = LANES - cols
    for q in range(t2):
        tail = both(m2 + q)
        for t in range(p2):
            store(t * t2 + q, jnp.where(inside, both(t * t2 + q), pltpu.roll(tail, cols - spare * t, 1)).astype(jnp.bfloat16))
    for q in range(0 if p2 else pairs):
        store(q, both(q).astype(jnp.bfloat16))


def early_kernel(J, n, pos_ref, lk_ref, lr_ref, *rest):
    own, up, down, far = rest[0:2], rest[2:4], rest[4:6], rest[6:8]
    outs = rest[8:14]
    rv, lm, acc, sem = rest[14:]
    half, TI, _ = lk_ref.shape
    row, col, sub = pos_ref[0], pos_ref[1], pos_ref[2]
    even = lax.rem(row, 2) == 0
    edge = (row == 0) | (row == n - 1)
    plan = [
        (None, own, 0),
        (even, down, 1),
        (jnp.logical_not(even), up, 1),
        (edge, far, 2),
        (jnp.logical_not(edge) & even, up, 2),
        (jnp.logical_not(edge) & jnp.logical_not(even), down, 2),
    ]

    def each(action):
        for cond, refs, k in plan:
            for u in range(2):
                c = pltpu.make_async_copy(refs[u], rv.at[k, sub if u == 0 else 1 - sub], sem.at[k, u])
                if cond is None:
                    action(c)
                else:
                    pl.when(cond)(lambda c=c: action(c))

    each(lambda c: c.start())
    masked_left(lk_ref, lr_ref, lm, J)
    each(lambda c: c.wait())
    for k in range(3):

        def store(r, x, k=k):
            acc[k, r] = x

        shard_products(lm, rv, k, J, half, TI, store)
    home = col == row // 2
    send = jnp.where(home, acc[2], acc[0])
    keep = jnp.where(home, acc[0], acc[2])
    for u in range(2):
        outs[u][...] = send[:, u * TI : (u + 1) * TI]
        outs[2 + u][...] = keep[:, u * TI : (u + 1) * TI]
        outs[4 + u][...] = acc[1, :, u * TI : (u + 1) * TI]


def late_kernel(J, n, pos_ref, lk_ref, lr_ref, a_ref, b_ref, *rest):
    up, down = rest[0:2], rest[2:4]
    outs = rest[4:8]
    rv, lm, acc, sem = rest[8:]
    half, TI, _ = lk_ref.shape
    row, col, sub = pos_ref[0], pos_ref[1], pos_ref[2]
    low = row < 2

    def each(action):
        for cond, refs in ((low, down), (jnp.logical_not(low), up)):
            for u in range(2):
                c = pltpu.make_async_copy(refs[u], rv.at[0, sub if u == 0 else 1 - sub], sem.at[u])
                pl.when(cond)(lambda c=c: action(c))

    each(lambda c: c.start())
    masked_left(lk_ref, lr_ref, lm, J)
    each(lambda c: c.wait())

    def store(r, x):
        acc[r] = x

    shard_products(lm, rv, 0, J, half, TI, store)
    home = col == row // 2
    for u, ref in enumerate((a_ref, b_ref)):
        late = acc[:, u * TI : (u + 1) * TI]
        early = ref[...]
        outs[u][...] = jnp.where(home, late, early)
        outs[2 + u][...] = jnp.where(home, early, late)


def split_call(kernel, shards, sems, n_out, pos, lk, lr, extra, slots, J, n):
    half, TI, _ = lk.shape
    parts, main = packing(half, J)
    rows = packing(half // 2, 4 * TI)[1]
    bf = jnp.bfloat16
    acc = (rows, 2 * TI, LANES)
    return pl.pallas_call(
        functools.partial(kernel, J, n),
        out_shape=[jax.ShapeDtypeStruct((rows, TI, LANES), bf)] * n_out,
        in_specs=[smem(), vmem(), vmem()] + [vmem()] * len(extra) + [pl.BlockSpec(memory_space=pl.ANY)] * len(slots),
        out_specs=[vmem()] * n_out,
        scratch_shapes=[
            pltpu.VMEM((shards, 2, main, TI, LANES), bf),
            pltpu.VMEM((main + (half - main) * max(parts, 1), 2 * TI, LANES), bf),
            pltpu.VMEM((shards,) + acc if shards > 1 else acc, bf),
            pltpu.SemaphoreType.DMA(sems),
        ],
        compiler_params=pltpu.CompilerParams(vmem_limit_bytes=VMEM_LIMIT),
        cost_estimate=pl.CostEstimate(flops=2 * shards * half * 48 * 48 * 512, bytes_accessed=shards * 2 * main * TI * LANES * 4, transcendentals=0),
    )(pos, lk, lr, *extra, *slots)


def final_pairs_kernel(cfg, pos_ref, *rest):
    C, J = cfg
    own = (rest[0:2], rest[2:4])
    other = (rest[4:6], rest[6:8])
    mid_ref, gate_ref, wx_ref, out_ref, sc = rest[8:]
    TI = mid_ref.shape[0]
    half = C // 2
    pairs = half // 2
    cols = 4 * TI
    parts, main = packing(pairs, cols)
    tails = pairs - main
    spare = LANES - cols
    row, col, sub = pos_ref[0], pos_ref[1], pos_ref[2]
    home = col == row // 2
    odd = lax.rem(row, 2) == 1
    first = jnp.where(home, jnp.logical_not(odd), odd)
    lanes = lane_index((TI, LANES))
    low = lanes < 2 * TI
    for groups, base in ((own, sub * half), (other, (1 - sub) * half)):

        def place(q, both):
            a = jnp.where(first, both[0], both[1])
            b = jnp.where(first, both[1], both[0])
            x = jnp.where(low, a, pltpu.roll(b, 2 * TI, 1))
            y = jnp.where(low, pltpu.roll(a, LANES - 2 * TI, 1), b)
            sc[pl.ds((base + q) * TI, TI), :] = x
            sc[pl.ds((base + q + pairs) * TI, TI), :] = y

        def total(g, r):
            x = groups[g][0][r].astype(jnp.float32) + groups[g][1][r].astype(jnp.float32)
            return x.astype(jnp.bfloat16).astype(jnp.float32)

        for q in range(tails if parts else 0):
            tail = [jnp.zeros((TI, LANES), jnp.float32)] * 2
            for t in range(parts):
                x = [total(g, t * tails + q) for g in range(2)]
                place(t * tails + q, x)
                part = (lanes >= spare * t) & (lanes < spare * (t + 1))
                tail = [jnp.where(part, pltpu.roll(x[g], LANES - cols + spare * t, 1), tail[g]) for g in range(2)]
            place(main + q, tail)
        for q in range(0 if parts else pairs):
            place(q, [total(g, q) for g in range(2)])
    finish(sc, mid_ref, gate_ref, wx_ref, out_ref)


def final_pairs(pos, pieces, mid, gate, wx):
    TI, C, J = mid.shape
    return pl.pallas_call(
        functools.partial(final_pairs_kernel, (C, J)),
        out_shape=jax.ShapeDtypeStruct((TI, J, C), jnp.bfloat16),
        in_specs=[smem()] + [vmem()] * (len(pieces) + 3),
        out_specs=vmem(),
        scratch_shapes=[pltpu.VMEM((C * TI, LANES), jnp.float32)],
        compiler_params=pltpu.CompilerParams(vmem_limit_bytes=VMEM_LIMIT),
    )(pos, *pieces, mid, gate, wx)


def shift(x, axis, d):
    n = lax.axis_size(axis)
    return lax.ppermute(x, axis, [(i, (i + d) % n) for i in range(n)])


def step_along(x, axis, d, t):
    n = lax.axis_size(axis)
    return lax.ppermute(x, axis, [(i, i + d) for i in range(n) if 0 <= i + d < n and 0 <= i - d * (t - 1) < n])


def across(x, d):
    nc = lax.axis_size("col")
    return lax.ppermute(x, ("col", "sub"), [(c * 2 + s, (c + d) % nc * 2 + 1 - s) for c in range(nc) for s in range(2)])


def per_device(
    homolog_activations,
    edge_activations,
    first_projection_matrix,
    second_projection_matrix,
    tensor_product_matrix,
    multiplicative_entry_matrix,
    multiplicative_exit_matrix,
):
    seqs, residues, features = homolog_activations.shape
    tile_rows, tile_cols, width = edge_activations.shape
    fw = first_projection_matrix.shape[1]
    nr, nc, ns = (lax.axis_size(a) for a in ("row", "col", "sub"))
    assert ns == 2
    row, col, sub = (lax.axis_index(a) for a in ("row", "col", "sub"))
    pos = jnp.stack([row, col, sub]).astype(jnp.int32)
    sub_id = pos[2:]
    m = tile_cols // residues

    normed = standardize_features(homolog_activations.astype(jnp.float32)).astype(jnp.bfloat16).reshape(seqs * residues, features)

    def project(matrix):
        return jnp.dot(normed, matrix, preferred_element_type=jnp.float32).astype(jnp.bfloat16).reshape(seqs, residues * fw)

    right = project(second_projection_matrix)
    left = project(first_projection_matrix)

    rows = jnp.stack([right] + [shift(right, "row", d) for d in range(1, nr)])

    def rows_of(c):
        return jnp.stack([lax.dynamic_index_in_dim(rows, lax.rem(row - (c * m + t) + nr, nr), 0, keepdims=False) for t in range(m)])

    rights, lefts = [rows_of(col)], [left]
    for d in range(1, nc):
        rights.append(shift(rows_of(lax.rem(col + d, nc)), "col", d))
        lefts.append(shift(left, "col", d))
    rights = jnp.stack(rights)
    lefts = jnp.concatenate(lefts, axis=0)
    rights_other = shift(rights, "sub", 1)
    span = tile_rows * fw
    left_own = lax.dynamic_slice_in_dim(lefts, sub * span, span, 1)
    left_other = shift(lax.dynamic_slice_in_dim(lefts, (1 - sub) * span, span, 1), "sub", 1)
    left_rows = jnp.concatenate([left_own, left_other], axis=0)
    right_t = prep(rights, rights_other, fw)

    outer_weight = tensor_product_matrix.reshape(fw, fw, width).transpose(2, 1, 0).reshape(width, fw * fw)
    entry = multiplicative_entry_matrix.T
    exit_matrix = multiplicative_exit_matrix.T
    fast = nr == 4 and nc == 2 and m == 2
    if fast:
        ends = [(0, nr - 1), (nr - 1, 0)]
        far_edges = lax.ppermute(edge_activations, "row", ends)
        far_rows = lax.ppermute(left_rows, "row", ends)
    mid, gate, lk, ls, rk, rs = pair(sub_id, left_rows, right_t, outer_weight, edge_activations, entry, tile_rows)

    rr = shift(rs, "sub", 1)
    lr = shift(ls, "sub", 1)
    if fast:
        up = [step_along(x, "row", 1, 1) for x in (rk, rr)]
        down = [step_along(x, "row", -1, 1) for x in (rk, rr)]
        far_k, far_s = pair(sub_id, far_rows, right_t, outer_weight, far_edges, entry, tile_rows, False)
        far = [far_k, shift(far_s, "sub", 1)]
        up2 = [step_along(x, "row", 1, 2) for x in up]
        down2 = [step_along(x, "row", -1, 2) for x in down]
        send1, send1o, keep1, keep1o, rest, resto = split_call(early_kernel, 3, (3, 2), 6, pos, lk, lr, [], [rk, rr, *up, *down, *far], tile_cols, nr)
        got1, got1o, keep1o = shift(send1, "col", 1), across(send1o, 1), shift(keep1o, "sub", 1)
        send2, send2o, keep2, keep2o = split_call(late_kernel, 1, (2,), 4, pos, lk, lr, [rest, resto], [*up2, *down2], tile_cols, nr)
        got2, got2o, keep2o = shift(send2, "col", 1), across(send2o, 1), shift(keep2o, "sub", 1)
        return final_pairs(pos, [keep1, got1, keep2, got2, keep1o, got1o, keep2o, got2o], mid, gate, exit_matrix)

    slots = [rk, rr]
    up, down = [rk, rr], [rk, rr]
    for t in range(1, nr):
        up = [step_along(x, "row", 1, t) for x in up]
        down = [step_along(x, "row", -1, t) for x in down]
        slots += up + down
    partial = triangle(pos, lk, lr, slots, nr, nc, m, tile_cols)

    own, other = [partial[0]], [shift(partial[1], "sub", 1)]
    for d in range(1, nc):
        own.append(shift(partial[2 * d], "col", d))
        other.append(across(partial[2 * d + 1], d))
    return final(sub_id, own, other, mid, gate, exit_matrix)


def solution(mesh):
    in_specs = (
        P(("grp", "col", "sub"), "row", None),
        P(("grp", "row", "sub"), "col", None),
        P(),
        P(),
        P(),
        P(),
        P(),
    )
    out_specs = P(("grp", "row", "sub"), "col", None)
    return jax.shard_map(per_device, mesh=mesh, in_specs=in_specs, out_specs=out_specs, check_vma=False)
```

```python
import functools

import jax
import jax.numpy as jnp
from jax import lax
from jax.experimental import pallas as pl
from jax.experimental.pallas import tpu as pltpu
from jax.sharding import PartitionSpec as P


EPSILON = 1e-05
LANES = 128
VMEM_LIMIT = 60 * 1024 * 1024


def standardize_features(values):
    centred = values - jnp.mean(values, axis=-1, keepdims=True)
    spread = jnp.mean(centred * centred, axis=-1, keepdims=True)
    return centred * lax.rsqrt(spread + EPSILON)


def standardize_columns(values):
    centred = values - jnp.mean(values, axis=0, keepdims=True)
    spread = jnp.mean(centred * centred, axis=0, keepdims=True)
    return centred * lax.rsqrt(spread + EPSILON)


def vmem():
    return pl.BlockSpec(memory_space=pltpu.VMEM)


def smem():
    return pl.BlockSpec(memory_space=pltpu.SMEM)


def packing(count, cols):
    spare = -cols % LANES
    if spare and cols < LANES and cols % spare == 0:
        parts = cols // spare
        if count % (parts + 1) == 0:
            return parts, count // (parts + 1) * parts
    return 0, count


def lane_index(shape):
    return lax.broadcasted_iota(jnp.int32, shape, len(shape) - 1)


def weights_kernel(fw, w_ref, n_ref, x_ref, wt_ref, nt_ref, xt_ref, sc, st):
    C = w_ref.shape[1]
    sc[...] = w_ref[...].astype(jnp.float32)
    for b in range(fw):
        st[b * fw : (b + 1) * fw, :] = sc[pl.ds(b, fw, stride=fw), :]
    for t in range(fw * fw // C):
        wt_ref[:, t * C : (t + 1) * C] = st[t * C : (t + 1) * C, :].T.astype(jnp.bfloat16)
    for t in range(n_ref.shape[1] // C):
        nt_ref[t * C : (t + 1) * C, :] = n_ref[:, t * C : (t + 1) * C].astype(jnp.float32).T.astype(jnp.bfloat16)
    xt_ref[...] = x_ref[...].astype(jnp.float32).T.astype(jnp.bfloat16)


def weights(w, n, x, fw):
    K, C = w.shape
    bf = jnp.bfloat16
    return pl.pallas_call(
        functools.partial(weights_kernel, fw),
        out_shape=[jax.ShapeDtypeStruct((C, K), bf), jax.ShapeDtypeStruct(n.shape[::-1], bf), jax.ShapeDtypeStruct(x.shape[::-1], bf)],
        in_specs=[vmem()] * 3,
        out_specs=[vmem()] * 3,
        scratch_shapes=[pltpu.VMEM((K, C), jnp.float32)] * 2,
    )(w, n, x)


def prep_kernel(fw, own_ref, recv_ref, rt_ref, sc):
    groups, m, seqs, row_lanes = own_ref.shape
    res = row_lanes // fw
    chunk = sc.shape[2]
    pieces = [(ref, g) for ref in (own_ref, recv_ref) for g in range(groups)]
    per = chunk // seqs
    for u in range(len(pieces) // per):
        for mm in range(m):
            for t in range(row_lanes // LANES):
                block = jnp.concatenate(
                    [ref[g, mm, :, t * LANES : (t + 1) * LANES].astype(jnp.float32) for ref, g in pieces[u * per : (u + 1) * per]], axis=0
                )
                start = mm * row_lanes + t * LANES
                sc[u, start : start + LANES, :] = block.T
        for b in range(fw):
            rt_ref[b, :, u * chunk : (u + 1) * chunk] = sc[u, pl.ds(b, m * res, stride=fw), :].astype(jnp.bfloat16)


def prep(own, recv, fw):
    groups, m, seqs, row_lanes = own.shape
    total = 2 * groups * seqs
    chunk = min(total, LANES)
    cols = m * row_lanes // fw
    return pl.pallas_call(
        functools.partial(prep_kernel, fw),
        out_shape=jax.ShapeDtypeStruct((fw, cols, total), jnp.bfloat16),
        in_specs=[vmem(), vmem()],
        out_specs=vmem(),
        scratch_shapes=[pltpu.VMEM((total // chunk, m * row_lanes, chunk), jnp.float32)],
    )(own, recv)


def pair_kernel(cfg, sub_ref, l_ref, lr_ref, rt_ref, wt_ref, e_ref, went_ref, *rest):
    fw, C, J, S, full = cfg
    if full:
        mid_ref, gate_ref, lk_ref, ls_ref, rk_ref, rs_ref, lt, ot, nts, lsc, rsc = rest
    else:
        rk_ref, rs_ref, lt, ot, nts, rsc = rest
    half = C // 2
    IG = l_ref.shape[1] // fw
    wide = ot.shape[2] // 2
    for t in range(IG * fw // LANES):
        part = slice(t * LANES, (t + 1) * LANES)
        block = jnp.concatenate([l_ref[:, part].astype(jnp.float32), lr_ref[:, part].astype(jnp.float32)], axis=0)
        lt[part, :] = block.T.astype(jnp.bfloat16)
    ltv = lt[...]
    for b in range(fw):
        o = lax.dot_general(ltv, rt_ref[b], (((1,), (1,)), ((), ())), preferred_element_type=jnp.float32).astype(jnp.bfloat16)
        for i in range(IG):
            ot[i // 2, b * fw : (b + 1) * fw, i % 2 * wide : i % 2 * wide + J] = o[i * fw : (i + 1) * fw, :]
    wt = wt_ref[...]
    for h in range(IG // 2):
        pt = lax.dot_general(wt, ot[h], (((1,), (0,)), ((), ())), preferred_element_type=jnp.float32)
        for k in range(2):
            i = 2 * h + k
            et = e_ref[i].astype(jnp.float32).T
            mid = (et + pt[:, k * wide : k * wide + J] * (1.0 / S)).astype(jnp.bfloat16)
            if full:
                mid_ref[i] = mid
            nts[h, :, k * wide : k * wide + J] = standardize_columns(mid.astype(jnp.float32)).astype(jnp.bfloat16)

    def project(first, count, h):
        return lax.dot_general(went_ref[first * C : (first + count) * C, :], nts[h], (((1,), (0,)), ((), ())), preferred_element_type=jnp.float32)

    for h in range(IG // 2):
        if full:
            p = project(0, 2, h)
            x = jax.nn.sigmoid(p[C:]) * p[:C]
            for k in range(2):
                lsc[pl.ds((2 * h + k) * C, C), :J] = x[:, k * wide : k * wide + J]
        p = project(2, 2, h)
        x = jax.nn.sigmoid(p[C:]) * p[:C]
        for k in range(2):
            rsc[pl.ds((2 * h + k) * C, C), :J] = x[:, k * wide : k * wide + J]
        if full:
            x = jax.nn.sigmoid(project(4, 1, h)).astype(jnp.bfloat16)
            for k in range(2):
                gate_ref[2 * h + k] = x[:, k * wide : k * wide + J]
    sub = sub_ref[0]
    parts, main = packing(half, J)
    inside = lane_index((IG, LANES)) < J
    if full:
        for ref, base in ((lk_ref, sub * half), (ls_ref, (1 - sub) * half)):
            for ch in range(half):
                x = lsc[pl.ds(base + ch, IG, stride=C), :]
                ref[ch] = jnp.where(inside, x, 0.0).astype(jnp.bfloat16)
    for ref, base in ((rk_ref, sub * half), (rs_ref, (1 - sub) * half)):
        if parts == 0:
            for ch in range(half):
                x = rsc[pl.ds(base + ch, IG, stride=C), :]
                ref[ch] = jnp.where(inside, x, 0.0).astype(jnp.bfloat16)
        else:
            tails = half - main
            spare = LANES - J
            for q in range(tails):
                tail = rsc[pl.ds(base + main + q, IG, stride=C), :]
                for t in range(parts):
                    x = rsc[pl.ds(base + t * tails + q, IG, stride=C), :]
                    moved = pltpu.roll(tail, J - spare * t, 1)
                    ref[t * tails + q] = jnp.where(inside, x, moved).astype(jnp.bfloat16)


def pair(sub, l, lr, which, rt, wt, e, went, IG, full=True):
    _, part, IA = l.shape
    S = 2 * part
    fw, J, _ = rt.shape
    TI = IA // fw
    C = wt.shape[0]
    half = C // 2
    rows = packing(half, J)[1]
    wide = -(-J // LANES) * LANES
    bf = jnp.bfloat16
    tile = (jax.ShapeDtypeStruct((TI, C, J), bf), pl.BlockSpec((IG, C, J), lambda g: (g, 0, 0)))
    lefts = (jax.ShapeDtypeStruct((half, TI, LANES), bf), pl.BlockSpec((half, IG, LANES), lambda g: (0, g, 0)))
    rights = (jax.ShapeDtypeStruct((rows, TI, LANES), bf), pl.BlockSpec((rows, IG, LANES), lambda g: (0, g, 0)))
    outs = ([tile] * 2 + [lefts] * 2 if full else []) + [rights] * 2
    gated = pltpu.VMEM((IG * C, LANES), jnp.float32)
    f = pl.pallas_call(
        functools.partial(pair_kernel, (fw, C, J, S, full)),
        grid=(TI // IG,),
        out_shape=[o[0] for o in outs],
        in_specs=[
            smem(),
            pl.BlockSpec((None, part, IG * fw), lambda g: (which, 0, g)),
            pl.BlockSpec((None, part, IG * fw), lambda g: (which, 0, g)),
            pl.BlockSpec((fw, J, S), lambda g: (0, 0, 0)),
            pl.BlockSpec(wt.shape, lambda g: (0, 0)),
            pl.BlockSpec((IG, J, C), lambda g: (g, 0, 0)),
            pl.BlockSpec(went.shape, lambda g: (0, 0)),
        ],
        out_specs=[o[1] for o in outs],
        scratch_shapes=[
            pltpu.VMEM((IG * fw, S), bf),
            pltpu.VMEM((IG // 2, fw * fw, 2 * wide), bf),
            pltpu.VMEM((IG // 2, C, 2 * wide), bf),
            gated,
        ]
        + ([gated] if full else []),
        compiler_params=pltpu.CompilerParams(vmem_limit_bytes=VMEM_LIMIT),
        cost_estimate=pl.CostEstimate(flops=2 * TI * J * (S * fw * fw + fw * fw * C + 5 * C * C), bytes_accessed=4 * TI * J * C * 6, transcendentals=TI * J * C * 3),
    )
    return f(sub, l, lr, rt, wt, e, went)


def tri_kernel(cfg, n_slots, pos_ref, lk_ref, lr_ref, *rest):
    nr, nc, m, J = cfg
    slots = rest[:n_slots]
    outs = rest[n_slots : n_slots + 2 * nc]
    rv, lm, sem = rest[n_slots + 2 * nc :]
    half, TI, _ = lk_ref.shape
    row, col, sub = pos_ref[0], pos_ref[1], pos_ref[2]
    parts, main = packing(half, J)
    tails = half - main
    spare = LANES - J

    def copy(index):
        step, u = index // 2, index % 2
        hop = (step + 1) // 2
        origin = row - hop if step % 2 else row + hop
        return origin, pltpu.make_async_copy(slots[index], rv.at[jnp.clip(origin, 0, nr - 1), sub if u == 0 else 1 - sub], sem.at[index])

    for index in range(n_slots):
        origin, c = copy(index)

        @pl.when((origin >= 0) & (origin < nr))
        def _(c=c):
            c.start()

    inside = lane_index((2 * TI, LANES)) < J
    for ch in range(half):
        x = jnp.concatenate([lk_ref[ch], lr_ref[ch]], axis=0)
        if ch < main:
            lm[ch] = x
        else:
            f = x.astype(jnp.float32)
            for t in range(parts):
                moved = pltpu.roll(f, J - spare * t, 1)
                lm[main + (ch - main) * parts + t] = jnp.where(inside, 0.0, moved).astype(jnp.bfloat16)

    for index in range(n_slots):
        origin, c = copy(index)

        @pl.when((origin >= 0) & (origin < nr))
        def _(c=c):
            c.wait()

    def block(ch, start, pieces):
        right = rv[pl.ds(start, m), :, ch].reshape(m * 2 * TI, LANES)
        return lax.dot_general(lm[pieces], right, (((1,), (1,)), ((), ())), preferred_element_type=jnp.float32)

    for dc in range(nc):
        start = lax.rem(col + dc, nc) * m
        own_ref, other_ref = outs[2 * dc], outs[2 * dc + 1]
        for q in range(tails if parts else 0):
            tail = 0.0
            for t in range(parts):
                tail = tail + block(t * tails + q, start, main + q * parts + t)
            tail = jnp.concatenate([tail, jnp.zeros((2 * TI, spare), jnp.float32)], axis=1)
            for t in range(parts):
                x = block(t * tails + q, start, t * tails + q)
                x = jnp.concatenate([x, jnp.zeros((2 * TI, spare), jnp.float32)], axis=1)
                x = jnp.where(inside, x, pltpu.roll(tail, J - spare * t, 1)).astype(jnp.bfloat16)
                own_ref[t * tails + q] = x[:TI]
                other_ref[t * tails + q] = x[TI:]
        if not parts:
            for ch in range(half):
                x = block(ch, start, ch)
                if spare:
                    x = jnp.concatenate([x, jnp.zeros((2 * TI, spare), jnp.float32)], axis=1)
                x = x.astype(jnp.bfloat16)
                own_ref[ch] = x[:TI]
                other_ref[ch] = x[TI:]


def triangle(pos, lk, lr, slots, nr, nc, m, J):
    half, TI, _ = lk.shape
    parts, main = packing(half, J)
    rows = main
    bf = jnp.bfloat16
    n = len(slots)
    return pl.pallas_call(
        functools.partial(tri_kernel, (nr, nc, m, J), n),
        out_shape=[jax.ShapeDtypeStruct((rows, TI, LANES), bf)] * (2 * nc),
        in_specs=[smem(), vmem(), vmem()] + [pl.BlockSpec(memory_space=pl.ANY)] * n,
        out_specs=[vmem()] * (2 * nc),
        scratch_shapes=[
            pltpu.VMEM((nr, 2, rows, TI, LANES), bf),
            pltpu.VMEM((main + (half - main) * max(parts, 1), 2 * TI, LANES), bf),
            pltpu.SemaphoreType.DMA((n,)),
        ],
        compiler_params=pltpu.CompilerParams(vmem_limit_bytes=VMEM_LIMIT),
    )(pos, lk, lr, *slots)


def finish(sc, nts, mid_ref, gate_ref, wx_ref, out_ref):
    TI, C, J = mid_ref.shape
    wide = nts.shape[2] // 2
    wx = wx_ref[...]
    for i in range(TI):
        tri = sc[pl.ds(i, C, stride=TI), :][:, :J]
        nts[i // 2, :, i % 2 * wide : i % 2 * wide + J] = standardize_columns(tri).astype(jnp.bfloat16)
    for h in range(TI // 2):
        update = lax.dot_general(wx, nts[h], (((1,), (0,)), ((), ())), preferred_element_type=jnp.float32)
        for k in range(2):
            i = 2 * h + k
            res = mid_ref[i].astype(jnp.float32) + gate_ref[i].astype(jnp.float32) * update[:, k * wide : k * wide + J]
            out_ref[i] = res.T.astype(jnp.bfloat16)


def final_kernel(cfg, n, sub_ref, *rest):
    C, J = cfg
    own = rest[:n]
    other = rest[n : 2 * n]
    mid_ref, gate_ref, wx_ref, out_ref, sc, nts = rest[2 * n :]
    TI = mid_ref.shape[0]
    half = C // 2
    parts, main = packing(half, J)
    tails = half - main
    spare = LANES - J
    sub = sub_ref[0]
    lanes = lane_index((TI, LANES))
    for refs, base in ((own, sub * half), (other, (1 - sub) * half)):
        def total(ch, refs=refs):
            x = refs[0][ch].astype(jnp.float32)
            for ref in refs[1:]:
                x = x + ref[ch].astype(jnp.float32)
            return x.astype(jnp.bfloat16).astype(jnp.float32)

        for q in range(tails if parts else 0):
            tail = jnp.zeros((TI, LANES), jnp.float32)
            for t in range(parts):
                x = total(t * tails + q)
                sc[pl.ds((base + t * tails + q) * TI, TI), :] = x
                tail = jnp.where((lanes >= spare * t) & (lanes < spare * (t + 1)), pltpu.roll(x, LANES - J + spare * t, 1), tail)
            sc[pl.ds((base + main + q) * TI, TI), :] = tail
        if not parts:
            for ch in range(half):
                sc[pl.ds((base + ch) * TI, TI), :] = total(ch)
    finish(sc, nts, mid_ref, gate_ref, wx_ref, out_ref)


def final(sub, own, other, mid, gate, wx):
    TI, C, J = mid.shape
    n = len(own)
    return pl.pallas_call(
        functools.partial(final_kernel, (C, J), n),
        out_shape=jax.ShapeDtypeStruct((TI, J, C), jnp.bfloat16),
        in_specs=[smem()] + [vmem()] * (2 * n + 3),
        out_specs=vmem(),
        scratch_shapes=[pltpu.VMEM((C * TI, LANES), jnp.float32), pltpu.VMEM((TI // 2, C, 2 * LANES), jnp.bfloat16)],
        compiler_params=pltpu.CompilerParams(vmem_limit_bytes=VMEM_LIMIT),
    )(sub, *own, *other, mid, gate, wx)


def masked_left(lk_ref, lr_ref, lm, J):
    half, TI, _ = lk_ref.shape
    parts, main = packing(half, J)
    spare = LANES - J
    inside = lane_index((2 * TI, LANES)) < J
    for ch in range(half):
        x = jnp.concatenate([lk_ref[ch], lr_ref[ch]], axis=0)
        if ch < main:
            lm[ch] = x
        else:
            f = x.astype(jnp.float32)
            for t in range(parts):
                moved = pltpu.roll(f, J - spare * t, 1)
                lm[main + (ch - main) * parts + t] = jnp.where(inside, 0.0, moved).astype(jnp.bfloat16)


def shard_products(lm, rv, k, J, half, TI, store):
    parts, main = packing(half, J)
    tails = half - main

    def dot(left, row):
        right = rv[k, :, row].reshape(2 * TI, LANES)
        return lax.dot_general(lm[left], right, (((1,), (1,)), ((), ())), preferred_element_type=jnp.float32)

    def channel(ch):
        if ch < main:
            return dot(ch, ch)
        q = ch - main
        x = dot(main + q * parts, q)
        for t in range(1, parts):
            x = x + dot(main + q * parts + t, t * tails + q)
        return x

    pairs = half // 2
    cols = 4 * TI
    pad = jnp.zeros((2 * TI, LANES - cols), jnp.float32)
    p2, m2 = packing(pairs, cols)
    t2 = pairs - m2

    def both(q):
        return jnp.concatenate([channel(q), channel(q + pairs), pad], axis=1)

    inside = lane_index((2 * TI, LANES)) < cols
    spare = LANES - cols
    for q in range(t2):
        tail = both(m2 + q)
        for t in range(p2):
            store(t * t2 + q, jnp.where(inside, both(t * t2 + q), pltpu.roll(tail, cols - spare * t, 1)).astype(jnp.bfloat16))
    for q in range(0 if p2 else pairs):
        store(q, both(q).astype(jnp.bfloat16))


def early_kernel(J, n, pos_ref, lk_ref, lr_ref, *rest):
    own, up, down, far = rest[0:2], rest[2:4], rest[4:6], rest[6:8]
    outs = rest[8:14]
    rv, lm, acc, sem = rest[14:]
    half, TI, _ = lk_ref.shape
    row, col, sub = pos_ref[0], pos_ref[1], pos_ref[2]
    even = lax.rem(row, 2) == 0
    edge = (row == 0) | (row == n - 1)
    plan = [
        (None, own, 0),
        (even, down, 1),
        (jnp.logical_not(even), up, 1),
        (edge, far, 2),
        (jnp.logical_not(edge) & even, up, 2),
        (jnp.logical_not(edge) & jnp.logical_not(even), down, 2),
    ]

    def each(action):
        for cond, refs, k in plan:
            for u in range(2):
                c = pltpu.make_async_copy(refs[u], rv.at[k, sub if u == 0 else 1 - sub], sem.at[k, u])
                if cond is None:
                    action(c)
                else:
                    pl.when(cond)(lambda c=c: action(c))

    each(lambda c: c.start())
    masked_left(lk_ref, lr_ref, lm, J)
    each(lambda c: c.wait())
    for k in range(3):

        def store(r, x, k=k):
            acc[k, r] = x

        shard_products(lm, rv, k, J, half, TI, store)
    home = col == row // 2
    send = jnp.where(home, acc[2], acc[0])
    keep = jnp.where(home, acc[0], acc[2])
    for u in range(2):
        outs[u][...] = send[:, u * TI : (u + 1) * TI]
        outs[2 + u][...] = keep[:, u * TI : (u + 1) * TI]
        outs[4 + u][...] = acc[1, :, u * TI : (u + 1) * TI]


def late_kernel(J, n, pos_ref, lk_ref, lr_ref, a_ref, b_ref, *rest):
    up, down = rest[0:2], rest[2:4]
    outs = rest[4:8]
    rv, lm, acc, sem = rest[8:]
    half, TI, _ = lk_ref.shape
    row, col, sub = pos_ref[0], pos_ref[1], pos_ref[2]
    low = row < 2

    def each(action):
        for cond, refs in ((low, down), (jnp.logical_not(low), up)):
            for u in range(2):
                c = pltpu.make_async_copy(refs[u], rv.at[0, sub if u == 0 else 1 - sub], sem.at[u])
                pl.when(cond)(lambda c=c: action(c))

    each(lambda c: c.start())
    masked_left(lk_ref, lr_ref, lm, J)
    each(lambda c: c.wait())

    def store(r, x):
        acc[r] = x

    shard_products(lm, rv, 0, J, half, TI, store)
    home = col == row // 2
    for u, ref in enumerate((a_ref, b_ref)):
        late = acc[:, u * TI : (u + 1) * TI]
        early = ref[...]
        outs[u][...] = jnp.where(home, late, early)
        outs[2 + u][...] = jnp.where(home, early, late)


def split_call(kernel, shards, sems, n_out, pos, lk, lr, extra, slots, J, n):
    half, TI, _ = lk.shape
    parts, main = packing(half, J)
    rows = packing(half // 2, 4 * TI)[1]
    bf = jnp.bfloat16
    acc = (rows, 2 * TI, LANES)
    return pl.pallas_call(
        functools.partial(kernel, J, n),
        out_shape=[jax.ShapeDtypeStruct((rows, TI, LANES), bf)] * n_out,
        in_specs=[smem(), vmem(), vmem()] + [vmem()] * len(extra) + [pl.BlockSpec(memory_space=pl.ANY)] * len(slots),
        out_specs=[vmem()] * n_out,
        scratch_shapes=[
            pltpu.VMEM((shards, 2, main, TI, LANES), bf),
            pltpu.VMEM((main + (half - main) * max(parts, 1), 2 * TI, LANES), bf),
            pltpu.VMEM((shards,) + acc if shards > 1 else acc, bf),
            pltpu.SemaphoreType.DMA(sems),
        ],
        compiler_params=pltpu.CompilerParams(vmem_limit_bytes=VMEM_LIMIT),
        cost_estimate=pl.CostEstimate(flops=2 * shards * half * 48 * 48 * 512, bytes_accessed=shards * 2 * main * TI * LANES * 4, transcendentals=0),
    )(pos, lk, lr, *extra, *slots)


def final_pairs_kernel(cfg, pos_ref, *rest):
    C, _ = cfg
    own = (rest[0:2], rest[2:4])
    other = (rest[4:6], rest[6:8])
    mid_ref, gate_ref, wx_ref, out_ref, sc, nts = rest[8:]
    TI = mid_ref.shape[0]
    half = C // 2
    pairs = half // 2
    cols = 4 * TI
    parts, main = packing(pairs, cols)
    tails = pairs - main
    spare = LANES - cols
    row, col, sub = pos_ref[0], pos_ref[1], pos_ref[2]
    home = col == row // 2
    odd = lax.rem(row, 2) == 1
    first = jnp.where(home, jnp.logical_not(odd), odd)
    lanes = lane_index((TI, LANES))
    low = lanes < 2 * TI
    for groups, base in ((own, sub * half), (other, (1 - sub) * half)):

        def place(q, both):
            a = jnp.where(first, both[0], both[1])
            b = jnp.where(first, both[1], both[0])
            x = jnp.where(low, a, pltpu.roll(b, 2 * TI, 1))
            y = jnp.where(low, pltpu.roll(a, LANES - 2 * TI, 1), b)
            sc[pl.ds((base + q) * TI, TI), :] = x
            sc[pl.ds((base + q + pairs) * TI, TI), :] = y

        def total(g, r):
            x = groups[g][0][r].astype(jnp.float32) + groups[g][1][r].astype(jnp.float32)
            return x.astype(jnp.bfloat16).astype(jnp.float32)

        for q in range(tails if parts else 0):
            tail = [jnp.zeros((TI, LANES), jnp.float32)] * 2
            for t in range(parts):
                x = [total(g, t * tails + q) for g in range(2)]
                place(t * tails + q, x)
                part = (lanes >= spare * t) & (lanes < spare * (t + 1))
                tail = [jnp.where(part, pltpu.roll(x[g], LANES - cols + spare * t, 1), tail[g]) for g in range(2)]
            place(main + q, tail)
        for q in range(0 if parts else pairs):
            place(q, [total(g, q) for g in range(2)])
    finish(sc, nts, mid_ref, gate_ref, wx_ref, out_ref)


def final_pairs(pos, pieces, mid, gate, wx):
    TI, C, J = mid.shape
    return pl.pallas_call(
        functools.partial(final_pairs_kernel, (C, J)),
        out_shape=jax.ShapeDtypeStruct((TI, J, C), jnp.bfloat16),
        in_specs=[smem()] + [vmem()] * (len(pieces) + 3),
        out_specs=vmem(),
        scratch_shapes=[pltpu.VMEM((C * TI, LANES), jnp.float32), pltpu.VMEM((TI // 2, C, 2 * LANES), jnp.bfloat16)],
        compiler_params=pltpu.CompilerParams(vmem_limit_bytes=VMEM_LIMIT),
    )(pos, *pieces, mid, gate, wx)


def shift(x, axis, d):
    n = lax.axis_size(axis)
    return lax.ppermute(x, axis, [(i, (i + d) % n) for i in range(n)])


def step_along(x, axis, d, t):
    n = lax.axis_size(axis)
    return lax.ppermute(x, axis, [(i, i + d) for i in range(n) if 0 <= i + d < n and 0 <= i - d * (t - 1) < n])


def across(x, d):
    nc = lax.axis_size("col")
    return lax.ppermute(x, ("col", "sub"), [(c * 2 + s, (c + d) % nc * 2 + 1 - s) for c in range(nc) for s in range(2)])


def per_device(
    homolog_activations,
    edge_activations,
    first_projection_matrix,
    second_projection_matrix,
    tensor_product_matrix,
    multiplicative_entry_matrix,
    multiplicative_exit_matrix,
):
    seqs, residues, features = homolog_activations.shape
    tile_rows, tile_cols, _ = edge_activations.shape
    fw = first_projection_matrix.shape[1]
    nr, nc, ns = (lax.axis_size(a) for a in ("row", "col", "sub"))
    assert ns == 2
    row, col, sub = (lax.axis_index(a) for a in ("row", "col", "sub"))
    pos = jnp.stack([row, col, sub]).astype(jnp.int32)
    sub_id = pos[2:]
    m = tile_cols // residues

    normed = standardize_features(homolog_activations.astype(jnp.float32)).astype(jnp.bfloat16).reshape(seqs * residues, features)

    def project(matrix):
        return jnp.dot(normed, matrix, preferred_element_type=jnp.float32).astype(jnp.bfloat16).reshape(seqs, residues * fw)

    right = project(second_projection_matrix)
    left = project(first_projection_matrix)

    span = tile_rows * fw
    fast = nr == 4 and nc == 2
    if fast:
        hops = [lax.ppermute(x, "row", [(i, i ^ d) for i in range(nr)]) for d, x in ((3, jnp.stack([right, left])), (2, right), (1, right))]
        left_x = shift(left, "col", 1)
        outer_weight, entry, exit_matrix = weights(tensor_product_matrix, multiplicative_entry_matrix, multiplicative_exit_matrix, fw)
        rows = jnp.stack([right, hops[2], hops[1], hops[0][0]])

        def rows_of(c):
            return [lax.dynamic_index_in_dim(rows, row ^ (c * m + t), 0, keepdims=False) for t in range(m)]

        got = shift(jnp.stack(rows_of(1 - col) + [hops[0][1]]), "col", 1)
        rights = jnp.stack([jnp.stack(rows_of(col)), got[:m]])
        lefts = jnp.stack([jnp.concatenate([left, left_x], axis=0), jnp.concatenate([hops[0][1], got[m]], axis=0)])
        far_edges = lax.ppermute(edge_activations, "row", [(0, nr - 1), (nr - 1, 0)])
        rights_other = shift(rights, "sub", 1)
        left_own = lax.dynamic_slice_in_dim(lefts, sub * span, span, 2)
        left_other = shift(lax.dynamic_slice_in_dim(lefts, (1 - sub) * span, span, 2), "sub", 1)
        right_t = prep(rights, rights_other, fw)
        mid, gate, lk, ls, rk, rs = pair(sub_id, left_own, left_other, 0, right_t, outer_weight, edge_activations, entry, tile_rows)
        up, down = [step_along(rk, "row", 1, 1)], [step_along(rk, "row", -1, 1)]
        rr = shift(rs, "sub", 1)
        up, down = up + [step_along(rr, "row", 1, 1)], down + [step_along(rr, "row", -1, 1)]
        lr = shift(ls, "sub", 1)
        far_k, far_s = pair(sub_id, left_own, left_other, 1, right_t, outer_weight, far_edges, entry, tile_rows, False)
        up2 = [step_along(x, "row", 1, 2) for x in up]
        down2 = [step_along(x, "row", -1, 2) for x in down]
        far = [far_k, shift(far_s, "sub", 1)]
        send1, send1o, keep1, keep1o, rest, resto = split_call(early_kernel, 3, (3, 2), 6, pos, lk, lr, [], [rk, rr, *up, *down, *far], tile_cols, nr)
        got1, got1o, keep1o = shift(send1, "col", 1), across(send1o, 1), shift(keep1o, "sub", 1)
        send2, send2o, keep2, keep2o = split_call(late_kernel, 1, (2,), 4, pos, lk, lr, [rest, resto], [*up2, *down2], tile_cols, nr)
        got2, got2o, keep2o = shift(send2, "col", 1), across(send2o, 1), shift(keep2o, "sub", 1)
        return final_pairs(pos, [keep1, got1, keep2, got2, keep1o, got1o, keep2o, got2o], mid, gate, exit_matrix)

    outer_weight, entry, exit_matrix = weights(tensor_product_matrix, multiplicative_entry_matrix, multiplicative_exit_matrix, fw)
    rows = jnp.stack([right] + [shift(right, "row", d) for d in range(1, nr)])

    def rows_of(c):
        return jnp.stack([lax.dynamic_index_in_dim(rows, lax.rem(row - (c * m + t) + nr, nr), 0, keepdims=False) for t in range(m)])

    rights, lefts = [rows_of(col)], [left]
    for d in range(1, nc):
        rights.append(shift(rows_of(lax.rem(col + d, nc)), "col", d))
        lefts.append(shift(left, "col", d))
    rights = jnp.stack(rights)
    lefts = jnp.concatenate(lefts, axis=0)[None]
    rights_other = shift(rights, "sub", 1)
    left_own = lax.dynamic_slice_in_dim(lefts, sub * span, span, 2)
    left_other = shift(lax.dynamic_slice_in_dim(lefts, (1 - sub) * span, span, 2), "sub", 1)
    right_t = prep(rights, rights_other, fw)
    mid, gate, lk, ls, rk, rs = pair(sub_id, left_own, left_other, 0, right_t, outer_weight, edge_activations, entry, tile_rows)

    rr = shift(rs, "sub", 1)
    lr = shift(ls, "sub", 1)
    slots = [rk, rr]
    up, down = [rk, rr], [rk, rr]
    for t in range(1, nr):
        up = [step_along(x, "row", 1, t) for x in up]
        down = [step_along(x, "row", -1, t) for x in down]
        slots += up + down
    partial = triangle(pos, lk, lr, slots, nr, nc, m, tile_cols)

    own, other = [partial[0]], [shift(partial[1], "sub", 1)]
    for d in range(1, nc):
        own.append(shift(partial[2 * d], "col", d))
        other.append(across(partial[2 * d + 1], d))
    return final(sub_id, own, other, mid, gate, exit_matrix)


def solution(mesh):
    in_specs = (
        P(("grp", "col", "sub"), "row", None),
        P(("grp", "row", "sub"), "col", None),
        P(),
        P(),
        P(),
        P(),
        P(),
    )
    out_specs = P(("grp", "row", "sub"), "col", None)

    return jax.shard_map(per_device, mesh=mesh, in_specs=in_specs, out_specs=out_specs, check_vma=False)
```

```python
import functools

import jax
import jax.numpy as jnp
from jax import lax
from jax.experimental import pallas as pl
from jax.experimental.pallas import tpu as pltpu
from jax.sharding import PartitionSpec as P


EPSILON = 1e-05
LANES = 128
VMEM_LIMIT = 60 * 1024 * 1024


def standardize_features(values):
    centred = values - jnp.mean(values, axis=-1, keepdims=True)
    spread = jnp.mean(centred * centred, axis=-1, keepdims=True)
    return centred * lax.rsqrt(spread + EPSILON)


def standardize_columns(values):
    centred = values - jnp.mean(values, axis=0, keepdims=True)
    spread = jnp.mean(centred * centred, axis=0, keepdims=True)
    return centred * lax.rsqrt(spread + EPSILON)


def vmem():
    return pl.BlockSpec(memory_space=pltpu.VMEM)


def smem():
    return pl.BlockSpec(memory_space=pltpu.SMEM)


def packing(count, cols):
    spare = -cols % LANES
    if spare and cols < LANES and cols % spare == 0:
        parts = cols // spare
        if count % (parts + 1) == 0:
            return parts, count // (parts + 1) * parts
    return 0, count


def lane_index(shape):
    return lax.broadcasted_iota(jnp.int32, shape, len(shape) - 1)


def weights_kernel(fw, w_ref, n_ref, x_ref, wt_ref, nt_ref, xt_ref, sc, st):
    C = w_ref.shape[1]
    sc[...] = w_ref[...].astype(jnp.float32)
    for b in range(fw):
        st[b * fw : (b + 1) * fw, :] = sc[pl.ds(b, fw, stride=fw), :]
    for t in range(fw * fw // C):
        wt_ref[:, t * C : (t + 1) * C] = st[t * C : (t + 1) * C, :].T.astype(jnp.bfloat16)
    for t in range(n_ref.shape[1] // C):
        nt_ref[t * C : (t + 1) * C, :] = n_ref[:, t * C : (t + 1) * C].astype(jnp.float32).T.astype(jnp.bfloat16)
    xt_ref[...] = x_ref[...].astype(jnp.float32).T.astype(jnp.bfloat16)


def weights(w, n, x, fw):
    K, C = w.shape
    bf = jnp.bfloat16
    return pl.pallas_call(
        functools.partial(weights_kernel, fw),
        out_shape=[jax.ShapeDtypeStruct((C, K), bf), jax.ShapeDtypeStruct(n.shape[::-1], bf), jax.ShapeDtypeStruct(x.shape[::-1], bf)],
        in_specs=[vmem()] * 3,
        out_specs=[vmem()] * 3,
        scratch_shapes=[pltpu.VMEM((K, C), jnp.float32)] * 2,
    )(w, n, x)


def prep_kernel(fw, own_ref, recv_ref, rt_ref, sc):
    groups, m, seqs, row_lanes = own_ref.shape
    res = row_lanes // fw
    chunk = sc.shape[2]
    pieces = [(ref, g) for ref in (own_ref, recv_ref) for g in range(groups)]
    per = chunk // seqs
    for u in range(len(pieces) // per):
        for mm in range(m):
            for t in range(row_lanes // LANES):
                block = jnp.concatenate(
                    [ref[g, mm, :, t * LANES : (t + 1) * LANES].astype(jnp.float32) for ref, g in pieces[u * per : (u + 1) * per]], axis=0
                )
                start = mm * row_lanes + t * LANES
                sc[u, start : start + LANES, :] = block.T
        for b in range(fw):
            rt_ref[b, :, u * chunk : (u + 1) * chunk] = sc[u, pl.ds(b, m * res, stride=fw), :].astype(jnp.bfloat16)


def prep(own, recv, fw):
    groups, m, seqs, row_lanes = own.shape
    total = 2 * groups * seqs
    chunk = min(total, LANES)
    cols = m * row_lanes // fw
    return pl.pallas_call(
        functools.partial(prep_kernel, fw),
        out_shape=jax.ShapeDtypeStruct((fw, cols, total), jnp.bfloat16),
        in_specs=[vmem(), vmem()],
        out_specs=vmem(),
        scratch_shapes=[pltpu.VMEM((total // chunk, m * row_lanes, chunk), jnp.float32)],
    )(own, recv)


def pair_kernel(cfg, sub_ref, l_ref, lr_ref, rt_ref, wt_ref, e_ref, went_ref, *rest):
    fw, C, J, S, full = cfg
    if full:
        mid_ref, gate_ref, lk_ref, ls_ref, rk_ref, rs_ref, lt, ot, nts, lsc, rsc = rest
    else:
        rk_ref, rs_ref, lt, ot, nts, rsc = rest
    half = C // 2
    IG = l_ref.shape[1] // fw
    wide = ot.shape[2] // 2
    for t in range(IG * fw // LANES):
        part = slice(t * LANES, (t + 1) * LANES)
        block = jnp.concatenate([l_ref[:, part].astype(jnp.float32), lr_ref[:, part].astype(jnp.float32)], axis=0)
        lt[part, :] = block.T.astype(jnp.bfloat16)
    ltv = lt[...]
    for b in range(fw):
        o = lax.dot_general(ltv, rt_ref[b], (((1,), (1,)), ((), ())), preferred_element_type=jnp.float32).astype(jnp.bfloat16)
        for i in range(IG):
            ot[i // 2, b * fw : (b + 1) * fw, i % 2 * wide : i % 2 * wide + J] = o[i * fw : (i + 1) * fw, :]
    wt = wt_ref[...]
    for h in range(IG // 2):
        pt = lax.dot_general(wt, ot[h], (((1,), (0,)), ((), ())), preferred_element_type=jnp.float32)
        for k in range(2):
            i = 2 * h + k
            et = e_ref[i].astype(jnp.float32).T
            mid = (et + pt[:, k * wide : k * wide + J] * (1.0 / S)).astype(jnp.bfloat16)
            if full:
                mid_ref[i] = mid
            nts[h, :, k * wide : k * wide + J] = standardize_columns(mid.astype(jnp.float32)).astype(jnp.bfloat16)

    def project(first, count, h):
        return lax.dot_general(went_ref[first * C : (first + count) * C, :], nts[h], (((1,), (0,)), ((), ())), preferred_element_type=jnp.float32)

    for h in range(IG // 2):
        if full:
            p = project(0, 2, h)
            x = jax.nn.sigmoid(p[C:]) * p[:C]
            for k in range(2):
                lsc[pl.ds((2 * h + k) * C, C), :J] = x[:, k * wide : k * wide + J]
        p = project(2, 2, h)
        x = jax.nn.sigmoid(p[C:]) * p[:C]
        for k in range(2):
            rsc[pl.ds((2 * h + k) * C, C), :J] = x[:, k * wide : k * wide + J]
        if full:
            x = jax.nn.sigmoid(project(4, 1, h)).astype(jnp.bfloat16)
            for k in range(2):
                gate_ref[2 * h + k] = x[:, k * wide : k * wide + J]
    sub = sub_ref[0]
    parts, main = packing(half, J)
    inside = lane_index((IG, LANES)) < J
    if full:
        for ref, base in ((lk_ref, sub * half), (ls_ref, (1 - sub) * half)):
            for ch in range(half):
                x = lsc[pl.ds(base + ch, IG, stride=C), :]
                ref[ch] = jnp.where(inside, x, 0.0).astype(jnp.bfloat16)
    for ref, base in ((rk_ref, sub * half), (rs_ref, (1 - sub) * half)):
        if parts == 0:
            for ch in range(half):
                x = rsc[pl.ds(base + ch, IG, stride=C), :]
                ref[ch] = jnp.where(inside, x, 0.0).astype(jnp.bfloat16)
        else:
            tails = half - main
            spare = LANES - J
            for q in range(tails):
                tail = rsc[pl.ds(base + main + q, IG, stride=C), :]
                for t in range(parts):
                    x = rsc[pl.ds(base + t * tails + q, IG, stride=C), :]
                    moved = pltpu.roll(tail, J - spare * t, 1)
                    ref[t * tails + q] = jnp.where(inside, x, moved).astype(jnp.bfloat16)


def pair(sub, l, lr, which, rt, wt, e, went, IG, full=True):
    _, part, IA = l.shape
    S = 2 * part
    fw, J, _ = rt.shape
    TI = IA // fw
    C = wt.shape[0]
    half = C // 2
    rows = packing(half, J)[1]
    wide = -(-J // LANES) * LANES
    bf = jnp.bfloat16
    tile = (jax.ShapeDtypeStruct((TI, C, J), bf), pl.BlockSpec((IG, C, J), lambda g: (g, 0, 0)))
    lefts = (jax.ShapeDtypeStruct((half, TI, LANES), bf), pl.BlockSpec((half, IG, LANES), lambda g: (0, g, 0)))
    rights = (jax.ShapeDtypeStruct((rows, TI, LANES), bf), pl.BlockSpec((rows, IG, LANES), lambda g: (0, g, 0)))
    outs = ([tile] * 2 + [lefts] * 2 if full else []) + [rights] * 2
    gated = pltpu.VMEM((IG * C, LANES), jnp.float32)
    f = pl.pallas_call(
        functools.partial(pair_kernel, (fw, C, J, S, full)),
        grid=(TI // IG,),
        out_shape=[o[0] for o in outs],
        in_specs=[
            smem(),
            pl.BlockSpec((None, part, IG * fw), lambda g: (which, 0, g)),
            pl.BlockSpec((None, part, IG * fw), lambda g: (which, 0, g)),
            pl.BlockSpec((fw, J, S), lambda g: (0, 0, 0)),
            pl.BlockSpec(wt.shape, lambda g: (0, 0)),
            pl.BlockSpec((IG, J, C), lambda g: (g, 0, 0)),
            pl.BlockSpec(went.shape, lambda g: (0, 0)),
        ],
        out_specs=[o[1] for o in outs],
        scratch_shapes=[
            pltpu.VMEM((IG * fw, S), bf),
            pltpu.VMEM((IG // 2, fw * fw, 2 * wide), bf),
            pltpu.VMEM((IG // 2, C, 2 * wide), bf),
            gated,
        ]
        + ([gated] if full else []),
        compiler_params=pltpu.CompilerParams(vmem_limit_bytes=VMEM_LIMIT),
        cost_estimate=pl.CostEstimate(flops=2 * TI * J * (S * fw * fw + fw * fw * C + 5 * C * C), bytes_accessed=4 * TI * J * C * 6, transcendentals=TI * J * C * 3),
    )
    return f(sub, l, lr, rt, wt, e, went)


def tri_kernel(cfg, n_slots, pos_ref, lk_ref, lr_ref, *rest):
    nr, nc, m, J = cfg
    slots = rest[:n_slots]
    outs = rest[n_slots : n_slots + 2 * nc]
    rv, lm, sem = rest[n_slots + 2 * nc :]
    half, TI, _ = lk_ref.shape
    row, col, sub = pos_ref[0], pos_ref[1], pos_ref[2]
    parts, main = packing(half, J)
    tails = half - main
    spare = LANES - J

    def copy(index):
        step, u = index // 2, index % 2
        hop = (step + 1) // 2
        origin = row - hop if step % 2 else row + hop
        return origin, pltpu.make_async_copy(slots[index], rv.at[jnp.clip(origin, 0, nr - 1), sub if u == 0 else 1 - sub], sem.at[index])

    for index in range(n_slots):
        origin, c = copy(index)

        @pl.when((origin >= 0) & (origin < nr))
        def _(c=c):
            c.start()

    inside = lane_index((2 * TI, LANES)) < J
    for ch in range(half):
        x = jnp.concatenate([lk_ref[ch], lr_ref[ch]], axis=0)
        if ch < main:
            lm[ch] = x
        else:
            f = x.astype(jnp.float32)
            for t in range(parts):
                moved = pltpu.roll(f, J - spare * t, 1)
                lm[main + (ch - main) * parts + t] = jnp.where(inside, 0.0, moved).astype(jnp.bfloat16)

    for index in range(n_slots):
        origin, c = copy(index)

        @pl.when((origin >= 0) & (origin < nr))
        def _(c=c):
            c.wait()

    def block(ch, start, pieces):
        right = rv[pl.ds(start, m), :, ch].reshape(m * 2 * TI, LANES)
        return lax.dot_general(lm[pieces], right, (((1,), (1,)), ((), ())), preferred_element_type=jnp.float32)

    for dc in range(nc):
        start = lax.rem(col + dc, nc) * m
        own_ref, other_ref = outs[2 * dc], outs[2 * dc + 1]
        for q in range(tails if parts else 0):
            tail = 0.0
            for t in range(parts):
                tail = tail + block(t * tails + q, start, main + q * parts + t)
            tail = jnp.concatenate([tail, jnp.zeros((2 * TI, spare), jnp.float32)], axis=1)
            for t in range(parts):
                x = block(t * tails + q, start, t * tails + q)
                x = jnp.concatenate([x, jnp.zeros((2 * TI, spare), jnp.float32)], axis=1)
                x = jnp.where(inside, x, pltpu.roll(tail, J - spare * t, 1)).astype(jnp.bfloat16)
                own_ref[t * tails + q] = x[:TI]
                other_ref[t * tails + q] = x[TI:]
        if not parts:
            for ch in range(half):
                x = block(ch, start, ch)
                if spare:
                    x = jnp.concatenate([x, jnp.zeros((2 * TI, spare), jnp.float32)], axis=1)
                x = x.astype(jnp.bfloat16)
                own_ref[ch] = x[:TI]
                other_ref[ch] = x[TI:]


def triangle(pos, lk, lr, slots, nr, nc, m, J):
    half, TI, _ = lk.shape
    parts, main = packing(half, J)
    rows = main
    bf = jnp.bfloat16
    n = len(slots)
    return pl.pallas_call(
        functools.partial(tri_kernel, (nr, nc, m, J), n),
        out_shape=[jax.ShapeDtypeStruct((rows, TI, LANES), bf)] * (2 * nc),
        in_specs=[smem(), vmem(), vmem()] + [pl.BlockSpec(memory_space=pl.ANY)] * n,
        out_specs=[vmem()] * (2 * nc),
        scratch_shapes=[
            pltpu.VMEM((nr, 2, rows, TI, LANES), bf),
            pltpu.VMEM((main + (half - main) * max(parts, 1), 2 * TI, LANES), bf),
            pltpu.SemaphoreType.DMA((n,)),
        ],
        compiler_params=pltpu.CompilerParams(vmem_limit_bytes=VMEM_LIMIT),
    )(pos, lk, lr, *slots)


def finish(sc, nts, mid_ref, gate_ref, wx_ref, out_ref):
    TI, C, J = mid_ref.shape
    wide = nts.shape[2] // 2
    wx = wx_ref[...]
    for i in range(TI):
        tri = sc[pl.ds(i, C, stride=TI), :][:, :J]
        nts[i // 2, :, i % 2 * wide : i % 2 * wide + J] = standardize_columns(tri).astype(jnp.bfloat16)
    for h in range(TI // 2):
        update = lax.dot_general(wx, nts[h], (((1,), (0,)), ((), ())), preferred_element_type=jnp.float32)
        for k in range(2):
            i = 2 * h + k
            res = mid_ref[i].astype(jnp.float32) + gate_ref[i].astype(jnp.float32) * update[:, k * wide : k * wide + J]
            out_ref[i] = res.T.astype(jnp.bfloat16)


def final_kernel(cfg, n, sub_ref, *rest):
    C, J = cfg
    own = rest[:n]
    other = rest[n : 2 * n]
    mid_ref, gate_ref, wx_ref, out_ref, sc, nts = rest[2 * n :]
    TI = mid_ref.shape[0]
    half = C // 2
    parts, main = packing(half, J)
    tails = half - main
    spare = LANES - J
    sub = sub_ref[0]
    lanes = lane_index((TI, LANES))
    for refs, base in ((own, sub * half), (other, (1 - sub) * half)):
        def total(ch, refs=refs):
            x = refs[0][ch].astype(jnp.float32)
            for ref in refs[1:]:
                x = x + ref[ch].astype(jnp.float32)
            return x.astype(jnp.bfloat16).astype(jnp.float32)

        for q in range(tails if parts else 0):
            tail = jnp.zeros((TI, LANES), jnp.float32)
            for t in range(parts):
                x = total(t * tails + q)
                sc[pl.ds((base + t * tails + q) * TI, TI), :] = x
                tail = jnp.where((lanes >= spare * t) & (lanes < spare * (t + 1)), pltpu.roll(x, LANES - J + spare * t, 1), tail)
            sc[pl.ds((base + main + q) * TI, TI), :] = tail
        if not parts:
            for ch in range(half):
                sc[pl.ds((base + ch) * TI, TI), :] = total(ch)
    finish(sc, nts, mid_ref, gate_ref, wx_ref, out_ref)


def final(sub, own, other, mid, gate, wx):
    TI, C, J = mid.shape
    n = len(own)
    return pl.pallas_call(
        functools.partial(final_kernel, (C, J), n),
        out_shape=jax.ShapeDtypeStruct((TI, J, C), jnp.bfloat16),
        in_specs=[smem()] + [vmem()] * (2 * n + 3),
        out_specs=vmem(),
        scratch_shapes=[pltpu.VMEM((C * TI, LANES), jnp.float32), pltpu.VMEM((TI // 2, C, 2 * LANES), jnp.bfloat16)],
        compiler_params=pltpu.CompilerParams(vmem_limit_bytes=VMEM_LIMIT),
    )(sub, *own, *other, mid, gate, wx)


def masked_left(lk_ref, lr_ref, lm, J):
    half, TI, _ = lk_ref.shape
    parts, main = packing(half, J)
    spare = LANES - J
    inside = lane_index((2 * TI, LANES)) < J
    for ch in range(main, half):
        f = jnp.concatenate([lk_ref[ch], lr_ref[ch]], axis=0).astype(jnp.float32)
        for t in range(parts):
            moved = pltpu.roll(f, J - spare * t, 1)
            lm[(ch - main) * parts + t] = jnp.where(inside, 0.0, moved).astype(jnp.bfloat16)


def shard_products(lk_ref, lr_ref, lm, rv, k, J, half, TI, store):
    parts, main = packing(half, J)
    tails = half - main

    def dot(left, row):
        right = rv[k, :, row].reshape(2 * TI, LANES)
        return lax.dot_general(left, right, (((1,), (1,)), ((), ())), preferred_element_type=jnp.float32)

    def channel(ch):
        if ch < main:
            return dot(jnp.concatenate([lk_ref[ch], lr_ref[ch]], axis=0), ch)
        q = ch - main
        x = dot(lm[q * parts], q)
        for t in range(1, parts):
            x = x + dot(lm[q * parts + t], t * tails + q)
        return x

    pairs = half // 2
    cols = 4 * TI
    pad = jnp.zeros((2 * TI, LANES - cols), jnp.float32)
    p2, m2 = packing(pairs, cols)
    t2 = pairs - m2

    def both(q):
        return jnp.concatenate([channel(q), channel(q + pairs), pad], axis=1)

    inside = lane_index((2 * TI, LANES)) < cols
    spare = LANES - cols
    for q in range(t2):
        tail = both(m2 + q)
        for t in range(p2):
            store(t * t2 + q, jnp.where(inside, both(t * t2 + q), pltpu.roll(tail, cols - spare * t, 1)).astype(jnp.bfloat16))
    for q in range(0 if p2 else pairs):
        store(q, both(q).astype(jnp.bfloat16))


def early_kernel(J, n, pos_ref, lk_ref, lr_ref, *rest):
    own, near, mids, far = rest[0:2], rest[2:4], rest[4:6], rest[6:8]
    outs = rest[8:14]
    rv, lm, acc, sem = rest[14:]
    half, TI, _ = lk_ref.shape
    row, col, sub = pos_ref[0], pos_ref[1], pos_ref[2]
    edge = (row == 0) | (row == n - 1)
    plan = [(None, own, 0), (None, near, 1), (edge, far, 2), (jnp.logical_not(edge), mids, 2)]

    def each(action):
        for cond, refs, k in plan:
            for u in range(2):
                c = pltpu.make_async_copy(refs[u], rv.at[k, sub if u == 0 else 1 - sub], sem.at[k, u])
                if cond is None:
                    action(c)
                else:
                    pl.when(cond)(lambda c=c: action(c))

    each(lambda c: c.start())
    masked_left(lk_ref, lr_ref, lm, J)
    each(lambda c: c.wait())
    for k in range(3):

        def store(r, x, k=k):
            acc[k, r] = x

        shard_products(lk_ref, lr_ref, lm, rv, k, J, half, TI, store)
    home = col == row // 2
    send = jnp.where(home, acc[2], acc[0])
    keep = jnp.where(home, acc[0], acc[2])
    for u in range(2):
        outs[u][...] = send[:, u * TI : (u + 1) * TI]
        outs[2 + u][...] = keep[:, u * TI : (u + 1) * TI]
        outs[4 + u][...] = acc[1, :, u * TI : (u + 1) * TI]


def late_kernel(J, n, pos_ref, lk_ref, lr_ref, a_ref, b_ref, *rest):
    inner, outward = rest[0:2], rest[2:4]
    outs = rest[4:8]
    rv, lm, acc, sem = rest[8:]
    half, TI, _ = lk_ref.shape
    row, col, sub = pos_ref[0], pos_ref[1], pos_ref[2]
    edge = (row == 0) | (row == n - 1)

    def each(action):
        for cond, refs in ((edge, outward), (jnp.logical_not(edge), inner)):
            for u in range(2):
                c = pltpu.make_async_copy(refs[u], rv.at[0, sub if u == 0 else 1 - sub], sem.at[u])
                pl.when(cond)(lambda c=c: action(c))

    each(lambda c: c.start())
    masked_left(lk_ref, lr_ref, lm, J)
    each(lambda c: c.wait())

    def store(r, x):
        acc[r] = x

    shard_products(lk_ref, lr_ref, lm, rv, 0, J, half, TI, store)
    home = col == row // 2
    for u, ref in enumerate((a_ref, b_ref)):
        late = acc[:, u * TI : (u + 1) * TI]
        early = ref[...]
        outs[u][...] = jnp.where(home, late, early)
        outs[2 + u][...] = jnp.where(home, early, late)


def split_call(kernel, shards, sems, n_out, pos, lk, lr, extra, slots, J, n):
    half, TI, _ = lk.shape
    parts, main = packing(half, J)
    rows = packing(half // 2, 4 * TI)[1]
    bf = jnp.bfloat16
    acc = (rows, 2 * TI, LANES)
    return pl.pallas_call(
        functools.partial(kernel, J, n),
        out_shape=[jax.ShapeDtypeStruct((rows, TI, LANES), bf)] * n_out,
        in_specs=[smem(), vmem(), vmem()] + [vmem()] * len(extra) + [pl.BlockSpec(memory_space=pl.ANY)] * len(slots),
        out_specs=[vmem()] * n_out,
        scratch_shapes=[
            pltpu.VMEM((shards, 2, main, TI, LANES), bf),
            pltpu.VMEM(((half - main) * max(parts, 1), 2 * TI, LANES), bf),
            pltpu.VMEM((shards,) + acc if shards > 1 else acc, bf),
            pltpu.SemaphoreType.DMA(sems),
        ],
        compiler_params=pltpu.CompilerParams(vmem_limit_bytes=VMEM_LIMIT),
        cost_estimate=pl.CostEstimate(flops=2 * shards * half * 48 * 48 * 512, bytes_accessed=shards * 2 * main * TI * LANES * 4, transcendentals=0),
    )(pos, lk, lr, *extra, *slots)


def add_group(C, TI, own, other, sub, sc):
    half = C // 2
    pairs = half // 2
    cols = 4 * TI
    parts, main = packing(pairs, cols)
    tails = pairs - main
    spare = LANES - cols
    lanes = lane_index((TI, LANES))
    for refs, base in ((own, sub * pairs), (other, (1 - sub) * pairs)):

        def put(q, x, base=base):
            sc[pl.ds((base + q) * TI, TI), :] = x

        def total(r, refs=refs):
            x = refs[0][r].astype(jnp.float32) + refs[1][r].astype(jnp.float32)
            return x.astype(jnp.bfloat16).astype(jnp.float32)

        for q in range(tails if parts else 0):
            tail = jnp.zeros((TI, LANES), jnp.float32)
            for t in range(parts):
                x = total(t * tails + q)
                put(t * tails + q, x)
                part = (lanes >= spare * t) & (lanes < spare * (t + 1))
                tail = jnp.where(part, pltpu.roll(x, LANES - cols + spare * t, 1), tail)
            put(main + q, tail)
        for q in range(0 if parts else pairs):
            put(q, total(q))


def group_updates(C, TI, sc, nts, wx_ref, emit):
    span = 2 * TI
    pairs = C // 4
    low = lane_index((C // 2, LANES)) < span
    for h in range(TI // 2):
        a = sc[pl.ds(2 * h, C // 2, stride=TI), :]
        b = sc[pl.ds(2 * h + 1, C // 2, stride=TI), :]
        x = jnp.where(low, a, pltpu.roll(b, span, 1))
        y = jnp.where(low, pltpu.roll(a, LANES - span, 1), b)
        tri = jnp.concatenate([x[:pairs], y[:pairs], x[pairs:], y[pairs:]], axis=0)
        nts[h // 2, :, h % 2 * LANES : (h % 2 + 1) * LANES] = standardize_columns(tri).astype(jnp.bfloat16)
    wx = wx_ref[...]
    for g in range(TI // 4):
        update = lax.dot_general(wx, nts[g], (((1,), (0,)), ((), ())), preferred_element_type=jnp.float32)
        for k in range(2):
            x = update[:, k * LANES : (k + 1) * LANES].T
            emit(4 * g + 2 * k, x[:span])
            emit(4 * g + 2 * k + 1, x[span : 2 * span])


def lower_half_first(pos_ref):
    home = pos_ref[1] == pos_ref[0] // 2
    odd = lax.rem(pos_ref[0], 2) == 1
    return jnp.where(home, jnp.logical_not(odd), odd)


def finish_early_kernel(pos_ref, a_ref, b_ref, c_ref, d_ref, mid_ref, gate_ref, wx_ref, out_ref, m_ref, g_ref, sc, nts):
    TI, C, _ = mid_ref.shape
    span = 2 * TI
    first = lower_half_first(pos_ref)
    add_group(C, TI, (a_ref, b_ref), (c_ref, d_ref), pos_ref[2], sc)

    def emit(i, update):
        mid = mid_ref[i].astype(jnp.float32).T
        gate = gate_ref[i].astype(jnp.float32).T
        m1, m2 = mid[:span], mid[span:]
        g1, g2 = gate[:span], gate[span:]
        out_ref[i] = (jnp.where(first, m1, m2) + jnp.where(first, g1, g2) * update).astype(jnp.bfloat16)
        m_ref[i] = jnp.where(first, m2, m1).astype(jnp.bfloat16)
        g_ref[i] = jnp.where(first, g2, g1).astype(jnp.bfloat16)

    group_updates(C, TI, sc, nts, wx_ref, emit)


def finish_late_kernel(pos_ref, a_ref, b_ref, c_ref, d_ref, early_ref, m_ref, g_ref, wx_ref, out_ref, sc, nts):
    TI, span, C = early_ref.shape
    first = lower_half_first(pos_ref)
    add_group(C, TI, (a_ref, b_ref), (c_ref, d_ref), pos_ref[2], sc)

    def emit(i, update):
        late = m_ref[i].astype(jnp.float32) + g_ref[i].astype(jnp.float32) * update
        early = early_ref[i].astype(jnp.float32)
        out_ref[i, :span] = jnp.where(first, early, late).astype(jnp.bfloat16)
        out_ref[i, span:] = jnp.where(first, late, early).astype(jnp.bfloat16)

    group_updates(C, TI, sc, nts, wx_ref, emit)


def finish_group(kernel, shapes, C, TI, *args):
    return pl.pallas_call(
        kernel,
        out_shape=[jax.ShapeDtypeStruct(x, jnp.bfloat16) for x in shapes],
        in_specs=[smem()] + [vmem()] * (len(args) - 1),
        out_specs=[vmem()] * len(shapes),
        scratch_shapes=[pltpu.VMEM((C // 2 * TI, LANES), jnp.float32), pltpu.VMEM((TI // 4, C, 2 * LANES), jnp.bfloat16)],
        compiler_params=pltpu.CompilerParams(vmem_limit_bytes=VMEM_LIMIT),
        cost_estimate=pl.CostEstimate(flops=2 * C * C * TI * 2 * TI, bytes_accessed=TI * TI * C * 20, transcendentals=0),
    )(*args)


def shift(x, axis, d):
    n = lax.axis_size(axis)
    return lax.ppermute(x, axis, [(i, (i + d) % n) for i in range(n)])


def step_along(x, axis, d, t):
    n = lax.axis_size(axis)
    return lax.ppermute(x, axis, [(i, i + d) for i in range(n) if 0 <= i + d < n and 0 <= i - d * (t - 1) < n])


def across(x, d):
    nc = lax.axis_size("col")
    return lax.ppermute(x, ("col", "sub"), [(c * 2 + s, (c + d) % nc * 2 + 1 - s) for c in range(nc) for s in range(2)])


def per_device(
    homolog_activations,
    edge_activations,
    first_projection_matrix,
    second_projection_matrix,
    tensor_product_matrix,
    multiplicative_entry_matrix,
    multiplicative_exit_matrix,
):
    seqs, residues, features = homolog_activations.shape
    tile_rows, tile_cols, width = edge_activations.shape
    fw = first_projection_matrix.shape[1]
    nr, nc, ns = (lax.axis_size(a) for a in ("row", "col", "sub"))
    assert ns == 2
    row, col, sub = (lax.axis_index(a) for a in ("row", "col", "sub"))
    pos = jnp.stack([row, col, sub]).astype(jnp.int32)
    sub_id = pos[2:]
    m = tile_cols // residues

    normed = standardize_features(homolog_activations.astype(jnp.float32)).astype(jnp.bfloat16).reshape(seqs * residues, features)

    def project(matrix):
        return jnp.dot(normed, matrix, preferred_element_type=jnp.float32).astype(jnp.bfloat16).reshape(seqs, residues * fw)

    right = project(second_projection_matrix)
    left = project(first_projection_matrix)

    span = tile_rows * fw
    fast = nr == 4 and nc == 2
    if fast:
        hops = [lax.ppermute(x, "row", [(i, i ^ d) for i in range(nr)]) for d, x in ((3, jnp.stack([right, left])), (2, right), (1, right))]
        left_x = shift(left, "col", 1)
        outer_weight, entry, exit_matrix = weights(tensor_product_matrix, multiplicative_entry_matrix, multiplicative_exit_matrix, fw)
        rows = jnp.stack([right, hops[2], hops[1], hops[0][0]])

        def rows_of(c):
            return [lax.dynamic_index_in_dim(rows, row ^ (c * m + t), 0, keepdims=False) for t in range(m)]

        got = shift(jnp.stack(rows_of(1 - col) + [hops[0][1]]), "col", 1)
        rights = jnp.stack([jnp.stack(rows_of(col)), got[:m]])
        lefts = jnp.stack([jnp.concatenate([left, left_x], axis=0), jnp.concatenate([hops[0][1], got[m]], axis=0)])
        far_edges = lax.ppermute(edge_activations, "row", [(0, nr - 1), (nr - 1, 0)])
        rights_other = shift(rights, "sub", 1)
        left_own = lax.dynamic_slice_in_dim(lefts, sub * span, span, 2)
        left_other = shift(lax.dynamic_slice_in_dim(lefts, (1 - sub) * span, span, 2), "sub", 1)
        right_t = prep(rights, rights_other, fw)
        mid, gate, lk, ls, rk, rs = pair(sub_id, left_own, left_other, 0, right_t, outer_weight, edge_activations, entry, tile_rows)
        outer = [(i, i ^ 1) for i in range(nr)]
        inner = [(1, 2), (2, 1)]
        outward = [(1, 0), (2, 3)]

        def along(x, pairs):
            return lax.ppermute(x, "row", pairs)

        near, mids = [along(rk, outer)], [along(rk, inner)]
        rr = shift(rs, "sub", 1)
        near, mids = near + [along(rr, outer)], mids + [along(rr, inner)]
        lr = shift(ls, "sub", 1)
        far_k, far_s = pair(sub_id, left_own, left_other, 1, right_t, outer_weight, far_edges, entry, tile_rows, False)
        last_in, last_out = [along(near[0], inner)], [along(mids[0], outward)]
        last_in, last_out = last_in + [along(near[1], inner)], last_out + [along(mids[1], outward)]
        far = [far_k, shift(far_s, "sub", 1)]
        send1, send1o, keep1, keep1o, rest, resto = split_call(early_kernel, 3, (3, 2), 6, pos, lk, lr, [], [rk, rr, *near, *mids, *far], tile_cols, nr)
        got1, got1o, keep1o = shift(send1, "col", 1), across(send1o, 1), shift(keep1o, "sub", 1)
        group = (tile_rows, 2 * tile_rows, width)
        done1, mid2, gate2 = finish_group(finish_early_kernel, [group] * 3, width, tile_rows, pos, keep1, got1, keep1o, got1o, mid, gate, exit_matrix)
        send2, send2o, keep2, keep2o = split_call(late_kernel, 1, (2,), 4, pos, lk, lr, [rest, resto], [*last_in, *last_out], tile_cols, nr)
        got2, got2o, keep2o = shift(send2, "col", 1), across(send2o, 1), shift(keep2o, "sub", 1)
        return finish_group(finish_late_kernel, [edge_activations.shape], width, tile_rows, pos, keep2, got2, keep2o, got2o, done1, mid2, gate2, exit_matrix)[0]

    outer_weight, entry, exit_matrix = weights(tensor_product_matrix, multiplicative_entry_matrix, multiplicative_exit_matrix, fw)
    rows = jnp.stack([right] + [shift(right, "row", d) for d in range(1, nr)])

    def rows_of(c):
        return jnp.stack([lax.dynamic_index_in_dim(rows, lax.rem(row - (c * m + t) + nr, nr), 0, keepdims=False) for t in range(m)])

    rights, lefts = [rows_of(col)], [left]
    for d in range(1, nc):
        rights.append(shift(rows_of(lax.rem(col + d, nc)), "col", d))
        lefts.append(shift(left, "col", d))
    rights = jnp.stack(rights)
    lefts = jnp.concatenate(lefts, axis=0)[None]
    rights_other = shift(rights, "sub", 1)
    left_own = lax.dynamic_slice_in_dim(lefts, sub * span, span, 2)
    left_other = shift(lax.dynamic_slice_in_dim(lefts, (1 - sub) * span, span, 2), "sub", 1)
    right_t = prep(rights, rights_other, fw)
    mid, gate, lk, ls, rk, rs = pair(sub_id, left_own, left_other, 0, right_t, outer_weight, edge_activations, entry, tile_rows)

    rr = shift(rs, "sub", 1)
    lr = shift(ls, "sub", 1)
    slots = [rk, rr]
    up, down = [rk, rr], [rk, rr]
    for t in range(1, nr):
        up = [step_along(x, "row", 1, t) for x in up]
        down = [step_along(x, "row", -1, t) for x in down]
        slots += up + down
    partial = triangle(pos, lk, lr, slots, nr, nc, m, tile_cols)

    own, other = [partial[0]], [shift(partial[1], "sub", 1)]
    for d in range(1, nc):
        own.append(shift(partial[2 * d], "col", d))
        other.append(across(partial[2 * d + 1], d))
    return final(sub_id, own, other, mid, gate, exit_matrix)


def solution(mesh):
    in_specs = (
        P(("grp", "col", "sub"), "row", None),
        P(("grp", "row", "sub"), "col", None),
        P(),
        P(),
        P(),
        P(),
        P(),
    )
    out_specs = P(("grp", "row", "sub"), "col", None)

    return jax.shard_map(per_device, mesh=mesh, in_specs=in_specs, out_specs=out_specs, check_vma=False)
```

```python
import functools

import jax
import jax.numpy as jnp
from jax import lax
from jax.experimental import pallas as pl
from jax.experimental.pallas import tpu as pltpu
from jax.sharding import PartitionSpec as P


EPSILON = 1e-05
LANES = 128
VMEM_LIMIT = 60 * 1024 * 1024


def grant(mib):
    return pltpu.CompilerParams(vmem_limit_bytes=mib * 1024 * 1024)


def standardize_features(values):
    centred = values - jnp.mean(values, axis=-1, keepdims=True)
    spread = jnp.mean(centred * centred, axis=-1, keepdims=True)
    return centred * lax.rsqrt(spread + EPSILON)


def standardize_columns(values):
    centred = values - jnp.mean(values, axis=0, keepdims=True)
    spread = jnp.mean(centred * centred, axis=0, keepdims=True)
    return centred * lax.rsqrt(spread + EPSILON)


def vmem():
    return pl.BlockSpec(memory_space=pltpu.VMEM)


def smem():
    return pl.BlockSpec(memory_space=pltpu.SMEM)


def packing(count, cols):
    spare = -cols % LANES
    if spare and cols < LANES and cols % spare == 0:
        parts = cols // spare
        if count % (parts + 1) == 0:
            return parts, count // (parts + 1) * parts
    return 0, count


def lane_index(shape):
    return lax.broadcasted_iota(jnp.int32, shape, len(shape) - 1)


def weights_kernel(fw, w_ref, n_ref, x_ref, wt_ref, nt_ref, xt_ref, sc, st):
    C = w_ref.shape[1]
    sc[...] = w_ref[...].astype(jnp.float32)
    for b in range(fw):
        st[b * fw : (b + 1) * fw, :] = sc[pl.ds(b, fw, stride=fw), :]
    for t in range(fw * fw // C):
        wt_ref[:, t * C : (t + 1) * C] = st[t * C : (t + 1) * C, :].T.astype(jnp.bfloat16)
    for t in range(n_ref.shape[1] // C):
        nt_ref[t * C : (t + 1) * C, :] = n_ref[:, t * C : (t + 1) * C].astype(jnp.float32).T.astype(jnp.bfloat16)
    xt_ref[...] = x_ref[...].astype(jnp.float32).T.astype(jnp.bfloat16)


def weights(w, n, x, fw):
    K, C = w.shape
    bf = jnp.bfloat16
    return pl.pallas_call(
        functools.partial(weights_kernel, fw),
        out_shape=[jax.ShapeDtypeStruct((C, K), bf), jax.ShapeDtypeStruct(n.shape[::-1], bf), jax.ShapeDtypeStruct(x.shape[::-1], bf)],
        in_specs=[vmem()] * 3,
        out_specs=[vmem()] * 3,
        scratch_shapes=[pltpu.VMEM((K, C), jnp.float32)] * 2,
        compiler_params=grant(4),
    )(w, n, x)


def prep_kernel(fw, own_ref, recv_ref, rt_ref, sc):
    groups, m, seqs, row_lanes = own_ref.shape
    res = row_lanes // fw
    chunk = sc.shape[2]
    pieces = [(ref, g) for ref in (own_ref, recv_ref) for g in range(groups)]
    per = chunk // seqs
    for u in range(len(pieces) // per):
        for mm in range(m):
            for t in range(row_lanes // LANES):
                block = jnp.concatenate(
                    [ref[g, mm, :, t * LANES : (t + 1) * LANES].astype(jnp.float32) for ref, g in pieces[u * per : (u + 1) * per]], axis=0
                )
                start = mm * row_lanes + t * LANES
                sc[u, start : start + LANES, :] = block.T
        for b in range(fw):
            rt_ref[b, :, u * chunk : (u + 1) * chunk] = sc[u, pl.ds(b, m * res, stride=fw), :].astype(jnp.bfloat16)


def prep(own, recv, fw):
    groups, m, seqs, row_lanes = own.shape
    total = 2 * groups * seqs
    chunk = min(total, LANES)
    cols = m * row_lanes // fw
    return pl.pallas_call(
        functools.partial(prep_kernel, fw),
        out_shape=jax.ShapeDtypeStruct((fw, cols, total), jnp.bfloat16),
        in_specs=[vmem(), vmem()],
        out_specs=vmem(),
        scratch_shapes=[pltpu.VMEM((total // chunk, m * row_lanes, chunk), jnp.float32)],
        compiler_params=grant(8),
    )(own, recv)


def pair_kernel(cfg, pos_ref, *refs):
    last = cfg[5]
    if last:
        pl.when((pos_ref[0] == 0) | (pos_ref[0] == last))(lambda: pair_body(cfg, pos_ref, *refs))
    else:
        pair_body(cfg, pos_ref, *refs)


def pair_body(cfg, pos_ref, l_ref, lr_ref, rt_ref, wt_ref, e_ref, went_ref, *rest):
    fw, C, J, S, full, _ = cfg
    if full:
        mid_ref, gate_ref, lk_ref, ls_ref, rk_ref, rs_ref, lt, ot, nts, lsc, rsc = rest
    else:
        rk_ref, rs_ref, lt, ot, nts, rsc = rest
    half = C // 2
    IG = l_ref.shape[1] // fw
    wide = ot.shape[2] // 2
    for t in range(IG * fw // LANES):
        part = slice(t * LANES, (t + 1) * LANES)
        block = jnp.concatenate([l_ref[:, part].astype(jnp.float32), lr_ref[:, part].astype(jnp.float32)], axis=0)
        lt[part, :] = block.T.astype(jnp.bfloat16)
    ltv = lt[...]
    for b in range(fw):
        o = lax.dot_general(ltv, rt_ref[b], (((1,), (1,)), ((), ())), preferred_element_type=jnp.float32).astype(jnp.bfloat16)
        for i in range(IG):
            ot[i // 2, b * fw : (b + 1) * fw, i % 2 * wide : i % 2 * wide + J] = o[i * fw : (i + 1) * fw, :]
    wt = wt_ref[...]
    for h in range(IG // 2):
        pt = lax.dot_general(wt, ot[h], (((1,), (0,)), ((), ())), preferred_element_type=jnp.float32)
        for k in range(2):
            i = 2 * h + k
            et = e_ref[i].astype(jnp.float32).T
            mid = (et + pt[:, k * wide : k * wide + J] * (1.0 / S)).astype(jnp.bfloat16)
            if full:
                mid_ref[i] = mid
            nts[h, :, k * wide : k * wide + J] = standardize_columns(mid.astype(jnp.float32)).astype(jnp.bfloat16)

    def project(first, count, h):
        return lax.dot_general(went_ref[first * C : (first + count) * C, :], nts[h], (((1,), (0,)), ((), ())), preferred_element_type=jnp.float32)

    for h in range(IG // 2):
        if full:
            p = project(0, 2, h)
            x = jax.nn.sigmoid(p[C:]) * p[:C]
            for k in range(2):
                lsc[pl.ds((2 * h + k) * C, C), :J] = x[:, k * wide : k * wide + J]
        p = project(2, 2, h)
        x = jax.nn.sigmoid(p[C:]) * p[:C]
        for k in range(2):
            rsc[pl.ds((2 * h + k) * C, C), :J] = x[:, k * wide : k * wide + J]
        if full:
            x = jax.nn.sigmoid(project(4, 1, h)).astype(jnp.bfloat16)
            for k in range(2):
                gate_ref[2 * h + k] = x[:, k * wide : k * wide + J]
    sub = pos_ref[2]
    parts, main = packing(half, J)
    inside = lane_index((IG, LANES)) < J
    if full:
        for ref, base in ((lk_ref, sub * half), (ls_ref, (1 - sub) * half)):
            for ch in range(half):
                x = lsc[pl.ds(base + ch, IG, stride=C), :]
                ref[ch] = jnp.where(inside, x, 0.0).astype(jnp.bfloat16)
    for ref, base in ((rk_ref, sub * half), (rs_ref, (1 - sub) * half)):
        if parts == 0:
            for ch in range(half):
                x = rsc[pl.ds(base + ch, IG, stride=C), :]
                ref[ch] = jnp.where(inside, x, 0.0).astype(jnp.bfloat16)
        else:
            tails = half - main
            spare = LANES - J
            for q in range(tails):
                tail = rsc[pl.ds(base + main + q, IG, stride=C), :]
                for t in range(parts):
                    x = rsc[pl.ds(base + t * tails + q, IG, stride=C), :]
                    moved = pltpu.roll(tail, J - spare * t, 1)
                    ref[t * tails + q] = jnp.where(inside, x, moved).astype(jnp.bfloat16)


def pair(pos, l, lr, which, rt, wt, e, went, IG, last=0):
    full = not last
    _, part, IA = l.shape
    S = 2 * part
    fw, J, _ = rt.shape
    TI = IA // fw
    C = wt.shape[0]
    half = C // 2
    rows = packing(half, J)[1]
    wide = -(-J // LANES) * LANES
    bf = jnp.bfloat16
    tile = (jax.ShapeDtypeStruct((TI, C, J), bf), pl.BlockSpec((IG, C, J), lambda g: (g, 0, 0)))
    lefts = (jax.ShapeDtypeStruct((half, TI, LANES), bf), pl.BlockSpec((half, IG, LANES), lambda g: (0, g, 0)))
    rights = (jax.ShapeDtypeStruct((rows, TI, LANES), bf), pl.BlockSpec((rows, IG, LANES), lambda g: (0, g, 0)))
    outs = ([tile] * 2 + [lefts] * 2 if full else []) + [rights] * 2
    gated = pltpu.VMEM((IG * C, LANES), jnp.float32)
    f = pl.pallas_call(
        functools.partial(pair_kernel, (fw, C, J, S, full, last)),
        grid=(TI // IG,),
        out_shape=[o[0] for o in outs],
        in_specs=[
            smem(),
            pl.BlockSpec((None, part, IG * fw), lambda g: (which, 0, g)),
            pl.BlockSpec((None, part, IG * fw), lambda g: (which, 0, g)),
            pl.BlockSpec((fw, J, S), lambda g: (0, 0, 0)),
            pl.BlockSpec(wt.shape, lambda g: (0, 0)),
            pl.BlockSpec((IG, J, C), lambda g: (g, 0, 0)),
            pl.BlockSpec(went.shape, lambda g: (0, 0)),
        ],
        out_specs=[o[1] for o in outs],
        scratch_shapes=[
            pltpu.VMEM((IG * fw, S), bf),
            pltpu.VMEM((IG // 2, fw * fw, 2 * wide), bf),
            pltpu.VMEM((IG // 2, C, 2 * wide), bf),
            gated,
        ]
        + ([gated] if full else []),
        compiler_params=grant(28),
        cost_estimate=pl.CostEstimate(flops=2 * TI * J * (S * fw * fw + fw * fw * C + 5 * C * C), bytes_accessed=4 * TI * J * C * 6, transcendentals=TI * J * C * 3),
    )
    return f(pos, l, lr, rt, wt, e, went)


def tri_kernel(cfg, n_slots, pos_ref, lk_ref, lr_ref, *rest):
    nr, nc, m, J = cfg
    slots = rest[:n_slots]
    outs = rest[n_slots : n_slots + 2 * nc]
    rv, lm, sem = rest[n_slots + 2 * nc :]
    half, TI, _ = lk_ref.shape
    row, col, sub = pos_ref[0], pos_ref[1], pos_ref[2]
    parts, main = packing(half, J)
    tails = half - main
    spare = LANES - J

    def copy(index):
        step, u = index // 2, index % 2
        hop = (step + 1) // 2
        origin = row - hop if step % 2 else row + hop
        return origin, pltpu.make_async_copy(slots[index], rv.at[jnp.clip(origin, 0, nr - 1), sub if u == 0 else 1 - sub], sem.at[index])

    for index in range(n_slots):
        origin, c = copy(index)

        @pl.when((origin >= 0) & (origin < nr))
        def _(c=c):
            c.start()

    inside = lane_index((2 * TI, LANES)) < J
    for ch in range(half):
        x = jnp.concatenate([lk_ref[ch], lr_ref[ch]], axis=0)
        if ch < main:
            lm[ch] = x
        else:
            f = x.astype(jnp.float32)
            for t in range(parts):
                moved = pltpu.roll(f, J - spare * t, 1)
                lm[main + (ch - main) * parts + t] = jnp.where(inside, 0.0, moved).astype(jnp.bfloat16)

    for index in range(n_slots):
        origin, c = copy(index)

        @pl.when((origin >= 0) & (origin < nr))
        def _(c=c):
            c.wait()

    def block(ch, start, pieces):
        right = rv[pl.ds(start, m), :, ch].reshape(m * 2 * TI, LANES)
        return lax.dot_general(lm[pieces], right, (((1,), (1,)), ((), ())), preferred_element_type=jnp.float32)

    for dc in range(nc):
        start = lax.rem(col + dc, nc) * m
        own_ref, other_ref = outs[2 * dc], outs[2 * dc + 1]
        for q in range(tails if parts else 0):
            tail = 0.0
            for t in range(parts):
                tail = tail + block(t * tails + q, start, main + q * parts + t)
            tail = jnp.concatenate([tail, jnp.zeros((2 * TI, spare), jnp.float32)], axis=1)
            for t in range(parts):
                x = block(t * tails + q, start, t * tails + q)
                x = jnp.concatenate([x, jnp.zeros((2 * TI, spare), jnp.float32)], axis=1)
                x = jnp.where(inside, x, pltpu.roll(tail, J - spare * t, 1)).astype(jnp.bfloat16)
                own_ref[t * tails + q] = x[:TI]
                other_ref[t * tails + q] = x[TI:]
        if not parts:
            for ch in range(half):
                x = block(ch, start, ch)
                if spare:
                    x = jnp.concatenate([x, jnp.zeros((2 * TI, spare), jnp.float32)], axis=1)
                x = x.astype(jnp.bfloat16)
                own_ref[ch] = x[:TI]
                other_ref[ch] = x[TI:]


def triangle(pos, lk, lr, slots, nr, nc, m, J):
    half, TI, _ = lk.shape
    parts, main = packing(half, J)
    rows = main
    bf = jnp.bfloat16
    n = len(slots)
    return pl.pallas_call(
        functools.partial(tri_kernel, (nr, nc, m, J), n),
        out_shape=[jax.ShapeDtypeStruct((rows, TI, LANES), bf)] * (2 * nc),
        in_specs=[smem(), vmem(), vmem()] + [pl.BlockSpec(memory_space=pl.ANY)] * n,
        out_specs=[vmem()] * (2 * nc),
        scratch_shapes=[
            pltpu.VMEM((nr, 2, rows, TI, LANES), bf),
            pltpu.VMEM((main + (half - main) * max(parts, 1), 2 * TI, LANES), bf),
            pltpu.SemaphoreType.DMA((n,)),
        ],
        compiler_params=pltpu.CompilerParams(vmem_limit_bytes=VMEM_LIMIT),
    )(pos, lk, lr, *slots)


def finish(sc, nts, mid_ref, gate_ref, wx_ref, out_ref):
    TI, C, J = mid_ref.shape
    wide = nts.shape[2] // 2
    wx = wx_ref[...]
    for i in range(TI):
        tri = sc[pl.ds(i, C, stride=TI), :][:, :J]
        nts[i // 2, :, i % 2 * wide : i % 2 * wide + J] = standardize_columns(tri).astype(jnp.bfloat16)
    for h in range(TI // 2):
        update = lax.dot_general(wx, nts[h], (((1,), (0,)), ((), ())), preferred_element_type=jnp.float32)
        for k in range(2):
            i = 2 * h + k
            res = mid_ref[i].astype(jnp.float32) + gate_ref[i].astype(jnp.float32) * update[:, k * wide : k * wide + J]
            out_ref[i] = res.T.astype(jnp.bfloat16)


def final_kernel(cfg, n, sub_ref, *rest):
    C, J = cfg
    own = rest[:n]
    other = rest[n : 2 * n]
    mid_ref, gate_ref, wx_ref, out_ref, sc, nts = rest[2 * n :]
    TI = mid_ref.shape[0]
    half = C // 2
    parts, main = packing(half, J)
    tails = half - main
    spare = LANES - J
    sub = sub_ref[0]
    lanes = lane_index((TI, LANES))
    for refs, base in ((own, sub * half), (other, (1 - sub) * half)):
        def total(ch, refs=refs):
            x = refs[0][ch].astype(jnp.float32)
            for ref in refs[1:]:
                x = x + ref[ch].astype(jnp.float32)
            return x.astype(jnp.bfloat16).astype(jnp.float32)

        for q in range(tails if parts else 0):
            tail = jnp.zeros((TI, LANES), jnp.float32)
            for t in range(parts):
                x = total(t * tails + q)
                sc[pl.ds((base + t * tails + q) * TI, TI), :] = x
                tail = jnp.where((lanes >= spare * t) & (lanes < spare * (t + 1)), pltpu.roll(x, LANES - J + spare * t, 1), tail)
            sc[pl.ds((base + main + q) * TI, TI), :] = tail
        if not parts:
            for ch in range(half):
                sc[pl.ds((base + ch) * TI, TI), :] = total(ch)
    finish(sc, nts, mid_ref, gate_ref, wx_ref, out_ref)


def final(sub, own, other, mid, gate, wx):
    TI, C, J = mid.shape
    n = len(own)
    return pl.pallas_call(
        functools.partial(final_kernel, (C, J), n),
        out_shape=jax.ShapeDtypeStruct((TI, J, C), jnp.bfloat16),
        in_specs=[smem()] + [vmem()] * (2 * n + 3),
        out_specs=vmem(),
        scratch_shapes=[pltpu.VMEM((C * TI, LANES), jnp.float32), pltpu.VMEM((TI // 2, C, 2 * LANES), jnp.bfloat16)],
        compiler_params=pltpu.CompilerParams(vmem_limit_bytes=VMEM_LIMIT),
    )(sub, *own, *other, mid, gate, wx)


def masked_left(lk_ref, lr_ref, lm, J):
    half, TI, _ = lk_ref.shape
    parts, main = packing(half, J)
    spare = LANES - J
    inside = lane_index((2 * TI, LANES)) < J
    for ch in range(main, half):
        f = jnp.concatenate([lk_ref[ch], lr_ref[ch]], axis=0).astype(jnp.float32)
        for t in range(parts):
            moved = pltpu.roll(f, J - spare * t, 1)
            lm[(ch - main) * parts + t] = jnp.where(inside, 0.0, moved).astype(jnp.bfloat16)


def shard_products(lk_ref, lr_ref, lm, rv, k, J, half, TI, store):
    parts, main = packing(half, J)
    tails = half - main

    def dot(left, row):
        right = rv[k, :, row].reshape(2 * TI, LANES)
        return lax.dot_general(left, right, (((1,), (1,)), ((), ())), preferred_element_type=jnp.float32)

    def channel(ch):
        if ch < main:
            return dot(jnp.concatenate([lk_ref[ch], lr_ref[ch]], axis=0), ch)
        q = ch - main
        x = dot(lm[q * parts], q)
        for t in range(1, parts):
            x = x + dot(lm[q * parts + t], t * tails + q)
        return x

    pairs = half // 2
    cols = 4 * TI
    pad = jnp.zeros((2 * TI, LANES - cols), jnp.float32)
    p2, m2 = packing(pairs, cols)
    t2 = pairs - m2

    def both(q):
        return jnp.concatenate([channel(q), channel(q + pairs), pad], axis=1)

    inside = lane_index((2 * TI, LANES)) < cols
    spare = LANES - cols
    for q in range(t2):
        tail = both(m2 + q)
        for t in range(p2):
            store(t * t2 + q, jnp.where(inside, both(t * t2 + q), pltpu.roll(tail, cols - spare * t, 1)).astype(jnp.bfloat16))
    for q in range(0 if p2 else pairs):
        store(q, both(q).astype(jnp.bfloat16))


def early_kernel(J, n, pos_ref, lk_ref, lr_ref, *rest):
    own, near, mids, far = rest[0:2], rest[2:4], rest[4:6], rest[6:8]
    outs = rest[8:14]
    rv, lm, acc, sem = rest[14:]
    half, TI, _ = lk_ref.shape
    row, col, sub = pos_ref[0], pos_ref[1], pos_ref[2]
    edge = (row == 0) | (row == n - 1)
    plan = [(None, own, 0), (None, near, 1), (edge, far, 2), (jnp.logical_not(edge), mids, 2)]

    def each(action):
        for cond, refs, k in plan:
            for u in range(2):
                c = pltpu.make_async_copy(refs[u], rv.at[k, sub if u == 0 else 1 - sub], sem.at[k, u])
                if cond is None:
                    action(c)
                else:
                    pl.when(cond)(lambda c=c: action(c))

    each(lambda c: c.start())
    masked_left(lk_ref, lr_ref, lm, J)
    each(lambda c: c.wait())
    for k in range(3):

        def store(r, x, k=k):
            acc[k, r] = x

        shard_products(lk_ref, lr_ref, lm, rv, k, J, half, TI, store)
    home = col == row // 2
    send = jnp.where(home, acc[2], acc[0])
    keep = jnp.where(home, acc[0], acc[2])
    for u in range(2):
        outs[u][...] = send[:, u * TI : (u + 1) * TI]
        outs[2 + u][...] = keep[:, u * TI : (u + 1) * TI]
        outs[4 + u][...] = acc[1, :, u * TI : (u + 1) * TI]


def late_kernel(J, n, pos_ref, lk_ref, lr_ref, a_ref, b_ref, *rest):
    inner, outward = rest[0:2], rest[2:4]
    outs = rest[4:8]
    rv, lm, acc, sem = rest[8:]
    half, TI, _ = lk_ref.shape
    row, col, sub = pos_ref[0], pos_ref[1], pos_ref[2]
    edge = (row == 0) | (row == n - 1)

    def each(action):
        for cond, refs in ((edge, outward), (jnp.logical_not(edge), inner)):
            for u in range(2):
                c = pltpu.make_async_copy(refs[u], rv.at[0, sub if u == 0 else 1 - sub], sem.at[u])
                pl.when(cond)(lambda c=c: action(c))

    each(lambda c: c.start())
    masked_left(lk_ref, lr_ref, lm, J)
    each(lambda c: c.wait())

    def store(r, x):
        acc[r] = x

    shard_products(lk_ref, lr_ref, lm, rv, 0, J, half, TI, store)
    home = col == row // 2
    for u, ref in enumerate((a_ref, b_ref)):
        late = acc[:, u * TI : (u + 1) * TI]
        early = ref[...]
        outs[u][...] = jnp.where(home, late, early)
        outs[2 + u][...] = jnp.where(home, early, late)


def split_call(kernel, shards, sems, n_out, pos, lk, lr, extra, slots, J, n):
    half, TI, _ = lk.shape
    parts, main = packing(half, J)
    rows = packing(half // 2, 4 * TI)[1]
    bf = jnp.bfloat16
    acc = (rows, 2 * TI, LANES)
    return pl.pallas_call(
        functools.partial(kernel, J, n),
        out_shape=[jax.ShapeDtypeStruct((rows, TI, LANES), bf)] * n_out,
        in_specs=[smem(), vmem(), vmem()] + [vmem()] * len(extra) + [pl.BlockSpec(memory_space=pl.ANY)] * len(slots),
        out_specs=[vmem()] * n_out,
        scratch_shapes=[
            pltpu.VMEM((shards, 2, main, TI, LANES), bf),
            pltpu.VMEM(((half - main) * max(parts, 1), 2 * TI, LANES), bf),
            pltpu.VMEM((shards,) + acc if shards > 1 else acc, bf),
            pltpu.SemaphoreType.DMA(sems),
        ],
        compiler_params=grant(12 if shards > 1 else 6),
        cost_estimate=pl.CostEstimate(flops=2 * shards * half * 48 * 48 * 512, bytes_accessed=shards * 2 * main * TI * LANES * 4, transcendentals=0),
    )(pos, lk, lr, *extra, *slots)


def add_group(C, TI, own, other, sub, sc):
    half = C // 2
    pairs = half // 2
    cols = 4 * TI
    parts, main = packing(pairs, cols)
    tails = pairs - main
    spare = LANES - cols
    lanes = lane_index((TI, LANES))
    for refs, base in ((own, sub * pairs), (other, (1 - sub) * pairs)):

        def put(q, x, base=base):
            sc[pl.ds((base + q) * TI, TI), :] = x

        def total(r, refs=refs):
            x = refs[0][r].astype(jnp.float32) + refs[1][r].astype(jnp.float32)
            return x.astype(jnp.bfloat16).astype(jnp.float32)

        for q in range(tails if parts else 0):
            tail = jnp.zeros((TI, LANES), jnp.float32)
            for t in range(parts):
                x = total(t * tails + q)
                put(t * tails + q, x)
                part = (lanes >= spare * t) & (lanes < spare * (t + 1))
                tail = jnp.where(part, pltpu.roll(x, LANES - cols + spare * t, 1), tail)
            put(main + q, tail)
        for q in range(0 if parts else pairs):
            put(q, total(q))


def group_updates(C, TI, sc, nts, wx_ref, emit):
    span = 2 * TI
    pairs = C // 4
    low = lane_index((C // 2, LANES)) < span
    for h in range(TI // 2):
        a = sc[pl.ds(2 * h, C // 2, stride=TI), :]
        b = sc[pl.ds(2 * h + 1, C // 2, stride=TI), :]
        x = jnp.where(low, a, pltpu.roll(b, span, 1))
        y = jnp.where(low, pltpu.roll(a, LANES - span, 1), b)
        tri = jnp.concatenate([x[:pairs], y[:pairs], x[pairs:], y[pairs:]], axis=0)
        nts[h // 2, :, h % 2 * LANES : (h % 2 + 1) * LANES] = standardize_columns(tri).astype(jnp.bfloat16)
    wx = wx_ref[...]
    for g in range(TI // 4):
        update = lax.dot_general(wx, nts[g], (((1,), (0,)), ((), ())), preferred_element_type=jnp.float32)
        for k in range(2):
            x = update[:, k * LANES : (k + 1) * LANES].T
            emit(4 * g + 2 * k, x[:span])
            emit(4 * g + 2 * k + 1, x[span : 2 * span])


def lower_half_first(pos_ref):
    home = pos_ref[1] == pos_ref[0] // 2
    odd = lax.rem(pos_ref[0], 2) == 1
    return jnp.where(home, jnp.logical_not(odd), odd)


def finish_early_kernel(pos_ref, a_ref, b_ref, c_ref, d_ref, mid_ref, gate_ref, wx_ref, out_ref, m_ref, g_ref, sc, nts):
    TI, C, _ = mid_ref.shape
    span = 2 * TI
    first = lower_half_first(pos_ref)
    add_group(C, TI, (a_ref, b_ref), (c_ref, d_ref), pos_ref[2], sc)

    def emit(i, update):
        mid = mid_ref[i].astype(jnp.float32).T
        gate = gate_ref[i].astype(jnp.float32).T
        m1, m2 = mid[:span], mid[span:]
        g1, g2 = gate[:span], gate[span:]
        out_ref[i] = (jnp.where(first, m1, m2) + jnp.where(first, g1, g2) * update).astype(jnp.bfloat16)
        m_ref[i] = jnp.where(first, m2, m1).astype(jnp.bfloat16)
        g_ref[i] = jnp.where(first, g2, g1).astype(jnp.bfloat16)

    group_updates(C, TI, sc, nts, wx_ref, emit)


def finish_late_kernel(pos_ref, a_ref, b_ref, c_ref, d_ref, early_ref, m_ref, g_ref, wx_ref, out_ref, sc, nts):
    TI, span, C = early_ref.shape
    first = lower_half_first(pos_ref)
    add_group(C, TI, (a_ref, b_ref), (c_ref, d_ref), pos_ref[2], sc)

    def emit(i, update):
        late = m_ref[i].astype(jnp.float32) + g_ref[i].astype(jnp.float32) * update
        early = early_ref[i].astype(jnp.float32)
        out_ref[i, :span] = jnp.where(first, early, late).astype(jnp.bfloat16)
        out_ref[i, span:] = jnp.where(first, late, early).astype(jnp.bfloat16)

    group_updates(C, TI, sc, nts, wx_ref, emit)


def finish_group(kernel, shapes, C, TI, *args):
    return pl.pallas_call(
        kernel,
        out_shape=[jax.ShapeDtypeStruct(x, jnp.bfloat16) for x in shapes],
        in_specs=[smem()] + [vmem()] * (len(args) - 1),
        out_specs=[vmem()] * len(shapes),
        scratch_shapes=[pltpu.VMEM((C // 2 * TI, LANES), jnp.float32), pltpu.VMEM((TI // 4, C, 2 * LANES), jnp.bfloat16)],
        compiler_params=grant(8),
        cost_estimate=pl.CostEstimate(flops=2 * C * C * TI * 2 * TI, bytes_accessed=TI * TI * C * 20, transcendentals=0),
    )(*args)


def shift(x, axis, d):
    n = lax.axis_size(axis)
    return lax.ppermute(x, axis, [(i, (i + d) % n) for i in range(n)])


def step_along(x, axis, d, t):
    n = lax.axis_size(axis)
    return lax.ppermute(x, axis, [(i, i + d) for i in range(n) if 0 <= i + d < n and 0 <= i - d * (t - 1) < n])


def across(x, d):
    nc = lax.axis_size("col")
    return lax.ppermute(x, ("col", "sub"), [(c * 2 + s, (c + d) % nc * 2 + 1 - s) for c in range(nc) for s in range(2)])


def per_device(
    homolog_activations,
    edge_activations,
    first_projection_matrix,
    second_projection_matrix,
    tensor_product_matrix,
    multiplicative_entry_matrix,
    multiplicative_exit_matrix,
):
    seqs, residues, features = homolog_activations.shape
    tile_rows, tile_cols, width = edge_activations.shape
    fw = first_projection_matrix.shape[1]
    nr, nc, ns = (lax.axis_size(a) for a in ("row", "col", "sub"))
    assert ns == 2
    row, col, sub = (lax.axis_index(a) for a in ("row", "col", "sub"))
    pos = jnp.stack([row, col, sub]).astype(jnp.int32)
    sub_id = pos[2:]
    m = tile_cols // residues

    normed = standardize_features(homolog_activations.astype(jnp.float32)).astype(jnp.bfloat16).reshape(seqs * residues, features)

    def project(matrix):
        return jnp.dot(normed, matrix, preferred_element_type=jnp.float32).astype(jnp.bfloat16).reshape(seqs, residues * fw)

    right = project(second_projection_matrix)
    left = project(first_projection_matrix)

    span = tile_rows * fw
    fast = nr == 4 and nc == 2
    if fast:
        hops = [lax.ppermute(x, "row", [(i, i ^ d) for i in range(nr)]) for d, x in ((3, jnp.stack([right, left])), (2, right), (1, right))]
        left_x = shift(left, "col", 1)
        outer_weight, entry, exit_matrix = weights(tensor_product_matrix, multiplicative_entry_matrix, multiplicative_exit_matrix, fw)
        rows = jnp.stack([right, hops[2], hops[1], hops[0][0]])

        def rows_of(c):
            return [lax.dynamic_index_in_dim(rows, row ^ (c * m + t), 0, keepdims=False) for t in range(m)]

        got = shift(jnp.stack(rows_of(1 - col) + [hops[0][1]]), "col", 1)
        rights = jnp.stack([jnp.stack(rows_of(col)), got[:m]])
        lefts = jnp.stack([jnp.concatenate([left, left_x], axis=0), jnp.concatenate([hops[0][1], got[m]], axis=0)])
        far_edges = lax.ppermute(edge_activations, "row", [(0, nr - 1), (nr - 1, 0)])
        rights_other = shift(rights, "sub", 1)
        left_own = lax.dynamic_slice_in_dim(lefts, sub * span, span, 2)
        left_other = shift(lax.dynamic_slice_in_dim(lefts, (1 - sub) * span, span, 2), "sub", 1)
        right_t = prep(rights, rights_other, fw)
        mid, gate, lk, ls, rk, rs = pair(pos, left_own, left_other, 0, right_t, outer_weight, edge_activations, entry, tile_rows)
        outer = [(i, i ^ 1) for i in range(nr)]
        inner = [(1, 2), (2, 1)]
        outward = [(1, 0), (2, 3)]

        def along(x, pairs):
            return lax.ppermute(x, "row", pairs)

        near, mids = [along(rk, outer)], [along(rk, inner)]
        rr = shift(rs, "sub", 1)
        near, mids = near + [along(rr, outer)], mids + [along(rr, inner)]
        lr = shift(ls, "sub", 1)
        far_k, far_s = pair(pos, left_own, left_other, 1, right_t, outer_weight, far_edges, entry, tile_rows, nr - 1)
        last_in, last_out = [along(near[0], inner)], [along(mids[0], outward)]
        last_in, last_out = last_in + [along(near[1], inner)], last_out + [along(mids[1], outward)]
        far = [far_k, shift(far_s, "sub", 1)]
        send1, send1o, keep1, keep1o, rest, resto = split_call(early_kernel, 3, (3, 2), 6, pos, lk, lr, [], [rk, rr, *near, *mids, *far], tile_cols, nr)
        got1, got1o, keep1o = shift(send1, "col", 1), across(send1o, 1), shift(keep1o, "sub", 1)
        group = (tile_rows, 2 * tile_rows, width)
        done1, mid2, gate2 = finish_group(finish_early_kernel, [group] * 3, width, tile_rows, pos, keep1, got1, keep1o, got1o, mid, gate, exit_matrix)
        send2, send2o, keep2, keep2o = split_call(late_kernel, 1, (2,), 4, pos, lk, lr, [rest, resto], [*last_in, *last_out], tile_cols, nr)
        got2, got2o, keep2o = shift(send2, "col", 1), across(send2o, 1), shift(keep2o, "sub", 1)
        return finish_group(finish_late_kernel, [edge_activations.shape], width, tile_rows, pos, keep2, got2, keep2o, got2o, done1, mid2, gate2, exit_matrix)[0]

    outer_weight, entry, exit_matrix = weights(tensor_product_matrix, multiplicative_entry_matrix, multiplicative_exit_matrix, fw)
    rows = jnp.stack([right] + [shift(right, "row", d) for d in range(1, nr)])

    def rows_of(c):
        return jnp.stack([lax.dynamic_index_in_dim(rows, lax.rem(row - (c * m + t) + nr, nr), 0, keepdims=False) for t in range(m)])

    rights, lefts = [rows_of(col)], [left]
    for d in range(1, nc):
        rights.append(shift(rows_of(lax.rem(col + d, nc)), "col", d))
        lefts.append(shift(left, "col", d))
    rights = jnp.stack(rights)
    lefts = jnp.concatenate(lefts, axis=0)[None]
    rights_other = shift(rights, "sub", 1)
    left_own = lax.dynamic_slice_in_dim(lefts, sub * span, span, 2)
    left_other = shift(lax.dynamic_slice_in_dim(lefts, (1 - sub) * span, span, 2), "sub", 1)
    right_t = prep(rights, rights_other, fw)
    mid, gate, lk, ls, rk, rs = pair(pos, left_own, left_other, 0, right_t, outer_weight, edge_activations, entry, tile_rows)

    rr = shift(rs, "sub", 1)
    lr = shift(ls, "sub", 1)
    slots = [rk, rr]
    up, down = [rk, rr], [rk, rr]
    for t in range(1, nr):
        up = [step_along(x, "row", 1, t) for x in up]
        down = [step_along(x, "row", -1, t) for x in down]
        slots += up + down
    partial = triangle(pos, lk, lr, slots, nr, nc, m, tile_cols)

    own, other = [partial[0]], [shift(partial[1], "sub", 1)]
    for d in range(1, nc):
        own.append(shift(partial[2 * d], "col", d))
        other.append(across(partial[2 * d + 1], d))
    return final(sub_id, own, other, mid, gate, exit_matrix)


def solution(mesh):
    in_specs = (
        P(("grp", "col", "sub"), "row", None),
        P(("grp", "row", "sub"), "col", None),
        P(),
        P(),
        P(),
        P(),
        P(),
    )
    out_specs = P(("grp", "row", "sub"), "col", None)

    return jax.shard_map(per_device, mesh=mesh, in_specs=in_specs, out_specs=out_specs, check_vma=False)
```

```python
import functools

import jax
import jax.numpy as jnp
from jax import lax
from jax.experimental import pallas as pl
from jax.experimental.pallas import tpu as pltpu
from jax.sharding import PartitionSpec as P


EPSILON = 1e-05
LANES = 128
VMEM_LIMIT = 60 * 1024 * 1024


def grant(mib):
    return pltpu.CompilerParams(vmem_limit_bytes=mib * 1024 * 1024)


def standardize_features(values):
    centred = values - jnp.mean(values, axis=-1, keepdims=True)
    spread = jnp.mean(centred * centred, axis=-1, keepdims=True)
    return centred * lax.rsqrt(spread + EPSILON)


def standardize_columns(values):
    centred = values - jnp.mean(values, axis=0, keepdims=True)
    spread = jnp.mean(centred * centred, axis=0, keepdims=True)
    return centred * lax.rsqrt(spread + EPSILON)


def vmem():
    return pl.BlockSpec(memory_space=pltpu.VMEM)


def smem():
    return pl.BlockSpec(memory_space=pltpu.SMEM)


def packing(count, cols):
    spare = -cols % LANES
    if spare and cols < LANES and cols % spare == 0:
        parts = cols // spare
        if count % (parts + 1) == 0:
            return parts, count // (parts + 1) * parts
    return 0, count


def lane_index(shape):
    return lax.broadcasted_iota(jnp.int32, shape, len(shape) - 1)


def weights_kernel(fw, w_ref, n_ref, x_ref, wt_ref, nt_ref, xt_ref, sc, st):
    C = w_ref.shape[1]
    sc[...] = w_ref[...].astype(jnp.float32)
    for b in range(fw):
        st[b * fw : (b + 1) * fw, :] = sc[pl.ds(b, fw, stride=fw), :]
    for t in range(fw * fw // C):
        wt_ref[:, t * C : (t + 1) * C] = st[t * C : (t + 1) * C, :].T.astype(jnp.bfloat16)
    for t in range(n_ref.shape[1] // C):
        nt_ref[t * C : (t + 1) * C, :] = n_ref[:, t * C : (t + 1) * C].astype(jnp.float32).T.astype(jnp.bfloat16)
    xt_ref[...] = x_ref[...].astype(jnp.float32).T.astype(jnp.bfloat16)


def weights(w, n, x, fw):
    K, C = w.shape
    bf = jnp.bfloat16
    return pl.pallas_call(
        functools.partial(weights_kernel, fw),
        out_shape=[jax.ShapeDtypeStruct((C, K), bf), jax.ShapeDtypeStruct(n.shape[::-1], bf), jax.ShapeDtypeStruct(x.shape[::-1], bf)],
        in_specs=[vmem()] * 3,
        out_specs=[vmem()] * 3,
        scratch_shapes=[pltpu.VMEM((K, C), jnp.float32)] * 2,
        compiler_params=grant(4),
    )(w, n, x)


def prep_kernel(fw, own_ref, recv_ref, rt_ref, sc):
    groups, m, seqs, row_lanes = own_ref.shape
    res = row_lanes // fw
    chunk = sc.shape[2]
    pieces = [(ref, g) for ref in (own_ref, recv_ref) for g in range(groups)]
    per = chunk // seqs
    for u in range(len(pieces) // per):
        for mm in range(m):
            for t in range(row_lanes // LANES):
                block = jnp.concatenate(
                    [ref[g, mm, :, t * LANES : (t + 1) * LANES].astype(jnp.float32) for ref, g in pieces[u * per : (u + 1) * per]], axis=0
                )
                start = mm * row_lanes + t * LANES
                sc[u, start : start + LANES, :] = block.T
        for b in range(fw):
            rt_ref[b, :, u * chunk : (u + 1) * chunk] = sc[u, pl.ds(b, m * res, stride=fw), :].astype(jnp.bfloat16)


def prep(own, recv, fw):
    groups, m, seqs, row_lanes = own.shape
    total = 2 * groups * seqs
    chunk = min(total, LANES)
    cols = m * row_lanes // fw
    return pl.pallas_call(
        functools.partial(prep_kernel, fw),
        out_shape=jax.ShapeDtypeStruct((fw, cols, total), jnp.bfloat16),
        in_specs=[vmem(), vmem()],
        out_specs=vmem(),
        scratch_shapes=[pltpu.VMEM((total // chunk, m * row_lanes, chunk), jnp.float32)],
        compiler_params=grant(8),
    )(own, recv)


def pair_kernel(cfg, pos_ref, *refs):
    last = cfg[5]
    if last:
        pl.when((pos_ref[0] == 0) | (pos_ref[0] == last))(lambda: pair_body(cfg, pos_ref, *refs))
    else:
        pair_body(cfg, pos_ref, *refs)


def pair_body(cfg, pos_ref, l_ref, lr_ref, rt_ref, wt_ref, e_ref, went_ref, *rest):
    fw, C, J, S, full, _ = cfg
    if full:
        mid_ref, gate_ref, lk_ref, ls_ref, rk_ref, rs_ref, lt, ot, nts, lsc, rsc = rest
    else:
        rk_ref, rs_ref, lt, ot, nts, rsc = rest
    half = C // 2
    IG = l_ref.shape[1] // fw
    wide = ot.shape[2] // 2
    for t in range(IG * fw // LANES):
        part = slice(t * LANES, (t + 1) * LANES)
        block = jnp.concatenate([l_ref[:, part].astype(jnp.float32), lr_ref[:, part].astype(jnp.float32)], axis=0)
        lt[part, :] = block.T.astype(jnp.bfloat16)
    ltv = lt[...]
    for b in range(fw):
        o = lax.dot_general(ltv, rt_ref[b], (((1,), (1,)), ((), ())), preferred_element_type=jnp.float32).astype(jnp.bfloat16)
        for i in range(IG):
            ot[i // 2, b * fw : (b + 1) * fw, i % 2 * wide : i % 2 * wide + J] = o[i * fw : (i + 1) * fw, :]
    wt = wt_ref[...]
    for h in range(IG // 2):
        pt = lax.dot_general(wt, ot[h], (((1,), (0,)), ((), ())), preferred_element_type=jnp.float32)
        for k in range(2):
            i = 2 * h + k
            et = e_ref[i].astype(jnp.float32).T
            mid = (et + pt[:, k * wide : k * wide + J] * (1.0 / S)).astype(jnp.bfloat16)
            if full:
                mid_ref[i] = mid
            nts[h, :, k * wide : k * wide + J] = standardize_columns(mid.astype(jnp.float32)).astype(jnp.bfloat16)

    def project(first, count, h):
        return lax.dot_general(went_ref[first * C : (first + count) * C, :], nts[h], (((1,), (0,)), ((), ())), preferred_element_type=jnp.float32)

    for h in range(IG // 2):
        if full:
            p = project(0, 2, h)
            x = jax.nn.sigmoid(p[C:]) * p[:C]
            for k in range(2):
                lsc[pl.ds((2 * h + k) * C, C), :J] = x[:, k * wide : k * wide + J]
        p = project(2, 2, h)
        x = jax.nn.sigmoid(p[C:]) * p[:C]
        for k in range(2):
            rsc[pl.ds((2 * h + k) * C, C), :J] = x[:, k * wide : k * wide + J]
        if full:
            x = jax.nn.sigmoid(project(4, 1, h)).astype(jnp.bfloat16)
            for k in range(2):
                gate_ref[2 * h + k] = x[:, k * wide : k * wide + J]
    sub = pos_ref[2]
    parts, main = packing(half, J)
    inside = lane_index((IG, LANES)) < J
    if full:
        for ref, base in ((lk_ref, sub * half), (ls_ref, (1 - sub) * half)):
            for ch in range(half):
                x = lsc[pl.ds(base + ch, IG, stride=C), :]
                ref[ch] = jnp.where(inside, x, 0.0).astype(jnp.bfloat16)
    for ref, base in ((rk_ref, sub * half), (rs_ref, (1 - sub) * half)):
        if parts == 0:
            for ch in range(half):
                x = rsc[pl.ds(base + ch, IG, stride=C), :]
                ref[ch] = jnp.where(inside, x, 0.0).astype(jnp.bfloat16)
        else:
            tails = half - main
            spare = LANES - J
            for q in range(tails):
                tail = rsc[pl.ds(base + main + q, IG, stride=C), :]
                for t in range(parts):
                    x = rsc[pl.ds(base + t * tails + q, IG, stride=C), :]
                    moved = pltpu.roll(tail, J - spare * t, 1)
                    ref[t * tails + q] = jnp.where(inside, x, moved).astype(jnp.bfloat16)


def pair(pos, l, lr, which, rt, wt, e, went, IG, last=0):
    full = not last
    _, part, IA = l.shape
    S = 2 * part
    fw, J, _ = rt.shape
    TI = IA // fw
    C = wt.shape[0]
    half = C // 2
    rows = packing(half, J)[1]
    wide = -(-J // LANES) * LANES
    bf = jnp.bfloat16
    tile = (jax.ShapeDtypeStruct((TI, C, J), bf), pl.BlockSpec((IG, C, J), lambda g: (g, 0, 0)))
    lefts = (jax.ShapeDtypeStruct((half, TI, LANES), bf), pl.BlockSpec((half, IG, LANES), lambda g: (0, g, 0)))
    rights = (jax.ShapeDtypeStruct((rows, TI, LANES), bf), pl.BlockSpec((rows, IG, LANES), lambda g: (0, g, 0)))
    outs = ([tile] * 2 + [lefts] * 2 if full else []) + [rights] * 2
    gated = pltpu.VMEM((IG * C, LANES), jnp.float32)
    f = pl.pallas_call(
        functools.partial(pair_kernel, (fw, C, J, S, full, last)),
        grid=(TI // IG,),
        out_shape=[o[0] for o in outs],
        in_specs=[
            smem(),
            pl.BlockSpec((None, part, IG * fw), lambda g: (which, 0, g)),
            pl.BlockSpec((None, part, IG * fw), lambda g: (which, 0, g)),
            pl.BlockSpec((fw, J, S), lambda g: (0, 0, 0)),
            pl.BlockSpec(wt.shape, lambda g: (0, 0)),
            pl.BlockSpec((IG, J, C), lambda g: (g, 0, 0)),
            pl.BlockSpec(went.shape, lambda g: (0, 0)),
        ],
        out_specs=[o[1] for o in outs],
        scratch_shapes=[
            pltpu.VMEM((IG * fw, S), bf),
            pltpu.VMEM((IG // 2, fw * fw, 2 * wide), bf),
            pltpu.VMEM((IG // 2, C, 2 * wide), bf),
            gated,
        ]
        + ([gated] if full else []),
        compiler_params=grant(28),
        cost_estimate=pl.CostEstimate(flops=2 * TI * J * (S * fw * fw + fw * fw * C + 5 * C * C), bytes_accessed=4 * TI * J * C * 6, transcendentals=TI * J * C * 3),
    )
    return f(pos, l, lr, rt, wt, e, went)


def tri_kernel(cfg, n_slots, pos_ref, lk_ref, lr_ref, *rest):
    nr, nc, m, J = cfg
    slots = rest[:n_slots]
    outs = rest[n_slots : n_slots + 2 * nc]
    rv, lm, sem = rest[n_slots + 2 * nc :]
    half, TI, _ = lk_ref.shape
    row, col, sub = pos_ref[0], pos_ref[1], pos_ref[2]
    parts, main = packing(half, J)
    tails = half - main
    spare = LANES - J

    def copy(index):
        step, u = index // 2, index % 2
        hop = (step + 1) // 2
        origin = row - hop if step % 2 else row + hop
        return origin, pltpu.make_async_copy(slots[index], rv.at[jnp.clip(origin, 0, nr - 1), sub if u == 0 else 1 - sub], sem.at[index])

    for index in range(n_slots):
        origin, c = copy(index)

        @pl.when((origin >= 0) & (origin < nr))
        def _(c=c):
            c.start()

    inside = lane_index((2 * TI, LANES)) < J
    for ch in range(half):
        x = jnp.concatenate([lk_ref[ch], lr_ref[ch]], axis=0)
        if ch < main:
            lm[ch] = x
        else:
            f = x.astype(jnp.float32)
            for t in range(parts):
                moved = pltpu.roll(f, J - spare * t, 1)
                lm[main + (ch - main) * parts + t] = jnp.where(inside, 0.0, moved).astype(jnp.bfloat16)

    for index in range(n_slots):
        origin, c = copy(index)

        @pl.when((origin >= 0) & (origin < nr))
        def _(c=c):
            c.wait()

    def block(ch, start, pieces):
        right = rv[pl.ds(start, m), :, ch].reshape(m * 2 * TI, LANES)
        return lax.dot_general(lm[pieces], right, (((1,), (1,)), ((), ())), preferred_element_type=jnp.float32)

    for dc in range(nc):
        start = lax.rem(col + dc, nc) * m
        own_ref, other_ref = outs[2 * dc], outs[2 * dc + 1]
        for q in range(tails if parts else 0):
            tail = 0.0
            for t in range(parts):
                tail = tail + block(t * tails + q, start, main + q * parts + t)
            tail = jnp.concatenate([tail, jnp.zeros((2 * TI, spare), jnp.float32)], axis=1)
            for t in range(parts):
                x = block(t * tails + q, start, t * tails + q)
                x = jnp.concatenate([x, jnp.zeros((2 * TI, spare), jnp.float32)], axis=1)
                x = jnp.where(inside, x, pltpu.roll(tail, J - spare * t, 1)).astype(jnp.bfloat16)
                own_ref[t * tails + q] = x[:TI]
                other_ref[t * tails + q] = x[TI:]
        if not parts:
            for ch in range(half):
                x = block(ch, start, ch)
                if spare:
                    x = jnp.concatenate([x, jnp.zeros((2 * TI, spare), jnp.float32)], axis=1)
                x = x.astype(jnp.bfloat16)
                own_ref[ch] = x[:TI]
                other_ref[ch] = x[TI:]


def triangle(pos, lk, lr, slots, nr, nc, m, J):
    half, TI, _ = lk.shape
    parts, main = packing(half, J)
    rows = main
    bf = jnp.bfloat16
    n = len(slots)
    return pl.pallas_call(
        functools.partial(tri_kernel, (nr, nc, m, J), n),
        out_shape=[jax.ShapeDtypeStruct((rows, TI, LANES), bf)] * (2 * nc),
        in_specs=[smem(), vmem(), vmem()] + [pl.BlockSpec(memory_space=pl.ANY)] * n,
        out_specs=[vmem()] * (2 * nc),
        scratch_shapes=[
            pltpu.VMEM((nr, 2, rows, TI, LANES), bf),
            pltpu.VMEM((main + (half - main) * max(parts, 1), 2 * TI, LANES), bf),
            pltpu.SemaphoreType.DMA((n,)),
        ],
        compiler_params=pltpu.CompilerParams(vmem_limit_bytes=VMEM_LIMIT),
    )(pos, lk, lr, *slots)


def finish(sc, nts, mid_ref, gate_ref, wx_ref, out_ref):
    TI, C, J = mid_ref.shape
    wide = nts.shape[2] // 2
    wx = wx_ref[...]
    for i in range(TI):
        tri = sc[pl.ds(i, C, stride=TI), :][:, :J]
        nts[i // 2, :, i % 2 * wide : i % 2 * wide + J] = standardize_columns(tri).astype(jnp.bfloat16)
    for h in range(TI // 2):
        update = lax.dot_general(wx, nts[h], (((1,), (0,)), ((), ())), preferred_element_type=jnp.float32)
        for k in range(2):
            i = 2 * h + k
            res = mid_ref[i].astype(jnp.float32) + gate_ref[i].astype(jnp.float32) * update[:, k * wide : k * wide + J]
            out_ref[i] = res.T.astype(jnp.bfloat16)


def final_kernel(cfg, n, sub_ref, *rest):
    C, J = cfg
    own = rest[:n]
    other = rest[n : 2 * n]
    mid_ref, gate_ref, wx_ref, out_ref, sc, nts = rest[2 * n :]
    TI = mid_ref.shape[0]
    half = C // 2
    parts, main = packing(half, J)
    tails = half - main
    spare = LANES - J
    sub = sub_ref[0]
    lanes = lane_index((TI, LANES))
    for refs, base in ((own, sub * half), (other, (1 - sub) * half)):
        def total(ch, refs=refs):
            x = refs[0][ch].astype(jnp.float32)
            for ref in refs[1:]:
                x = x + ref[ch].astype(jnp.float32)
            return x.astype(jnp.bfloat16).astype(jnp.float32)

        for q in range(tails if parts else 0):
            tail = jnp.zeros((TI, LANES), jnp.float32)
            for t in range(parts):
                x = total(t * tails + q)
                sc[pl.ds((base + t * tails + q) * TI, TI), :] = x
                tail = jnp.where((lanes >= spare * t) & (lanes < spare * (t + 1)), pltpu.roll(x, LANES - J + spare * t, 1), tail)
            sc[pl.ds((base + main + q) * TI, TI), :] = tail
        if not parts:
            for ch in range(half):
                sc[pl.ds((base + ch) * TI, TI), :] = total(ch)
    finish(sc, nts, mid_ref, gate_ref, wx_ref, out_ref)


def final(sub, own, other, mid, gate, wx):
    TI, C, J = mid.shape
    n = len(own)
    return pl.pallas_call(
        functools.partial(final_kernel, (C, J), n),
        out_shape=jax.ShapeDtypeStruct((TI, J, C), jnp.bfloat16),
        in_specs=[smem()] + [vmem()] * (2 * n + 3),
        out_specs=vmem(),
        scratch_shapes=[pltpu.VMEM((C * TI, LANES), jnp.float32), pltpu.VMEM((TI // 2, C, 2 * LANES), jnp.bfloat16)],
        compiler_params=pltpu.CompilerParams(vmem_limit_bytes=VMEM_LIMIT),
    )(sub, *own, *other, mid, gate, wx)


def masked_left(lk_ref, lr_ref, lm, J):
    half, TI, _ = lk_ref.shape
    parts, main = packing(half, J)
    spare = LANES - J
    inside = lane_index((2 * TI, LANES)) < J
    for ch in range(main, half):
        f = jnp.concatenate([lk_ref[ch], lr_ref[ch]], axis=0).astype(jnp.float32)
        for t in range(parts):
            moved = pltpu.roll(f, J - spare * t, 1)
            lm[(ch - main) * parts + t] = jnp.where(inside, 0.0, moved).astype(jnp.bfloat16)


def shard_products(lk_ref, lr_ref, lm, right, ways, J, half, TI, store):
    parts, main = packing(half, J)
    tails = half - main

    def dot(left, row):
        return lax.dot_general(left, right(row), (((1,), (1,)), ((), ())), preferred_element_type=jnp.float32)

    def channel(ch):
        if ch < main:
            return dot(jnp.concatenate([lk_ref[ch], lr_ref[ch]], axis=0), ch)
        q = ch - main
        x = dot(lm[q * parts], q)
        for t in range(1, parts):
            x = x + dot(lm[q * parts + t], t * tails + q)
        return x

    count = half // ways
    cols = 4 * TI
    pad = jnp.zeros((2 * TI, LANES - cols), jnp.float32)
    p2, m2 = packing(count, cols)
    t2 = count - m2

    def beside(q):
        return jnp.concatenate([channel(q + w * count) for w in range(ways)] + [pad], axis=1)

    inside = lane_index((2 * TI, LANES)) < cols
    spare = LANES - cols
    for q in range(t2):
        tail = beside(m2 + q)
        for t in range(p2):
            store(t * t2 + q, jnp.where(inside, beside(t * t2 + q), pltpu.roll(tail, cols - spare * t, 1)).astype(jnp.bfloat16))
    for q in range(0 if p2 else count):
        store(q, beside(q).astype(jnp.bfloat16))


def early_kernel(J, n, pos_ref, lk_ref, lr_ref, *rest):
    own, near, mids, far = rest[0:2], rest[2:4], rest[4:6], rest[6:8]
    outs = rest[8:14]
    rv, lm, acc, sem = rest[14:]
    half, TI, _ = lk_ref.shape
    row, col, sub = pos_ref[0], pos_ref[1], pos_ref[2]
    edge = (row == 0) | (row == n - 1)
    plan = [(None, own, 0), (None, near, 1), (edge, far, 2), (jnp.logical_not(edge), mids, 2)]

    def each(action):
        for cond, refs, k in plan:
            for u in range(2):
                c = pltpu.make_async_copy(refs[u], rv.at[k, sub if u == 0 else 1 - sub], sem.at[k, u])
                if cond is None:
                    action(c)
                else:
                    pl.when(cond)(lambda c=c: action(c))

    each(lambda c: c.start())
    masked_left(lk_ref, lr_ref, lm, J)
    each(lambda c: c.wait())
    for k in range(3):

        def store(r, x, k=k):
            acc[k, r] = x

        shard_products(lk_ref, lr_ref, lm, lambda r, k=k: rv[k, :, r].reshape(2 * TI, LANES), 2, J, half, TI, store)
    home = col == row // 2
    send = jnp.where(home, acc[2], acc[0])
    keep = jnp.where(home, acc[0], acc[2])
    for u in range(2):
        outs[u][...] = send[:, u * TI : (u + 1) * TI]
        outs[2 + u][...] = keep[:, u * TI : (u + 1) * TI]
        outs[4 + u][...] = acc[1, :, u * TI : (u + 1) * TI]


def late_kernel(u, J, n, pos_ref, lk_ref, lr_ref, a_ref, b_ref, inner, outward, *rest):
    outs = rest[:4]
    rv, lm, acc, sem = rest[4:]
    half, TI, _ = lk_ref.shape
    row, col = pos_ref[0], pos_ref[1]
    edge = (row == 0) | (row == n - 1)

    def each(action):
        for cond, ref in ((edge, outward), (jnp.logical_not(edge), inner)):
            c = pltpu.make_async_copy(ref, rv, sem.at[0])
            pl.when(cond)(lambda c=c: action(c))

    each(lambda c: c.start())
    masked_left(lk_ref, lr_ref, lm, J)
    each(lambda c: c.wait())

    def store(r, x):
        acc[r] = x

    shard_products(lk_ref, lr_ref, lm, lambda r: rv[r], 4, J, half, TI, store)
    home = col == row // 2
    count = acc.shape[0]
    for k, ref in enumerate((a_ref, b_ref)):
        late = acc[:, k * TI : (k + 1) * TI]
        early = ref[u * count : (u + 1) * count]
        outs[k][...] = jnp.where(home, late, early)
        outs[2 + k][...] = jnp.where(home, early, late)


def products(kernel, right_shape, acc_shape, sems, n_out, pos, lk, lr, extra, slots, J, n):
    half, TI, _ = lk.shape
    parts, main = packing(half, J)
    bf = jnp.bfloat16
    rows = acc_shape[-3]
    return pl.pallas_call(
        functools.partial(kernel, J, n),
        out_shape=[jax.ShapeDtypeStruct((rows, TI, LANES), bf)] * n_out,
        in_specs=[smem(), vmem(), vmem()] + [vmem()] * len(extra) + [pl.BlockSpec(memory_space=pl.ANY)] * len(slots),
        out_specs=[vmem()] * n_out,
        scratch_shapes=[
            pltpu.VMEM(right_shape, bf),
            pltpu.VMEM(((half - main) * max(parts, 1), 2 * TI, LANES), bf),
            pltpu.VMEM(acc_shape, bf),
            pltpu.SemaphoreType.DMA(sems),
        ],
        compiler_params=grant(12 if len(right_shape) > 3 else 6),
        cost_estimate=pl.CostEstimate(flops=half * TI * TI * J * 4, bytes_accessed=main * TI * LANES * 16, transcendentals=0),
    )(pos, lk, lr, *extra, *slots)


def add_group(C, TI, own, other, sub, sc, quads):
    half = C // 2
    pairs = half // 2
    cols = 4 * TI
    spare = LANES - cols
    lanes = lane_index((TI, LANES))

    def total(refs, r):
        x = refs[0][r].astype(jnp.float32) + refs[1][r].astype(jnp.float32)
        return x.astype(jnp.bfloat16).astype(jnp.float32)

    def unpack(count, rows):
        parts, main = packing(count, cols)
        if not parts:
            return [rows(r) for r in range(count)]
        tails = count - main
        out = [rows(r) for r in range(main)]
        for q in range(tails):
            tail = jnp.zeros((TI, LANES), jnp.float32)
            for t in range(parts):
                part = (lanes >= spare * t) & (lanes < spare * (t + 1))
                tail = jnp.where(part, pltpu.roll(out[t * tails + q], LANES - cols + spare * t, 1), tail)
            out.append(tail)
        return out

    for k, (refs, base) in enumerate(((own, sub * pairs), (other, (1 - sub) * pairs))):

        def put(q, x, base=base):
            sc[pl.ds((base + q) * TI, TI), :] = x

        if not quads:
            size = refs[0][0].shape[0]
            for q, x in enumerate(unpack(pairs, lambda r, refs=refs: total(refs[r // size], r % size))):
                put(q, x)
        else:
            swap = sub == (0 if k else 1)
            left = lax.rem(lanes, 2 * TI) < TI
            a, b = (unpack(pairs // 2, lambda r, refs=refs, u=u: total(refs[u], r)) for u in range(2))
            for q in range(pairs // 2):
                x = jnp.where(swap, b[q], a[q])
                y = jnp.where(swap, a[q], b[q])
                put(q, jnp.where(left, x, pltpu.roll(y, TI, 1)))
                put(q + pairs // 2, jnp.where(left, pltpu.roll(x, LANES - TI, 1), y))


def group_updates(C, TI, sc, nts, wx_ref, emit):
    span = 2 * TI
    pairs = C // 4
    low = lane_index((C // 2, LANES)) < span
    for h in range(TI // 2):
        a = sc[pl.ds(2 * h, C // 2, stride=TI), :]
        b = sc[pl.ds(2 * h + 1, C // 2, stride=TI), :]
        x = jnp.where(low, a, pltpu.roll(b, span, 1))
        y = jnp.where(low, pltpu.roll(a, LANES - span, 1), b)
        tri = jnp.concatenate([x[:pairs], y[:pairs], x[pairs:], y[pairs:]], axis=0)
        nts[h // 2, :, h % 2 * LANES : (h % 2 + 1) * LANES] = standardize_columns(tri).astype(jnp.bfloat16)
    wx = wx_ref[...]
    for g in range(TI // 4):
        update = lax.dot_general(wx, nts[g], (((1,), (0,)), ((), ())), preferred_element_type=jnp.float32)
        for k in range(2):
            x = update[:, k * LANES : (k + 1) * LANES].T
            emit(4 * g + 2 * k, x[:span])
            emit(4 * g + 2 * k + 1, x[span : 2 * span])


def lower_half_first(pos_ref):
    home = pos_ref[1] == pos_ref[0] // 2
    odd = lax.rem(pos_ref[0], 2) == 1
    return jnp.where(home, jnp.logical_not(odd), odd)


def finish_early_kernel(pos_ref, a_ref, b_ref, c_ref, d_ref, mid_ref, gate_ref, wx_ref, out_ref, m_ref, g_ref, sc, nts):
    TI, C, _ = mid_ref.shape
    span = 2 * TI
    first = lower_half_first(pos_ref)
    add_group(C, TI, [(a_ref, b_ref)], [(c_ref, d_ref)], pos_ref[2], sc, False)

    def emit(i, update):
        mid = mid_ref[i].astype(jnp.float32).T
        gate = gate_ref[i].astype(jnp.float32).T
        m1, m2 = mid[:span], mid[span:]
        g1, g2 = gate[:span], gate[span:]
        out_ref[i] = (jnp.where(first, m1, m2) + jnp.where(first, g1, g2) * update).astype(jnp.bfloat16)
        m_ref[i] = jnp.where(first, m2, m1).astype(jnp.bfloat16)
        g_ref[i] = jnp.where(first, g2, g1).astype(jnp.bfloat16)

    group_updates(C, TI, sc, nts, wx_ref, emit)


def finish_late_kernel(pos_ref, *refs):
    pieces, (early_ref, m_ref, g_ref, wx_ref, out_ref, sc, nts) = refs[:8], refs[8:]
    TI, span, C = early_ref.shape
    first = lower_half_first(pos_ref)
    home = pos_ref[1] == pos_ref[0] // 2
    args = (C, TI, [pieces[0:2], pieces[2:4]], [pieces[4:6], pieces[6:8]], pos_ref[2], sc)
    pl.when(home)(lambda: add_group(*args, False))
    pl.when(jnp.logical_not(home))(lambda: add_group(*args, True))

    def emit(i, update):
        late = m_ref[i].astype(jnp.float32) + g_ref[i].astype(jnp.float32) * update
        early = early_ref[i].astype(jnp.float32)
        out_ref[i, :span] = jnp.where(first, early, late).astype(jnp.bfloat16)
        out_ref[i, span:] = jnp.where(first, late, early).astype(jnp.bfloat16)

    group_updates(C, TI, sc, nts, wx_ref, emit)


def finish_group(kernel, shapes, C, TI, *args):
    return pl.pallas_call(
        kernel,
        out_shape=[jax.ShapeDtypeStruct(x, jnp.bfloat16) for x in shapes],
        in_specs=[smem()] + [vmem()] * (len(args) - 1),
        out_specs=[vmem()] * len(shapes),
        scratch_shapes=[pltpu.VMEM((C // 2 * TI, LANES), jnp.float32), pltpu.VMEM((TI // 4, C, 2 * LANES), jnp.bfloat16)],
        compiler_params=grant(8),
        cost_estimate=pl.CostEstimate(flops=2 * C * C * TI * 2 * TI, bytes_accessed=TI * TI * C * 20, transcendentals=0),
    )(*args)


def shift(x, axis, d):
    n = lax.axis_size(axis)
    return lax.ppermute(x, axis, [(i, (i + d) % n) for i in range(n)])


def step_along(x, axis, d, t):
    n = lax.axis_size(axis)
    return lax.ppermute(x, axis, [(i, i + d) for i in range(n) if 0 <= i + d < n and 0 <= i - d * (t - 1) < n])


def across(x, d):
    nc = lax.axis_size("col")
    return lax.ppermute(x, ("col", "sub"), [(c * 2 + s, (c + d) % nc * 2 + 1 - s) for c in range(nc) for s in range(2)])


def per_device(
    homolog_activations,
    edge_activations,
    first_projection_matrix,
    second_projection_matrix,
    tensor_product_matrix,
    multiplicative_entry_matrix,
    multiplicative_exit_matrix,
):
    seqs, residues, features = homolog_activations.shape
    tile_rows, tile_cols, width = edge_activations.shape
    fw = first_projection_matrix.shape[1]
    nr, nc, ns = (lax.axis_size(a) for a in ("row", "col", "sub"))
    assert ns == 2
    row, col, sub = (lax.axis_index(a) for a in ("row", "col", "sub"))
    pos = jnp.stack([row, col, sub]).astype(jnp.int32)
    sub_id = pos[2:]
    m = tile_cols // residues

    normed = standardize_features(homolog_activations.astype(jnp.float32)).astype(jnp.bfloat16).reshape(seqs * residues, features)

    def project(matrix):
        return jnp.dot(normed, matrix, preferred_element_type=jnp.float32).astype(jnp.bfloat16).reshape(seqs, residues * fw)

    right = project(second_projection_matrix)
    left = project(first_projection_matrix)

    span = tile_rows * fw
    fast = nr == 4 and nc == 2
    if fast:
        hops = [lax.ppermute(x, "row", [(i, i ^ d) for i in range(nr)]) for d, x in ((3, jnp.stack([right, left])), (2, right), (1, right))]
        left_x = shift(left, "col", 1)
        outer_weight, entry, exit_matrix = weights(tensor_product_matrix, multiplicative_entry_matrix, multiplicative_exit_matrix, fw)
        rows = jnp.stack([right, hops[2], hops[1], hops[0][0]])

        def rows_of(c):
            return [lax.dynamic_index_in_dim(rows, row ^ (c * m + t), 0, keepdims=False) for t in range(m)]

        got = shift(jnp.stack(rows_of(1 - col) + [hops[0][1]]), "col", 1)
        rights = jnp.stack([jnp.stack(rows_of(col)), got[:m]])
        lefts = jnp.stack([jnp.concatenate([left, left_x], axis=0), jnp.concatenate([hops[0][1], got[m]], axis=0)])
        far_edges = lax.ppermute(edge_activations, "row", [(0, nr - 1), (nr - 1, 0)])
        rights_other = shift(rights, "sub", 1)
        left_own = lax.dynamic_slice_in_dim(lefts, sub * span, span, 2)
        left_other = shift(lax.dynamic_slice_in_dim(lefts, (1 - sub) * span, span, 2), "sub", 1)
        right_t = prep(rights, rights_other, fw)
        mid, gate, lk, ls, rk, rs = pair(pos, left_own, left_other, 0, right_t, outer_weight, edge_activations, entry, tile_rows)
        outer = [(i, i ^ 1) for i in range(nr)]
        inner = [(1, 2), (2, 1)]
        outward = [(1, 0), (2, 3)]

        def along(x, pairs):
            return lax.ppermute(x, "row", pairs)

        near, mids = [along(rk, outer)], [along(rk, inner)]
        rr = shift(rs, "sub", 1)
        near, mids = near + [along(rr, outer)], mids + [along(rr, inner)]
        lr = shift(ls, "sub", 1)
        far_k, far_s = pair(pos, left_own, left_other, 1, right_t, outer_weight, far_edges, entry, tile_rows, nr - 1)
        last_in, last_out = [along(near[0], inner)], [along(mids[0], outward)]
        last_in, last_out = last_in + [along(near[1], inner)], last_out + [along(mids[1], outward)]
        far = [far_k, shift(far_s, "sub", 1)]
        rows, pairs = rk.shape[0], packing(width // 4, 4 * tile_rows)[1]
        shards = (3, 2, rows, tile_rows, LANES)
        acc = (3, pairs, 2 * tile_rows, LANES)
        send1, send1o, keep1, keep1o, rest, resto = products(early_kernel, shards, acc, (3, 2), 6, pos, lk, lr, [], [rk, rr, *near, *mids, *far], tile_cols, nr)
        got1, got1o, keep1o = shift(send1, "col", 1), across(send1o, 1), shift(keep1o, "sub", 1)
        group = (tile_rows, 2 * tile_rows, width)
        done1, mid2, gate2 = finish_group(finish_early_kernel, [group] * 3, width, tile_rows, pos, keep1, got1, keep1o, got1o, mid, gate, exit_matrix)
        own, other = [], []
        acc = (pairs // 2, 2 * tile_rows, LANES)
        for u in range(2):
            kernel = functools.partial(late_kernel, u)
            send, sendo, keep, keepo = products(kernel, rk.shape, acc, (1,), 4, pos, lk, lr, [rest, resto], [last_in[u], last_out[u]], tile_cols, nr)
            own += [keep, shift(send, "col", 1)]
            other += [shift(keepo, "sub", 1), across(sendo, 1)]
        return finish_group(finish_late_kernel, [edge_activations.shape], width, tile_rows, pos, *own, *other, done1, mid2, gate2, exit_matrix)[0]

    outer_weight, entry, exit_matrix = weights(tensor_product_matrix, multiplicative_entry_matrix, multiplicative_exit_matrix, fw)
    rows = jnp.stack([right] + [shift(right, "row", d) for d in range(1, nr)])

    def rows_of(c):
        return jnp.stack([lax.dynamic_index_in_dim(rows, lax.rem(row - (c * m + t) + nr, nr), 0, keepdims=False) for t in range(m)])

    rights, lefts = [rows_of(col)], [left]
    for d in range(1, nc):
        rights.append(shift(rows_of(lax.rem(col + d, nc)), "col", d))
        lefts.append(shift(left, "col", d))
    rights = jnp.stack(rights)
    lefts = jnp.concatenate(lefts, axis=0)[None]
    rights_other = shift(rights, "sub", 1)
    left_own = lax.dynamic_slice_in_dim(lefts, sub * span, span, 2)
    left_other = shift(lax.dynamic_slice_in_dim(lefts, (1 - sub) * span, span, 2), "sub", 1)
    right_t = prep(rights, rights_other, fw)
    mid, gate, lk, ls, rk, rs = pair(pos, left_own, left_other, 0, right_t, outer_weight, edge_activations, entry, tile_rows)

    rr = shift(rs, "sub", 1)
    lr = shift(ls, "sub", 1)
    slots = [rk, rr]
    up, down = [rk, rr], [rk, rr]
    for t in range(1, nr):
        up = [step_along(x, "row", 1, t) for x in up]
        down = [step_along(x, "row", -1, t) for x in down]
        slots += up + down
    partial = triangle(pos, lk, lr, slots, nr, nc, m, tile_cols)

    own, other = [partial[0]], [shift(partial[1], "sub", 1)]
    for d in range(1, nc):
        own.append(shift(partial[2 * d], "col", d))
        other.append(across(partial[2 * d + 1], d))
    return final(sub_id, own, other, mid, gate, exit_matrix)


def solution(mesh):
    in_specs = (
        P(("grp", "col", "sub"), "row", None),
        P(("grp", "row", "sub"), "col", None),
        P(),
        P(),
        P(),
        P(),
        P(),
    )
    out_specs = P(("grp", "row", "sub"), "col", None)

    return jax.shard_map(per_device, mesh=mesh, in_specs=in_specs, out_specs=out_specs, check_vma=False)
```

```python
import functools

import jax
import jax.numpy as jnp
from jax import lax
from jax.experimental import pallas as pl
from jax.experimental.pallas import tpu as pltpu
from jax.sharding import PartitionSpec as P


EPSILON = 1e-05
LANES = 128
VMEM_LIMIT = 60 * 1024 * 1024


def grant(mib):
    return pltpu.CompilerParams(vmem_limit_bytes=mib * 1024 * 1024)


def standardize_features(values):
    centred = values - jnp.mean(values, axis=-1, keepdims=True)
    spread = jnp.mean(centred * centred, axis=-1, keepdims=True)
    return centred * lax.rsqrt(spread + EPSILON)


def standardize_columns(values):
    centred = values - jnp.mean(values, axis=0, keepdims=True)
    spread = jnp.mean(centred * centred, axis=0, keepdims=True)
    return centred * lax.rsqrt(spread + EPSILON)


def vmem():
    return pl.BlockSpec(memory_space=pltpu.VMEM)


def smem():
    return pl.BlockSpec(memory_space=pltpu.SMEM)


def packing(count, cols):
    spare = -cols % LANES
    if spare and cols < LANES and cols % spare == 0:
        parts = cols // spare
        if count % (parts + 1) == 0:
            return parts, count // (parts + 1) * parts
    return 0, count


def lane_index(shape):
    return lax.broadcasted_iota(jnp.int32, shape, len(shape) - 1)


def factors_kernel(x_ref, first_ref, second_ref, left_ref, right_ref):
    rows = x_ref.shape[0]
    step = rows // 8 if rows % 128 == 0 else rows
    for t in range(rows // step):
        part = slice(t * step, (t + 1) * step)
        normed = standardize_features(x_ref[part, :].astype(jnp.float32)).astype(jnp.bfloat16)
        right_ref[part, :] = jnp.dot(normed, second_ref[...], preferred_element_type=jnp.float32).astype(jnp.bfloat16)
        left_ref[part, :] = jnp.dot(normed, first_ref[...], preferred_element_type=jnp.float32).astype(jnp.bfloat16)


def factors(x, first, second):
    shape = jax.ShapeDtypeStruct((x.shape[0], first.shape[1]), jnp.bfloat16)
    return pl.pallas_call(
        factors_kernel,
        out_shape=[shape, shape],
        in_specs=[vmem()] * 3,
        out_specs=[vmem()] * 2,
        compiler_params=grant(6),
    )(x, first, second)


def weights_kernel(fw, w_ref, n_ref, x_ref, wt_ref, nt_ref, xt_ref, sc, st):
    C = w_ref.shape[1]
    sc[...] = w_ref[...].astype(jnp.float32)
    for b in range(fw):
        st[b * fw : (b + 1) * fw, :] = sc[pl.ds(b, fw, stride=fw), :]
    for t in range(fw * fw // C):
        wt_ref[:, t * C : (t + 1) * C] = st[t * C : (t + 1) * C, :].T.astype(jnp.bfloat16)
    for t in range(n_ref.shape[1] // C):
        nt_ref[t * C : (t + 1) * C, :] = n_ref[:, t * C : (t + 1) * C].astype(jnp.float32).T.astype(jnp.bfloat16)
    xt_ref[...] = x_ref[...].astype(jnp.float32).T.astype(jnp.bfloat16)


def weights(w, n, x, fw):
    K, C = w.shape
    bf = jnp.bfloat16
    return pl.pallas_call(
        functools.partial(weights_kernel, fw),
        out_shape=[jax.ShapeDtypeStruct((C, K), bf), jax.ShapeDtypeStruct(n.shape[::-1], bf), jax.ShapeDtypeStruct(x.shape[::-1], bf)],
        in_specs=[vmem()] * 3,
        out_specs=[vmem()] * 3,
        scratch_shapes=[pltpu.VMEM((K, C), jnp.float32)] * 2,
        compiler_params=grant(4),
    )(w, n, x)


def prep_kernel(fw, own_ref, recv_ref, rt_ref, sc):
    groups, m, seqs, row_lanes = own_ref.shape
    res = row_lanes // fw
    chunk = sc.shape[2]
    pieces = [(ref, g) for ref in (own_ref, recv_ref) for g in range(groups)]
    per = chunk // seqs
    for u in range(len(pieces) // per):
        for mm in range(m):
            for t in range(row_lanes // LANES):
                block = jnp.concatenate(
                    [ref[g, mm, :, t * LANES : (t + 1) * LANES].astype(jnp.float32) for ref, g in pieces[u * per : (u + 1) * per]], axis=0
                )
                start = mm * row_lanes + t * LANES
                sc[u, start : start + LANES, :] = block.T
        for b in range(fw):
            rt_ref[b, :, u * chunk : (u + 1) * chunk] = sc[u, pl.ds(b, m * res, stride=fw), :].astype(jnp.bfloat16)


def prep(own, recv, fw):
    groups, m, seqs, row_lanes = own.shape
    total = 2 * groups * seqs
    chunk = min(total, LANES)
    cols = m * row_lanes // fw
    return pl.pallas_call(
        functools.partial(prep_kernel, fw),
        out_shape=jax.ShapeDtypeStruct((fw, cols, total), jnp.bfloat16),
        in_specs=[vmem(), vmem()],
        out_specs=vmem(),
        scratch_shapes=[pltpu.VMEM((total // chunk, m * row_lanes, chunk), jnp.float32)],
        compiler_params=grant(8),
    )(own, recv)


def pair_kernel(cfg, pos_ref, *refs):
    last = cfg[5]
    if last:
        pl.when((pos_ref[0] == 0) | (pos_ref[0] == last))(lambda: pair_body(cfg, pos_ref, *refs))
    else:
        pair_body(cfg, pos_ref, *refs)


def pair_body(cfg, pos_ref, l_ref, lr_ref, rt_ref, wt_ref, e_ref, went_ref, *rest):
    fw, C, J, S, full, _ = cfg
    if full:
        mid_ref, gate_ref, lk_ref, ls_ref, rk_ref, rs_ref, lt, ot, nts, lsc, rsc = rest
    else:
        rk_ref, rs_ref, lt, ot, nts, rsc = rest
    half = C // 2
    IG = l_ref.shape[1] // fw
    wide = ot.shape[2] // 2
    for t in range(IG * fw // LANES):
        part = slice(t * LANES, (t + 1) * LANES)
        block = jnp.concatenate([l_ref[:, part].astype(jnp.float32), lr_ref[:, part].astype(jnp.float32)], axis=0)
        lt[part, :] = block.T.astype(jnp.bfloat16)
    ltv = lt[...]
    for b in range(fw):
        o = lax.dot_general(ltv, rt_ref[b], (((1,), (1,)), ((), ())), preferred_element_type=jnp.float32).astype(jnp.bfloat16)
        for i in range(IG):
            ot[i // 2, b * fw : (b + 1) * fw, i % 2 * wide : i % 2 * wide + J] = o[i * fw : (i + 1) * fw, :]
    wt = wt_ref[...]
    for h in range(IG // 2):
        pt = lax.dot_general(wt, ot[h], (((1,), (0,)), ((), ())), preferred_element_type=jnp.float32)
        for k in range(2):
            i = 2 * h + k
            et = e_ref[i].astype(jnp.float32).T
            mid = (et + pt[:, k * wide : k * wide + J] * (1.0 / S)).astype(jnp.bfloat16)
            if full:
                mid_ref[i] = mid
            nts[h, :, k * wide : k * wide + J] = standardize_columns(mid.astype(jnp.float32)).astype(jnp.bfloat16)

    def project(first, count, h):
        return lax.dot_general(went_ref[first * C : (first + count) * C, :], nts[h], (((1,), (0,)), ((), ())), preferred_element_type=jnp.float32)

    for h in range(IG // 2):
        if full:
            p = project(0, 2, h)
            x = jax.nn.sigmoid(p[C:]) * p[:C]
            for k in range(2):
                lsc[pl.ds((2 * h + k) * C, C), :J] = x[:, k * wide : k * wide + J]
        p = project(2, 2, h)
        x = jax.nn.sigmoid(p[C:]) * p[:C]
        for k in range(2):
            rsc[pl.ds((2 * h + k) * C, C), :J] = x[:, k * wide : k * wide + J]
        if full:
            x = jax.nn.sigmoid(project(4, 1, h)).astype(jnp.bfloat16)
            for k in range(2):
                gate_ref[2 * h + k] = x[:, k * wide : k * wide + J]
    sub = pos_ref[2]
    parts, main = packing(half, J)
    inside = lane_index((IG, LANES)) < J
    if full:
        for ref, base in ((lk_ref, sub * half), (ls_ref, (1 - sub) * half)):
            for ch in range(half):
                x = lsc[pl.ds(base + ch, IG, stride=C), :]
                ref[ch] = jnp.where(inside, x, 0.0).astype(jnp.bfloat16)
    for ref, base in ((rk_ref, sub * half), (rs_ref, (1 - sub) * half)):
        if parts == 0:
            for ch in range(half):
                x = rsc[pl.ds(base + ch, IG, stride=C), :]
                ref[ch] = jnp.where(inside, x, 0.0).astype(jnp.bfloat16)
        else:
            tails = half - main
            spare = LANES - J
            for q in range(tails):
                tail = rsc[pl.ds(base + main + q, IG, stride=C), :]
                for t in range(parts):
                    x = rsc[pl.ds(base + t * tails + q, IG, stride=C), :]
                    moved = pltpu.roll(tail, J - spare * t, 1)
                    ref[t * tails + q] = jnp.where(inside, x, moved).astype(jnp.bfloat16)


def pair(pos, l, lr, which, rt, wt, e, went, IG, last=0):
    full = not last
    _, part, IA = l.shape
    S = 2 * part
    fw, J, _ = rt.shape
    TI = IA // fw
    C = wt.shape[0]
    half = C // 2
    rows = packing(half, J)[1]
    wide = -(-J // LANES) * LANES
    bf = jnp.bfloat16
    tile = (jax.ShapeDtypeStruct((TI, C, J), bf), pl.BlockSpec((IG, C, J), lambda g: (g, 0, 0)))
    lefts = (jax.ShapeDtypeStruct((half, TI, LANES), bf), pl.BlockSpec((half, IG, LANES), lambda g: (0, g, 0)))
    rights = (jax.ShapeDtypeStruct((rows, TI, LANES), bf), pl.BlockSpec((rows, IG, LANES), lambda g: (0, g, 0)))
    outs = ([tile] * 2 + [lefts] * 2 if full else []) + [rights] * 2
    gated = pltpu.VMEM((IG * C, LANES), jnp.float32)
    f = pl.pallas_call(
        functools.partial(pair_kernel, (fw, C, J, S, full, last)),
        grid=(TI // IG,),
        out_shape=[o[0] for o in outs],
        in_specs=[
            smem(),
            pl.BlockSpec((None, part, IG * fw), lambda g: (which, 0, g)),
            pl.BlockSpec((None, part, IG * fw), lambda g: (which, 0, g)),
            pl.BlockSpec((fw, J, S), lambda g: (0, 0, 0)),
            pl.BlockSpec(wt.shape, lambda g: (0, 0)),
            pl.BlockSpec((IG, J, C), lambda g: (g, 0, 0)),
            pl.BlockSpec(went.shape, lambda g: (0, 0)),
        ],
        out_specs=[o[1] for o in outs],
        scratch_shapes=[
            pltpu.VMEM((IG * fw, S), bf),
            pltpu.VMEM((IG // 2, fw * fw, 2 * wide), bf),
            pltpu.VMEM((IG // 2, C, 2 * wide), bf),
            gated,
        ]
        + ([gated] if full else []),
        compiler_params=grant(28),
        cost_estimate=pl.CostEstimate(flops=2 * TI * J * (S * fw * fw + fw * fw * C + 5 * C * C), bytes_accessed=4 * TI * J * C * 6, transcendentals=TI * J * C * 3),
    )
    return f(pos, l, lr, rt, wt, e, went)


def tri_kernel(cfg, n_slots, pos_ref, lk_ref, lr_ref, *rest):
    nr, nc, m, J = cfg
    slots = rest[:n_slots]
    outs = rest[n_slots : n_slots + 2 * nc]
    rv, lm, sem = rest[n_slots + 2 * nc :]
    half, TI, _ = lk_ref.shape
    row, col, sub = pos_ref[0], pos_ref[1], pos_ref[2]
    parts, main = packing(half, J)
    tails = half - main
    spare = LANES - J

    def copy(index):
        step, u = index // 2, index % 2
        hop = (step + 1) // 2
        origin = row - hop if step % 2 else row + hop
        return origin, pltpu.make_async_copy(slots[index], rv.at[jnp.clip(origin, 0, nr - 1), sub if u == 0 else 1 - sub], sem.at[index])

    for index in range(n_slots):
        origin, c = copy(index)

        @pl.when((origin >= 0) & (origin < nr))
        def _(c=c):
            c.start()

    inside = lane_index((2 * TI, LANES)) < J
    for ch in range(half):
        x = jnp.concatenate([lk_ref[ch], lr_ref[ch]], axis=0)
        if ch < main:
            lm[ch] = x
        else:
            f = x.astype(jnp.float32)
            for t in range(parts):
                moved = pltpu.roll(f, J - spare * t, 1)
                lm[main + (ch - main) * parts + t] = jnp.where(inside, 0.0, moved).astype(jnp.bfloat16)

    for index in range(n_slots):
        origin, c = copy(index)

        @pl.when((origin >= 0) & (origin < nr))
        def _(c=c):
            c.wait()

    def block(ch, start, pieces):
        right = rv[pl.ds(start, m), :, ch].reshape(m * 2 * TI, LANES)
        return lax.dot_general(lm[pieces], right, (((1,), (1,)), ((), ())), preferred_element_type=jnp.float32)

    for dc in range(nc):
        start = lax.rem(col + dc, nc) * m
        own_ref, other_ref = outs[2 * dc], outs[2 * dc + 1]
        for q in range(tails if parts else 0):
            tail = 0.0
            for t in range(parts):
                tail = tail + block(t * tails + q, start, main + q * parts + t)
            tail = jnp.concatenate([tail, jnp.zeros((2 * TI, spare), jnp.float32)], axis=1)
            for t in range(parts):
                x = block(t * tails + q, start, t * tails + q)
                x = jnp.concatenate([x, jnp.zeros((2 * TI, spare), jnp.float32)], axis=1)
                x = jnp.where(inside, x, pltpu.roll(tail, J - spare * t, 1)).astype(jnp.bfloat16)
                own_ref[t * tails + q] = x[:TI]
                other_ref[t * tails + q] = x[TI:]
        if not parts:
            for ch in range(half):
                x = block(ch, start, ch)
                if spare:
                    x = jnp.concatenate([x, jnp.zeros((2 * TI, spare), jnp.float32)], axis=1)
                x = x.astype(jnp.bfloat16)
                own_ref[ch] = x[:TI]
                other_ref[ch] = x[TI:]


def triangle(pos, lk, lr, slots, nr, nc, m, J):
    half, TI, _ = lk.shape
    parts, main = packing(half, J)
    rows = main
    bf = jnp.bfloat16
    n = len(slots)
    return pl.pallas_call(
        functools.partial(tri_kernel, (nr, nc, m, J), n),
        out_shape=[jax.ShapeDtypeStruct((rows, TI, LANES), bf)] * (2 * nc),
        in_specs=[smem(), vmem(), vmem()] + [pl.BlockSpec(memory_space=pl.ANY)] * n,
        out_specs=[vmem()] * (2 * nc),
        scratch_shapes=[
            pltpu.VMEM((nr, 2, rows, TI, LANES), bf),
            pltpu.VMEM((main + (half - main) * max(parts, 1), 2 * TI, LANES), bf),
            pltpu.SemaphoreType.DMA((n,)),
        ],
        compiler_params=pltpu.CompilerParams(vmem_limit_bytes=VMEM_LIMIT),
    )(pos, lk, lr, *slots)


def finish(sc, nts, mid_ref, gate_ref, wx_ref, out_ref):
    TI, C, J = mid_ref.shape
    wide = nts.shape[2] // 2
    wx = wx_ref[...]
    for i in range(TI):
        tri = sc[pl.ds(i, C, stride=TI), :][:, :J]
        nts[i // 2, :, i % 2 * wide : i % 2 * wide + J] = standardize_columns(tri).astype(jnp.bfloat16)
    for h in range(TI // 2):
        update = lax.dot_general(wx, nts[h], (((1,), (0,)), ((), ())), preferred_element_type=jnp.float32)
        for k in range(2):
            i = 2 * h + k
            res = mid_ref[i].astype(jnp.float32) + gate_ref[i].astype(jnp.float32) * update[:, k * wide : k * wide + J]
            out_ref[i] = res.T.astype(jnp.bfloat16)


def final_kernel(cfg, n, sub_ref, *rest):
    C, J = cfg
    own = rest[:n]
    other = rest[n : 2 * n]
    mid_ref, gate_ref, wx_ref, out_ref, sc, nts = rest[2 * n :]
    TI = mid_ref.shape[0]
    half = C // 2
    parts, main = packing(half, J)
    tails = half - main
    spare = LANES - J
    sub = sub_ref[0]
    lanes = lane_index((TI, LANES))
    for refs, base in ((own, sub * half), (other, (1 - sub) * half)):
        def total(ch, refs=refs):
            x = refs[0][ch].astype(jnp.float32)
            for ref in refs[1:]:
                x = x + ref[ch].astype(jnp.float32)
            return x.astype(jnp.bfloat16).astype(jnp.float32)

        for q in range(tails if parts else 0):
            tail = jnp.zeros((TI, LANES), jnp.float32)
            for t in range(parts):
                x = total(t * tails + q)
                sc[pl.ds((base + t * tails + q) * TI, TI), :] = x
                tail = jnp.where((lanes >= spare * t) & (lanes < spare * (t + 1)), pltpu.roll(x, LANES - J + spare * t, 1), tail)
            sc[pl.ds((base + main + q) * TI, TI), :] = tail
        if not parts:
            for ch in range(half):
                sc[pl.ds((base + ch) * TI, TI), :] = total(ch)
    finish(sc, nts, mid_ref, gate_ref, wx_ref, out_ref)


def final(sub, own, other, mid, gate, wx):
    TI, C, J = mid.shape
    n = len(own)
    return pl.pallas_call(
        functools.partial(final_kernel, (C, J), n),
        out_shape=jax.ShapeDtypeStruct((TI, J, C), jnp.bfloat16),
        in_specs=[smem()] + [vmem()] * (2 * n + 3),
        out_specs=vmem(),
        scratch_shapes=[pltpu.VMEM((C * TI, LANES), jnp.float32), pltpu.VMEM((TI // 2, C, 2 * LANES), jnp.bfloat16)],
        compiler_params=pltpu.CompilerParams(vmem_limit_bytes=VMEM_LIMIT),
    )(sub, *own, *other, mid, gate, wx)


def masked_left(lk_ref, lr_ref, lm, J):
    half, TI, _ = lk_ref.shape
    parts, main = packing(half, J)
    spare = LANES - J
    inside = lane_index((2 * TI, LANES)) < J
    for ch in range(main, half):
        f = jnp.concatenate([lk_ref[ch], lr_ref[ch]], axis=0).astype(jnp.float32)
        for t in range(parts):
            moved = pltpu.roll(f, J - spare * t, 1)
            lm[(ch - main) * parts + t] = jnp.where(inside, 0.0, moved).astype(jnp.bfloat16)


def shard_products(lk_ref, lr_ref, lm, right, ways, J, half, TI, store):
    parts, main = packing(half, J)
    tails = half - main

    def dot(left, row):
        return lax.dot_general(left, right(row), (((1,), (1,)), ((), ())), preferred_element_type=jnp.float32)

    def channel(ch):
        if ch < main:
            return dot(jnp.concatenate([lk_ref[ch], lr_ref[ch]], axis=0), ch)
        q = ch - main
        x = dot(lm[q * parts], q)
        for t in range(1, parts):
            x = x + dot(lm[q * parts + t], t * tails + q)
        return x

    count = half // ways
    cols = 4 * TI
    pad = jnp.zeros((2 * TI, LANES - cols), jnp.float32)
    p2, m2 = packing(count, cols)
    t2 = count - m2

    def beside(q):
        return jnp.concatenate([channel(q + w * count) for w in range(ways)] + [pad], axis=1)

    inside = lane_index((2 * TI, LANES)) < cols
    spare = LANES - cols
    for q in range(t2):
        tail = beside(m2 + q)
        for t in range(p2):
            store(t * t2 + q, jnp.where(inside, beside(t * t2 + q), pltpu.roll(tail, cols - spare * t, 1)).astype(jnp.bfloat16))
    for q in range(0 if p2 else count):
        store(q, beside(q).astype(jnp.bfloat16))


def early_kernel(J, n, pos_ref, lk_ref, lr_ref, *rest):
    own, near, mids, far = rest[0:2], rest[2:4], rest[4:6], rest[6:8]
    outs = rest[8:14]
    rv, lm, acc, sem = rest[14:]
    half, TI, _ = lk_ref.shape
    row, col, sub = pos_ref[0], pos_ref[1], pos_ref[2]
    edge = (row == 0) | (row == n - 1)
    plan = [(None, own, 0), (None, near, 1), (edge, far, 2), (jnp.logical_not(edge), mids, 2)]

    def each(action):
        for cond, refs, k in plan:
            for u in range(2):
                c = pltpu.make_async_copy(refs[u], rv.at[k, sub if u == 0 else 1 - sub], sem.at[k, u])
                if cond is None:
                    action(c)
                else:
                    pl.when(cond)(lambda c=c: action(c))

    each(lambda c: c.start())
    masked_left(lk_ref, lr_ref, lm, J)
    each(lambda c: c.wait())
    for k in range(3):

        def store(r, x, k=k):
            acc[k, r] = x

        shard_products(lk_ref, lr_ref, lm, lambda r, k=k: rv[k, :, r].reshape(2 * TI, LANES), 2, J, half, TI, store)
    home = col == row // 2
    send = jnp.where(home, acc[2], acc[0])
    keep = jnp.where(home, acc[0], acc[2])
    for u in range(2):
        outs[u][...] = send[:, u * TI : (u + 1) * TI]
        outs[2 + u][...] = keep[:, u * TI : (u + 1) * TI]
        outs[4 + u][...] = acc[1, :, u * TI : (u + 1) * TI]


def late_kernel(u, J, n, pos_ref, lk_ref, lr_ref, a_ref, b_ref, inner, outward, *rest):
    outs = rest[:4]
    rv, lm, acc, sem = rest[4:]
    half, TI, _ = lk_ref.shape
    row, col = pos_ref[0], pos_ref[1]
    edge = (row == 0) | (row == n - 1)

    def each(action):
        for cond, ref in ((edge, outward), (jnp.logical_not(edge), inner)):
            c = pltpu.make_async_copy(ref, rv, sem.at[0])
            pl.when(cond)(lambda c=c: action(c))

    each(lambda c: c.start())
    masked_left(lk_ref, lr_ref, lm, J)
    each(lambda c: c.wait())

    def store(r, x):
        acc[r] = x

    shard_products(lk_ref, lr_ref, lm, lambda r: rv[r], 4, J, half, TI, store)
    home = col == row // 2
    count = acc.shape[0]
    for k, ref in enumerate((a_ref, b_ref)):
        late = acc[:, k * TI : (k + 1) * TI]
        early = ref[u * count : (u + 1) * count]
        outs[k][...] = jnp.where(home, late, early)
        outs[2 + k][...] = jnp.where(home, early, late)


def products(kernel, right_shape, acc_shape, sems, n_out, pos, lk, lr, extra, slots, J, n):
    half, TI, _ = lk.shape
    parts, main = packing(half, J)
    bf = jnp.bfloat16
    rows = acc_shape[-3]
    return pl.pallas_call(
        functools.partial(kernel, J, n),
        out_shape=[jax.ShapeDtypeStruct((rows, TI, LANES), bf)] * n_out,
        in_specs=[smem(), vmem(), vmem()] + [vmem()] * len(extra) + [pl.BlockSpec(memory_space=pl.ANY)] * len(slots),
        out_specs=[vmem()] * n_out,
        scratch_shapes=[
            pltpu.VMEM(right_shape, bf),
            pltpu.VMEM(((half - main) * max(parts, 1), 2 * TI, LANES), bf),
            pltpu.VMEM(acc_shape, bf),
            pltpu.SemaphoreType.DMA(sems),
        ],
        compiler_params=grant(12 if len(right_shape) > 3 else 6),
        cost_estimate=pl.CostEstimate(flops=half * TI * TI * J * 4, bytes_accessed=main * TI * LANES * 16, transcendentals=0),
    )(pos, lk, lr, *extra, *slots)


def add_group(C, TI, own, other, sub, sc, quads):
    half = C // 2
    pairs = half // 2
    cols = 4 * TI
    spare = LANES - cols
    lanes = lane_index((TI, LANES))

    def total(refs, r):
        x = refs[0][r].astype(jnp.float32) + refs[1][r].astype(jnp.float32)
        return x.astype(jnp.bfloat16).astype(jnp.float32)

    def unpack(count, rows):
        parts, main = packing(count, cols)
        if not parts:
            return [rows(r) for r in range(count)]
        tails = count - main
        out = [rows(r) for r in range(main)]
        for q in range(tails):
            tail = jnp.zeros((TI, LANES), jnp.float32)
            for t in range(parts):
                part = (lanes >= spare * t) & (lanes < spare * (t + 1))
                tail = jnp.where(part, pltpu.roll(out[t * tails + q], LANES - cols + spare * t, 1), tail)
            out.append(tail)
        return out

    for k, (refs, base) in enumerate(((own, sub * pairs), (other, (1 - sub) * pairs))):

        def put(q, x, base=base):
            sc[pl.ds((base + q) * TI, TI), :] = x

        if not quads:
            size = refs[0][0].shape[0]
            for q, x in enumerate(unpack(pairs, lambda r, refs=refs: total(refs[r // size], r % size))):
                put(q, x)
        else:
            swap = sub == (0 if k else 1)
            left = lax.rem(lanes, 2 * TI) < TI
            a, b = (unpack(pairs // 2, lambda r, refs=refs, u=u: total(refs[u], r)) for u in range(2))
            for q in range(pairs // 2):
                x = jnp.where(swap, b[q], a[q])
                y = jnp.where(swap, a[q], b[q])
                put(q, jnp.where(left, x, pltpu.roll(y, TI, 1)))
                put(q + pairs // 2, jnp.where(left, pltpu.roll(x, LANES - TI, 1), y))


def group_updates(C, TI, sc, nts, wx_ref, emit):
    span = 2 * TI
    pairs = C // 4
    low = lane_index((C // 2, LANES)) < span
    for h in range(TI // 2):
        a = sc[pl.ds(2 * h, C // 2, stride=TI), :]
        b = sc[pl.ds(2 * h + 1, C // 2, stride=TI), :]
        x = jnp.where(low, a, pltpu.roll(b, span, 1))
        y = jnp.where(low, pltpu.roll(a, LANES - span, 1), b)
        tri = jnp.concatenate([x[:pairs], y[:pairs], x[pairs:], y[pairs:]], axis=0)
        nts[h // 2, :, h % 2 * LANES : (h % 2 + 1) * LANES] = standardize_columns(tri).astype(jnp.bfloat16)
    wx = wx_ref[...]
    for g in range(TI // 4):
        update = lax.dot_general(wx, nts[g], (((1,), (0,)), ((), ())), preferred_element_type=jnp.float32)
        for k in range(2):
            x = update[:, k * LANES : (k + 1) * LANES].T
            emit(4 * g + 2 * k, x[:span])
            emit(4 * g + 2 * k + 1, x[span : 2 * span])


def lower_half_first(pos_ref):
    home = pos_ref[1] == pos_ref[0] // 2
    odd = lax.rem(pos_ref[0], 2) == 1
    return jnp.where(home, jnp.logical_not(odd), odd)


def finish_early_kernel(pos_ref, a_ref, b_ref, c_ref, d_ref, mid_ref, gate_ref, wx_ref, out_ref, m_ref, g_ref, sc, nts):
    TI, C, _ = mid_ref.shape
    span = 2 * TI
    first = lower_half_first(pos_ref)
    add_group(C, TI, [(a_ref, b_ref)], [(c_ref, d_ref)], pos_ref[2], sc, False)

    def emit(i, update):
        mid = mid_ref[i].astype(jnp.float32).T
        gate = gate_ref[i].astype(jnp.float32).T
        m1, m2 = mid[:span], mid[span:]
        g1, g2 = gate[:span], gate[span:]
        out_ref[i] = (jnp.where(first, m1, m2) + jnp.where(first, g1, g2) * update).astype(jnp.bfloat16)
        m_ref[i] = jnp.where(first, m2, m1).astype(jnp.bfloat16)
        g_ref[i] = jnp.where(first, g2, g1).astype(jnp.bfloat16)

    group_updates(C, TI, sc, nts, wx_ref, emit)


def finish_late_kernel(pos_ref, *refs):
    pieces, (early_ref, m_ref, g_ref, wx_ref, out_ref, sc, nts) = refs[:8], refs[8:]
    TI, span, C = early_ref.shape
    first = lower_half_first(pos_ref)
    home = pos_ref[1] == pos_ref[0] // 2
    args = (C, TI, [pieces[0:2], pieces[2:4]], [pieces[4:6], pieces[6:8]], pos_ref[2], sc)
    pl.when(home)(lambda: add_group(*args, False))
    pl.when(jnp.logical_not(home))(lambda: add_group(*args, True))

    def emit(i, update):
        late = m_ref[i].astype(jnp.float32) + g_ref[i].astype(jnp.float32) * update
        early = early_ref[i].astype(jnp.float32)
        out_ref[i, :span] = jnp.where(first, early, late).astype(jnp.bfloat16)
        out_ref[i, span:] = jnp.where(first, late, early).astype(jnp.bfloat16)

    group_updates(C, TI, sc, nts, wx_ref, emit)


def finish_group(kernel, shapes, C, TI, *args):
    return pl.pallas_call(
        kernel,
        out_shape=[jax.ShapeDtypeStruct(x, jnp.bfloat16) for x in shapes],
        in_specs=[smem()] + [vmem()] * (len(args) - 1),
        out_specs=[vmem()] * len(shapes),
        scratch_shapes=[pltpu.VMEM((C // 2 * TI, LANES), jnp.float32), pltpu.VMEM((TI // 4, C, 2 * LANES), jnp.bfloat16)],
        compiler_params=grant(8),
        cost_estimate=pl.CostEstimate(flops=2 * C * C * TI * 2 * TI, bytes_accessed=TI * TI * C * 20, transcendentals=0),
    )(*args)


def shift(x, axis, d):
    n = lax.axis_size(axis)
    return lax.ppermute(x, axis, [(i, (i + d) % n) for i in range(n)])


def step_along(x, axis, d, t):
    n = lax.axis_size(axis)
    return lax.ppermute(x, axis, [(i, i + d) for i in range(n) if 0 <= i + d < n and 0 <= i - d * (t - 1) < n])


def across(x, d):
    nc = lax.axis_size("col")
    return lax.ppermute(x, ("col", "sub"), [(c * 2 + s, (c + d) % nc * 2 + 1 - s) for c in range(nc) for s in range(2)])


def per_device(
    homolog_activations,
    edge_activations,
    first_projection_matrix,
    second_projection_matrix,
    tensor_product_matrix,
    multiplicative_entry_matrix,
    multiplicative_exit_matrix,
):
    seqs, residues, features = homolog_activations.shape
    tile_rows, tile_cols, width = edge_activations.shape
    fw = first_projection_matrix.shape[1]
    nr, nc, ns = (lax.axis_size(a) for a in ("row", "col", "sub"))
    assert ns == 2
    row, col, sub = (lax.axis_index(a) for a in ("row", "col", "sub"))
    pos = jnp.stack([row, col, sub]).astype(jnp.int32)
    sub_id = pos[2:]
    m = tile_cols // residues

    left, right = (
        x.reshape(seqs, residues * fw)
        for x in factors(homolog_activations.reshape(seqs * residues, features), first_projection_matrix, second_projection_matrix)
    )
    span = tile_rows * fw
    fast = nr == 4 and nc == 2
    if fast:
        hops = []
        for d, x in ((3, jnp.stack([right, left])), (2, right), (1, right)):
            hops.append(lax.ppermute(x, "row", [(i, i ^ d) for i in range(nr)]))
        left_x = shift(left, "col", 1)
        outer_weight, entry, exit_matrix = weights(tensor_product_matrix, multiplicative_entry_matrix, multiplicative_exit_matrix, fw)
        rows = jnp.stack([right, hops[2], hops[1], hops[0][0]])

        def rows_of(c):
            return [lax.dynamic_index_in_dim(rows, row ^ (c * m + t), 0, keepdims=False) for t in range(m)]

        got = shift(jnp.stack(rows_of(1 - col) + [hops[0][1]]), "col", 1)
        rights = jnp.stack([jnp.stack(rows_of(col)), got[:m]])
        lefts = jnp.stack([jnp.concatenate([left, left_x], axis=0), jnp.concatenate([hops[0][1], got[m]], axis=0)])
        far_edges = lax.ppermute(edge_activations, "row", [(0, nr - 1), (nr - 1, 0)])
        rights_other = shift(rights, "sub", 1)
        left_own = lax.dynamic_slice_in_dim(lefts, sub * span, span, 2)
        left_other = shift(lax.dynamic_slice_in_dim(lefts, (1 - sub) * span, span, 2), "sub", 1)
        right_t = prep(rights, rights_other, fw)
        mid, gate, lk, ls, rk, rs = pair(pos, left_own, left_other, 0, right_t, outer_weight, edge_activations, entry, tile_rows)
        outer = [(i, i ^ 1) for i in range(nr)]
        inner = [(1, 2), (2, 1)]
        outward = [(1, 0), (2, 3)]

        def along(x, pairs):
            return lax.ppermute(x, "row", pairs)

        near, mids = [along(rk, outer)], [along(rk, inner)]
        rr = shift(rs, "sub", 1)
        near, mids = near + [along(rr, outer)], mids + [along(rr, inner)]
        lr = shift(ls, "sub", 1)
        far_k, far_s = pair(pos, left_own, left_other, 1, right_t, outer_weight, far_edges, entry, tile_rows, nr - 1)
        last_in, last_out = [along(near[0], inner)], [along(mids[0], outward)]
        last_in, last_out = last_in + [along(near[1], inner)], last_out + [along(mids[1], outward)]
        far = [far_k, shift(far_s, "sub", 1)]
        rows, pairs = rk.shape[0], packing(width // 4, 4 * tile_rows)[1]
        shards = (3, 2, rows, tile_rows, LANES)
        acc = (3, pairs, 2 * tile_rows, LANES)
        send1, send1o, keep1, keep1o, rest, resto = products(early_kernel, shards, acc, (3, 2), 6, pos, lk, lr, [], [rk, rr, *near, *mids, *far], tile_cols, nr)
        got1, got1o, keep1o = shift(send1, "col", 1), across(send1o, 1), shift(keep1o, "sub", 1)
        group = (tile_rows, 2 * tile_rows, width)
        done1, mid2, gate2 = finish_group(finish_early_kernel, [group] * 3, width, tile_rows, pos, keep1, got1, keep1o, got1o, mid, gate, exit_matrix)
        own, other = [], []
        acc = (pairs // 2, 2 * tile_rows, LANES)
        for u in range(2):
            kernel = functools.partial(late_kernel, u)
            send, sendo, keep, keepo = products(kernel, rk.shape, acc, (1,), 4, pos, lk, lr, [rest, resto], [last_in[u], last_out[u]], tile_cols, nr)
            own += [keep, shift(send, "col", 1)]
            other += [shift(keepo, "sub", 1), across(sendo, 1)]
        return finish_group(finish_late_kernel, [edge_activations.shape], width, tile_rows, pos, *own, *other, done1, mid2, gate2, exit_matrix)[0]

    outer_weight, entry, exit_matrix = weights(tensor_product_matrix, multiplicative_entry_matrix, multiplicative_exit_matrix, fw)
    rows = jnp.stack([right] + [shift(right, "row", d) for d in range(1, nr)])

    def rows_of(c):
        return jnp.stack([lax.dynamic_index_in_dim(rows, lax.rem(row - (c * m + t) + nr, nr), 0, keepdims=False) for t in range(m)])

    rights, lefts = [rows_of(col)], [left]
    for d in range(1, nc):
        rights.append(shift(rows_of(lax.rem(col + d, nc)), "col", d))
        lefts.append(shift(left, "col", d))
    rights = jnp.stack(rights)
    lefts = jnp.concatenate(lefts, axis=0)[None]
    rights_other = shift(rights, "sub", 1)
    left_own = lax.dynamic_slice_in_dim(lefts, sub * span, span, 2)
    left_other = shift(lax.dynamic_slice_in_dim(lefts, (1 - sub) * span, span, 2), "sub", 1)
    right_t = prep(rights, rights_other, fw)
    mid, gate, lk, ls, rk, rs = pair(pos, left_own, left_other, 0, right_t, outer_weight, edge_activations, entry, tile_rows)

    rr = shift(rs, "sub", 1)
    lr = shift(ls, "sub", 1)
    slots = [rk, rr]
    up, down = [rk, rr], [rk, rr]
    for t in range(1, nr):
        up = [step_along(x, "row", 1, t) for x in up]
        down = [step_along(x, "row", -1, t) for x in down]
        slots += up + down
    partial = triangle(pos, lk, lr, slots, nr, nc, m, tile_cols)

    own, other = [partial[0]], [shift(partial[1], "sub", 1)]
    for d in range(1, nc):
        own.append(shift(partial[2 * d], "col", d))
        other.append(across(partial[2 * d + 1], d))
    return final(sub_id, own, other, mid, gate, exit_matrix)


def solution(mesh):
    in_specs = (
        P(("grp", "col", "sub"), "row", None),
        P(("grp", "row", "sub"), "col", None),
        P(),
        P(),
        P(),
        P(),
        P(),
    )
    out_specs = P(("grp", "row", "sub"), "col", None)

    return jax.shard_map(per_device, mesh=mesh, in_specs=in_specs, out_specs=out_specs, check_vma=False)
```

```python
import functools

import jax
import jax.numpy as jnp
from jax import lax
from jax.experimental import pallas as pl
from jax.experimental.pallas import tpu as pltpu
from jax.sharding import PartitionSpec as P


EPSILON = 1e-05
LANES = 128
VMEM_LIMIT = 60 * 1024 * 1024


def grant(mib):
    return pltpu.CompilerParams(vmem_limit_bytes=mib * 1024 * 1024)


def standardize_features(values):
    centred = values - jnp.mean(values, axis=-1, keepdims=True)
    spread = jnp.mean(centred * centred, axis=-1, keepdims=True)
    return centred * lax.rsqrt(spread + EPSILON)


def standardize_columns(values):
    centred = values - jnp.mean(values, axis=0, keepdims=True)
    spread = jnp.mean(centred * centred, axis=0, keepdims=True)
    return centred * lax.rsqrt(spread + EPSILON)


def vmem():
    return pl.BlockSpec(memory_space=pltpu.VMEM)


def smem():
    return pl.BlockSpec(memory_space=pltpu.SMEM)


def packing(count, cols):
    spare = -cols % LANES
    if spare and cols < LANES and cols % spare == 0:
        parts = cols // spare
        if count % (parts + 1) == 0:
            return parts, count // (parts + 1) * parts
    return 0, count


def lane_index(shape):
    return lax.broadcasted_iota(jnp.int32, shape, len(shape) - 1)


def factors_kernel(x_ref, both_ref, left_ref, right_ref):
    rows = x_ref.shape[0]
    fw = left_ref.shape[1]
    step = rows // 8 if rows % 128 == 0 else rows
    for t in range(rows // step):
        part = slice(t * step, (t + 1) * step)
        normed = standardize_features(x_ref[part, :].astype(jnp.float32)).astype(jnp.bfloat16)
        for k, out_ref in enumerate((right_ref, left_ref)):
            matrix = both_ref[k * fw : (k + 1) * fw, :]
            out = lax.dot_general(normed, matrix, (((1,), (1,)), ((), ())), preferred_element_type=jnp.float32)
            out_ref[part, :] = out.astype(jnp.bfloat16)


def factors(x, first, second):
    shape = jax.ShapeDtypeStruct((x.shape[0], first.shape[1]), jnp.bfloat16)
    return pl.pallas_call(
        factors_kernel,
        out_shape=[shape, shape],
        in_specs=[vmem()] * 2,
        out_specs=[vmem()] * 2,
        compiler_params=grant(6),
    )(x, jnp.concatenate([second.T, first.T], axis=0))


def weights_kernel(fw, w_ref, n_ref, x_ref, wt_ref, nt_ref, xt_ref, sc, st):
    C = w_ref.shape[1]
    sc[...] = w_ref[...].astype(jnp.float32)
    for b in range(fw):
        st[b * fw : (b + 1) * fw, :] = sc[pl.ds(b, fw, stride=fw), :]
    for t in range(fw * fw // C):
        wt_ref[:, t * C : (t + 1) * C] = st[t * C : (t + 1) * C, :].T.astype(jnp.bfloat16)
    for t in range(n_ref.shape[1] // C):
        nt_ref[t * C : (t + 1) * C, :] = n_ref[:, t * C : (t + 1) * C].astype(jnp.float32).T.astype(jnp.bfloat16)
    xt_ref[...] = x_ref[...].astype(jnp.float32).T.astype(jnp.bfloat16)


def weights(w, n, x, fw):
    K, C = w.shape
    bf = jnp.bfloat16
    return pl.pallas_call(
        functools.partial(weights_kernel, fw),
        out_shape=[jax.ShapeDtypeStruct((C, K), bf), jax.ShapeDtypeStruct(n.shape[::-1], bf), jax.ShapeDtypeStruct(x.shape[::-1], bf)],
        in_specs=[vmem()] * 3,
        out_specs=[vmem()] * 3,
        scratch_shapes=[pltpu.VMEM((K, C), jnp.float32)] * 2,
        compiler_params=grant(4),
    )(w, n, x)


def prep_kernel(fw, own_ref, recv_ref, rt_ref, sc):
    groups, m, seqs, row_lanes = own_ref.shape
    res = row_lanes // fw
    chunk = sc.shape[2]
    pieces = [(ref, g) for ref in (own_ref, recv_ref) for g in range(groups)]
    per = chunk // seqs
    for u in range(len(pieces) // per):
        for mm in range(m):
            for t in range(row_lanes // LANES):
                block = jnp.concatenate(
                    [ref[g, mm, :, t * LANES : (t + 1) * LANES].astype(jnp.float32) for ref, g in pieces[u * per : (u + 1) * per]], axis=0
                )
                start = mm * row_lanes + t * LANES
                sc[u, start : start + LANES, :] = block.T
        for b in range(fw):
            rt_ref[b, :, u * chunk : (u + 1) * chunk] = sc[u, pl.ds(b, m * res, stride=fw), :].astype(jnp.bfloat16)


def prep(own, recv, fw):
    groups, m, seqs, row_lanes = own.shape
    total = 2 * groups * seqs
    chunk = min(total, LANES)
    cols = m * row_lanes // fw
    return pl.pallas_call(
        functools.partial(prep_kernel, fw),
        out_shape=jax.ShapeDtypeStruct((fw, cols, total), jnp.bfloat16),
        in_specs=[vmem(), vmem()],
        out_specs=vmem(),
        scratch_shapes=[pltpu.VMEM((total // chunk, m * row_lanes, chunk), jnp.float32)],
        compiler_params=grant(8),
    )(own, recv)


def pair_kernel(cfg, pos_ref, *refs):
    last = cfg[5]
    if last:
        pl.when((pos_ref[0] == 0) | (pos_ref[0] == last))(lambda: pair_body(cfg, pos_ref, *refs))
    else:
        pair_body(cfg, pos_ref, *refs)


def pair_body(cfg, pos_ref, l_ref, lr_ref, rt_ref, wt_ref, e_ref, went_ref, *rest):
    fw, C, J, S, full, _ = cfg
    if full:
        mid_ref, gate_ref, lk_ref, ls_ref, rk_ref, rs_ref, lt, ot, nts, lsc, rsc = rest
    else:
        rk_ref, rs_ref, lt, ot, nts, rsc = rest
    half = C // 2
    IG = l_ref.shape[1] // fw
    wide = ot.shape[2] // 2
    for t in range(IG * fw // LANES):
        part = slice(t * LANES, (t + 1) * LANES)
        block = jnp.concatenate([l_ref[:, part].astype(jnp.float32), lr_ref[:, part].astype(jnp.float32)], axis=0)
        lt[part, :] = block.T.astype(jnp.bfloat16)
    ltv = lt[...]
    for b in range(fw):
        o = lax.dot_general(ltv, rt_ref[b], (((1,), (1,)), ((), ())), preferred_element_type=jnp.float32).astype(jnp.bfloat16)
        for i in range(IG):
            ot[i // 2, b * fw : (b + 1) * fw, i % 2 * wide : i % 2 * wide + J] = o[i * fw : (i + 1) * fw, :]
    wt = wt_ref[...]
    for h in range(IG // 2):
        pt = lax.dot_general(wt, ot[h], (((1,), (0,)), ((), ())), preferred_element_type=jnp.float32)
        for k in range(2):
            i = 2 * h + k
            et = e_ref[i].astype(jnp.float32).T
            mid = (et + pt[:, k * wide : k * wide + J] * (1.0 / S)).astype(jnp.bfloat16)
            if full:
                mid_ref[i] = mid
            nts[h, :, k * wide : k * wide + J] = standardize_columns(mid.astype(jnp.float32)).astype(jnp.bfloat16)

    def project(first, count, h):
        return lax.dot_general(went_ref[first * C : (first + count) * C, :], nts[h], (((1,), (0,)), ((), ())), preferred_element_type=jnp.float32)

    for h in range(IG // 2):
        if full:
            p = project(0, 2, h)
            x = jax.nn.sigmoid(p[C:]) * p[:C]
            for k in range(2):
                lsc[pl.ds((2 * h + k) * C, C), :J] = x[:, k * wide : k * wide + J]
        p = project(2, 2, h)
        x = jax.nn.sigmoid(p[C:]) * p[:C]
        for k in range(2):
            rsc[pl.ds((2 * h + k) * C, C), :J] = x[:, k * wide : k * wide + J]
        if full:
            x = jax.nn.sigmoid(project(4, 1, h)).astype(jnp.bfloat16)
            for k in range(2):
                gate_ref[2 * h + k] = x[:, k * wide : k * wide + J]
    sub = pos_ref[2]
    parts, main = packing(half, J)
    inside = lane_index((IG, LANES)) < J
    if full:
        for ref, base in ((lk_ref, sub * half), (ls_ref, (1 - sub) * half)):
            for ch in range(half):
                x = lsc[pl.ds(base + ch, IG, stride=C), :]
                ref[ch] = jnp.where(inside, x, 0.0).astype(jnp.bfloat16)
    for ref, base in ((rk_ref, sub * half), (rs_ref, (1 - sub) * half)):
        if parts == 0:
            for ch in range(half):
                x = rsc[pl.ds(base + ch, IG, stride=C), :]
                ref[ch] = jnp.where(inside, x, 0.0).astype(jnp.bfloat16)
        else:
            tails = half - main
            spare = LANES - J
            for q in range(tails):
                tail = rsc[pl.ds(base + main + q, IG, stride=C), :]
                for t in range(parts):
                    x = rsc[pl.ds(base + t * tails + q, IG, stride=C), :]
                    moved = pltpu.roll(tail, J - spare * t, 1)
                    ref[t * tails + q] = jnp.where(inside, x, moved).astype(jnp.bfloat16)


def pair(pos, l, lr, which, rt, wt, e, went, IG, last=0):
    full = not last
    _, part, IA = l.shape
    S = 2 * part
    fw, J, _ = rt.shape
    TI = IA // fw
    C = wt.shape[0]
    half = C // 2
    rows = packing(half, J)[1]
    wide = -(-J // LANES) * LANES
    bf = jnp.bfloat16
    tile = (jax.ShapeDtypeStruct((TI, C, J), bf), pl.BlockSpec((IG, C, J), lambda g: (g, 0, 0)))
    lefts = (jax.ShapeDtypeStruct((half, TI, LANES), bf), pl.BlockSpec((half, IG, LANES), lambda g: (0, g, 0)))
    rights = (jax.ShapeDtypeStruct((rows, TI, LANES), bf), pl.BlockSpec((rows, IG, LANES), lambda g: (0, g, 0)))
    outs = ([tile] * 2 + [lefts] * 2 if full else []) + [rights] * 2
    gated = pltpu.VMEM((IG * C, LANES), jnp.float32)
    f = pl.pallas_call(
        functools.partial(pair_kernel, (fw, C, J, S, full, last)),
        grid=(TI // IG,),
        out_shape=[o[0] for o in outs],
        in_specs=[
            smem(),
            pl.BlockSpec((None, part, IG * fw), lambda g: (which, 0, g)),
            pl.BlockSpec((None, part, IG * fw), lambda g: (which, 0, g)),
            pl.BlockSpec((fw, J, S), lambda g: (0, 0, 0)),
            pl.BlockSpec(wt.shape, lambda g: (0, 0)),
            pl.BlockSpec((IG, J, C), lambda g: (g, 0, 0)),
            pl.BlockSpec(went.shape, lambda g: (0, 0)),
        ],
        out_specs=[o[1] for o in outs],
        scratch_shapes=[
            pltpu.VMEM((IG * fw, S), bf),
            pltpu.VMEM((IG // 2, fw * fw, 2 * wide), bf),
            pltpu.VMEM((IG // 2, C, 2 * wide), bf),
            gated,
        ]
        + ([gated] if full else []),
        compiler_params=grant(28),
        cost_estimate=pl.CostEstimate(flops=2 * TI * J * (S * fw * fw + fw * fw * C + 5 * C * C), bytes_accessed=4 * TI * J * C * 6, transcendentals=TI * J * C * 3),
    )
    return f(pos, l, lr, rt, wt, e, went)


def tri_kernel(cfg, n_slots, pos_ref, lk_ref, lr_ref, *rest):
    nr, nc, m, J = cfg
    slots = rest[:n_slots]
    outs = rest[n_slots : n_slots + 2 * nc]
    rv, lm, sem = rest[n_slots + 2 * nc :]
    half, TI, _ = lk_ref.shape
    row, col, sub = pos_ref[0], pos_ref[1], pos_ref[2]
    parts, main = packing(half, J)
    tails = half - main
    spare = LANES - J

    def copy(index):
        step, u = index // 2, index % 2
        hop = (step + 1) // 2
        origin = row - hop if step % 2 else row + hop
        return origin, pltpu.make_async_copy(slots[index], rv.at[jnp.clip(origin, 0, nr - 1), sub if u == 0 else 1 - sub], sem.at[index])

    for index in range(n_slots):
        origin, c = copy(index)

        @pl.when((origin >= 0) & (origin < nr))
        def _(c=c):
            c.start()

    inside = lane_index((2 * TI, LANES)) < J
    for ch in range(half):
        x = jnp.concatenate([lk_ref[ch], lr_ref[ch]], axis=0)
        if ch < main:
            lm[ch] = x
        else:
            f = x.astype(jnp.float32)
            for t in range(parts):
                moved = pltpu.roll(f, J - spare * t, 1)
                lm[main + (ch - main) * parts + t] = jnp.where(inside, 0.0, moved).astype(jnp.bfloat16)

    for index in range(n_slots):
        origin, c = copy(index)

        @pl.when((origin >= 0) & (origin < nr))
        def _(c=c):
            c.wait()

    def block(ch, start, pieces):
        right = rv[pl.ds(start, m), :, ch].reshape(m * 2 * TI, LANES)
        return lax.dot_general(lm[pieces], right, (((1,), (1,)), ((), ())), preferred_element_type=jnp.float32)

    for dc in range(nc):
        start = lax.rem(col + dc, nc) * m
        own_ref, other_ref = outs[2 * dc], outs[2 * dc + 1]
        for q in range(tails if parts else 0):
            tail = 0.0
            for t in range(parts):
                tail = tail + block(t * tails + q, start, main + q * parts + t)
            tail = jnp.concatenate([tail, jnp.zeros((2 * TI, spare), jnp.float32)], axis=1)
            for t in range(parts):
                x = block(t * tails + q, start, t * tails + q)
                x = jnp.concatenate([x, jnp.zeros((2 * TI, spare), jnp.float32)], axis=1)
                x = jnp.where(inside, x, pltpu.roll(tail, J - spare * t, 1)).astype(jnp.bfloat16)
                own_ref[t * tails + q] = x[:TI]
                other_ref[t * tails + q] = x[TI:]
        if not parts:
            for ch in range(half):
                x = block(ch, start, ch)
                if spare:
                    x = jnp.concatenate([x, jnp.zeros((2 * TI, spare), jnp.float32)], axis=1)
                x = x.astype(jnp.bfloat16)
                own_ref[ch] = x[:TI]
                other_ref[ch] = x[TI:]


def triangle(pos, lk, lr, slots, nr, nc, m, J):
    half, TI, _ = lk.shape
    parts, main = packing(half, J)
    rows = main
    bf = jnp.bfloat16
    n = len(slots)
    return pl.pallas_call(
        functools.partial(tri_kernel, (nr, nc, m, J), n),
        out_shape=[jax.ShapeDtypeStruct((rows, TI, LANES), bf)] * (2 * nc),
        in_specs=[smem(), vmem(), vmem()] + [pl.BlockSpec(memory_space=pl.ANY)] * n,
        out_specs=[vmem()] * (2 * nc),
        scratch_shapes=[
            pltpu.VMEM((nr, 2, rows, TI, LANES), bf),
            pltpu.VMEM((main + (half - main) * max(parts, 1), 2 * TI, LANES), bf),
            pltpu.SemaphoreType.DMA((n,)),
        ],
        compiler_params=pltpu.CompilerParams(vmem_limit_bytes=VMEM_LIMIT),
    )(pos, lk, lr, *slots)


def finish(sc, nts, mid_ref, gate_ref, wx_ref, out_ref):
    TI, C, J = mid_ref.shape
    wide = nts.shape[2] // 2
    wx = wx_ref[...]
    for i in range(TI):
        tri = sc[pl.ds(i, C, stride=TI), :][:, :J]
        nts[i // 2, :, i % 2 * wide : i % 2 * wide + J] = standardize_columns(tri).astype(jnp.bfloat16)
    for h in range(TI // 2):
        update = lax.dot_general(wx, nts[h], (((1,), (0,)), ((), ())), preferred_element_type=jnp.float32)
        for k in range(2):
            i = 2 * h + k
            res = mid_ref[i].astype(jnp.float32) + gate_ref[i].astype(jnp.float32) * update[:, k * wide : k * wide + J]
            out_ref[i] = res.T.astype(jnp.bfloat16)


def final_kernel(cfg, n, sub_ref, *rest):
    C, J = cfg
    own = rest[:n]
    other = rest[n : 2 * n]
    mid_ref, gate_ref, wx_ref, out_ref, sc, nts = rest[2 * n :]
    TI = mid_ref.shape[0]
    half = C // 2
    parts, main = packing(half, J)
    tails = half - main
    spare = LANES - J
    sub = sub_ref[0]
    lanes = lane_index((TI, LANES))
    for refs, base in ((own, sub * half), (other, (1 - sub) * half)):
        def total(ch, refs=refs):
            x = refs[0][ch].astype(jnp.float32)
            for ref in refs[1:]:
                x = x + ref[ch].astype(jnp.float32)
            return x.astype(jnp.bfloat16).astype(jnp.float32)

        for q in range(tails if parts else 0):
            tail = jnp.zeros((TI, LANES), jnp.float32)
            for t in range(parts):
                x = total(t * tails + q)
                sc[pl.ds((base + t * tails + q) * TI, TI), :] = x
                tail = jnp.where((lanes >= spare * t) & (lanes < spare * (t + 1)), pltpu.roll(x, LANES - J + spare * t, 1), tail)
            sc[pl.ds((base + main + q) * TI, TI), :] = tail
        if not parts:
            for ch in range(half):
                sc[pl.ds((base + ch) * TI, TI), :] = total(ch)
    finish(sc, nts, mid_ref, gate_ref, wx_ref, out_ref)


def final(sub, own, other, mid, gate, wx):
    TI, C, J = mid.shape
    n = len(own)
    return pl.pallas_call(
        functools.partial(final_kernel, (C, J), n),
        out_shape=jax.ShapeDtypeStruct((TI, J, C), jnp.bfloat16),
        in_specs=[smem()] + [vmem()] * (2 * n + 3),
        out_specs=vmem(),
        scratch_shapes=[pltpu.VMEM((C * TI, LANES), jnp.float32), pltpu.VMEM((TI // 2, C, 2 * LANES), jnp.bfloat16)],
        compiler_params=pltpu.CompilerParams(vmem_limit_bytes=VMEM_LIMIT),
    )(sub, *own, *other, mid, gate, wx)


def masked_left(lk_ref, lr_ref, lm, J):
    half, TI, _ = lk_ref.shape
    parts, main = packing(half, J)
    spare = LANES - J
    inside = lane_index((2 * TI, LANES)) < J
    for ch in range(main, half):
        f = jnp.concatenate([lk_ref[ch], lr_ref[ch]], axis=0).astype(jnp.float32)
        for t in range(parts):
            moved = pltpu.roll(f, J - spare * t, 1)
            lm[(ch - main) * parts + t] = jnp.where(inside, 0.0, moved).astype(jnp.bfloat16)


def shard_products(lk_ref, lr_ref, lm, right, ways, J, half, TI, store):
    parts, main = packing(half, J)
    tails = half - main

    def dot(left, row):
        return lax.dot_general(left, right(row), (((1,), (1,)), ((), ())), preferred_element_type=jnp.float32)

    def channel(ch):
        if ch < main:
            return dot(jnp.concatenate([lk_ref[ch], lr_ref[ch]], axis=0), ch)
        q = ch - main
        x = dot(lm[q * parts], q)
        for t in range(1, parts):
            x = x + dot(lm[q * parts + t], t * tails + q)
        return x

    count = half // ways
    cols = 4 * TI
    pad = jnp.zeros((2 * TI, LANES - cols), jnp.float32)
    p2, m2 = packing(count, cols)
    t2 = count - m2

    def beside(q):
        return jnp.concatenate([channel(q + w * count) for w in range(ways)] + [pad], axis=1)

    inside = lane_index((2 * TI, LANES)) < cols
    spare = LANES - cols
    for q in range(t2):
        tail = beside(m2 + q)
        for t in range(p2):
            store(t * t2 + q, jnp.where(inside, beside(t * t2 + q), pltpu.roll(tail, cols - spare * t, 1)).astype(jnp.bfloat16))
    for q in range(0 if p2 else count):
        store(q, beside(q).astype(jnp.bfloat16))


def early_kernel(J, n, pos_ref, lk_ref, lr_ref, *rest):
    own, near, mids, far = rest[0:2], rest[2:4], rest[4:6], rest[6:8]
    outs = rest[8:14]
    rv, lm, acc, sem = rest[14:]
    half, TI, _ = lk_ref.shape
    row, col, sub = pos_ref[0], pos_ref[1], pos_ref[2]
    edge = (row == 0) | (row == n - 1)
    plan = [(None, own, 0), (None, near, 1), (edge, far, 2), (jnp.logical_not(edge), mids, 2)]

    def each(action):
        for cond, refs, k in plan:
            for u in range(2):
                c = pltpu.make_async_copy(refs[u], rv.at[k, sub if u == 0 else 1 - sub], sem.at[k, u])
                if cond is None:
                    action(c)
                else:
                    pl.when(cond)(lambda c=c: action(c))

    each(lambda c: c.start())
    masked_left(lk_ref, lr_ref, lm, J)
    each(lambda c: c.wait())
    for k in range(3):

        def store(r, x, k=k):
            acc[k, r] = x

        shard_products(lk_ref, lr_ref, lm, lambda r, k=k: rv[k, :, r].reshape(2 * TI, LANES), 2, J, half, TI, store)
    home = col == row // 2
    send = jnp.where(home, acc[2], acc[0])
    keep = jnp.where(home, acc[0], acc[2])
    for u in range(2):
        outs[u][...] = send[:, u * TI : (u + 1) * TI]
        outs[2 + u][...] = keep[:, u * TI : (u + 1) * TI]
        outs[4 + u][...] = acc[1, :, u * TI : (u + 1) * TI]


def late_kernel(u, J, n, pos_ref, lk_ref, lr_ref, a_ref, b_ref, inner, outward, *rest):
    outs = rest[:4]
    rv, lm, acc, sem = rest[4:]
    half, TI, _ = lk_ref.shape
    row, col = pos_ref[0], pos_ref[1]
    edge = (row == 0) | (row == n - 1)

    def each(action):
        for cond, ref in ((edge, outward), (jnp.logical_not(edge), inner)):
            c = pltpu.make_async_copy(ref, rv, sem.at[0])
            pl.when(cond)(lambda c=c: action(c))

    each(lambda c: c.start())
    masked_left(lk_ref, lr_ref, lm, J)
    each(lambda c: c.wait())

    def store(r, x):
        acc[r] = x

    shard_products(lk_ref, lr_ref, lm, lambda r: rv[r], 4, J, half, TI, store)
    home = col == row // 2
    count = acc.shape[0]
    for k, ref in enumerate((a_ref, b_ref)):
        late = acc[:, k * TI : (k + 1) * TI]
        early = ref[u * count : (u + 1) * count]
        outs[k][...] = jnp.where(home, late, early)
        outs[2 + k][...] = jnp.where(home, early, late)


def products(kernel, right_shape, acc_shape, sems, n_out, pos, lk, lr, extra, slots, J, n):
    half, TI, _ = lk.shape
    parts, main = packing(half, J)
    bf = jnp.bfloat16
    rows = acc_shape[-3]
    return pl.pallas_call(
        functools.partial(kernel, J, n),
        out_shape=[jax.ShapeDtypeStruct((rows, TI, LANES), bf)] * n_out,
        in_specs=[smem(), vmem(), vmem()] + [vmem()] * len(extra) + [pl.BlockSpec(memory_space=pl.ANY)] * len(slots),
        out_specs=[vmem()] * n_out,
        scratch_shapes=[
            pltpu.VMEM(right_shape, bf),
            pltpu.VMEM(((half - main) * max(parts, 1), 2 * TI, LANES), bf),
            pltpu.VMEM(acc_shape, bf),
            pltpu.SemaphoreType.DMA(sems),
        ],
        compiler_params=grant(12 if len(right_shape) > 3 else 6),
        cost_estimate=pl.CostEstimate(flops=half * TI * TI * J * 4, bytes_accessed=main * TI * LANES * 16, transcendentals=0),
    )(pos, lk, lr, *extra, *slots)


def add_group(C, TI, own, other, sub, sc, quads):
    half = C // 2
    pairs = half // 2
    cols = 4 * TI
    spare = LANES - cols
    lanes = lane_index((TI, LANES))

    def total(refs, r):
        x = refs[0][r].astype(jnp.float32) + refs[1][r].astype(jnp.float32)
        return x.astype(jnp.bfloat16).astype(jnp.float32)

    def unpack(count, rows):
        parts, main = packing(count, cols)
        if not parts:
            return [rows(r) for r in range(count)]
        tails = count - main
        out = [rows(r) for r in range(main)]
        for q in range(tails):
            tail = jnp.zeros((TI, LANES), jnp.float32)
            for t in range(parts):
                part = (lanes >= spare * t) & (lanes < spare * (t + 1))
                tail = jnp.where(part, pltpu.roll(out[t * tails + q], LANES - cols + spare * t, 1), tail)
            out.append(tail)
        return out

    for k, (refs, base) in enumerate(((own, sub * pairs), (other, (1 - sub) * pairs))):

        def put(q, x, base=base):
            sc[pl.ds((base + q) * TI, TI), :] = x

        if not quads:
            size = refs[0][0].shape[0]
            for q, x in enumerate(unpack(pairs, lambda r, refs=refs: total(refs[r // size], r % size))):
                put(q, x)
        else:
            swap = sub == (0 if k else 1)
            left = lax.rem(lanes, 2 * TI) < TI
            a, b = (unpack(pairs // 2, lambda r, refs=refs, u=u: total(refs[u], r)) for u in range(2))
            for q in range(pairs // 2):
                x = jnp.where(swap, b[q], a[q])
                y = jnp.where(swap, a[q], b[q])
                put(q, jnp.where(left, x, pltpu.roll(y, TI, 1)))
                put(q + pairs // 2, jnp.where(left, pltpu.roll(x, LANES - TI, 1), y))


def group_updates(C, TI, sc, nts, wx_ref, emit):
    span = 2 * TI
    pairs = C // 4
    low = lane_index((C // 2, LANES)) < span
    for h in range(TI // 2):
        a = sc[pl.ds(2 * h, C // 2, stride=TI), :]
        b = sc[pl.ds(2 * h + 1, C // 2, stride=TI), :]
        x = jnp.where(low, a, pltpu.roll(b, span, 1))
        y = jnp.where(low, pltpu.roll(a, LANES - span, 1), b)
        tri = jnp.concatenate([x[:pairs], y[:pairs], x[pairs:], y[pairs:]], axis=0)
        nts[h // 2, :, h % 2 * LANES : (h % 2 + 1) * LANES] = standardize_columns(tri).astype(jnp.bfloat16)
    wx = wx_ref[...]
    for g in range(TI // 4):
        update = lax.dot_general(wx, nts[g], (((1,), (0,)), ((), ())), preferred_element_type=jnp.float32)
        for k in range(2):
            x = update[:, k * LANES : (k + 1) * LANES].T
            emit(4 * g + 2 * k, x[:span])
            emit(4 * g + 2 * k + 1, x[span : 2 * span])


def lower_half_first(pos_ref):
    home = pos_ref[1] == pos_ref[0] // 2
    odd = lax.rem(pos_ref[0], 2) == 1
    return jnp.where(home, jnp.logical_not(odd), odd)


def finish_early_kernel(pos_ref, a_ref, b_ref, c_ref, d_ref, mid_ref, gate_ref, wx_ref, out_ref, m_ref, g_ref, sc, nts):
    TI, C, _ = mid_ref.shape
    span = 2 * TI
    first = lower_half_first(pos_ref)
    add_group(C, TI, [(a_ref, b_ref)], [(c_ref, d_ref)], pos_ref[2], sc, False)

    def emit(i, update):
        mid = mid_ref[i].astype(jnp.float32).T
        gate = gate_ref[i].astype(jnp.float32).T
        m1, m2 = mid[:span], mid[span:]
        g1, g2 = gate[:span], gate[span:]
        out_ref[i] = (jnp.where(first, m1, m2) + jnp.where(first, g1, g2) * update).astype(jnp.bfloat16)
        m_ref[i] = jnp.where(first, m2, m1).astype(jnp.bfloat16)
        g_ref[i] = jnp.where(first, g2, g1).astype(jnp.bfloat16)

    group_updates(C, TI, sc, nts, wx_ref, emit)


def finish_late_kernel(pos_ref, *refs):
    pieces, (early_ref, m_ref, g_ref, wx_ref, out_ref, sc, nts) = refs[:8], refs[8:]
    TI, span, C = early_ref.shape
    first = lower_half_first(pos_ref)
    home = pos_ref[1] == pos_ref[0] // 2
    args = (C, TI, [pieces[0:2], pieces[2:4]], [pieces[4:6], pieces[6:8]], pos_ref[2], sc)
    pl.when(home)(lambda: add_group(*args, False))
    pl.when(jnp.logical_not(home))(lambda: add_group(*args, True))

    def emit(i, update):
        late = m_ref[i].astype(jnp.float32) + g_ref[i].astype(jnp.float32) * update
        early = early_ref[i].astype(jnp.float32)
        out_ref[i, :span] = jnp.where(first, early, late).astype(jnp.bfloat16)
        out_ref[i, span:] = jnp.where(first, late, early).astype(jnp.bfloat16)

    group_updates(C, TI, sc, nts, wx_ref, emit)


def finish_group(kernel, shapes, C, TI, *args):
    return pl.pallas_call(
        kernel,
        out_shape=[jax.ShapeDtypeStruct(x, jnp.bfloat16) for x in shapes],
        in_specs=[smem()] + [vmem()] * (len(args) - 1),
        out_specs=[vmem()] * len(shapes),
        scratch_shapes=[pltpu.VMEM((C // 2 * TI, LANES), jnp.float32), pltpu.VMEM((TI // 4, C, 2 * LANES), jnp.bfloat16)],
        compiler_params=grant(8),
        cost_estimate=pl.CostEstimate(flops=2 * C * C * TI * 2 * TI, bytes_accessed=TI * TI * C * 20, transcendentals=0),
    )(*args)


def shift(x, axis, d):
    n = lax.axis_size(axis)
    return lax.ppermute(x, axis, [(i, (i + d) % n) for i in range(n)])


def step_along(x, axis, d, t):
    n = lax.axis_size(axis)
    return lax.ppermute(x, axis, [(i, i + d) for i in range(n) if 0 <= i + d < n and 0 <= i - d * (t - 1) < n])


def across(x, d):
    nc = lax.axis_size("col")
    return lax.ppermute(x, ("col", "sub"), [(c * 2 + s, (c + d) % nc * 2 + 1 - s) for c in range(nc) for s in range(2)])


def per_device(
    homolog_activations,
    edge_activations,
    first_projection_matrix,
    second_projection_matrix,
    tensor_product_matrix,
    multiplicative_entry_matrix,
    multiplicative_exit_matrix,
):
    seqs, residues, features = homolog_activations.shape
    tile_rows, tile_cols, width = edge_activations.shape
    fw = first_projection_matrix.shape[1]
    nr, nc, ns = (lax.axis_size(a) for a in ("row", "col", "sub"))
    assert ns == 2
    row, col, sub = (lax.axis_index(a) for a in ("row", "col", "sub"))
    pos = jnp.stack([row, col, sub]).astype(jnp.int32)
    sub_id = pos[2:]
    m = tile_cols // residues

    left, right = (
        x.reshape(seqs, residues * fw)
        for x in factors(homolog_activations.reshape(seqs * residues, features), first_projection_matrix, second_projection_matrix)
    )
    span = tile_rows * fw
    fast = nr == 4 and nc == 2
    if fast:
        hops = []
        for d, x in ((3, jnp.stack([right, left])), (2, right), (1, right)):
            hops.append(lax.ppermute(x, "row", [(i, i ^ d) for i in range(nr)]))
        left_x = shift(left, "col", 1)
        outer_weight, entry, exit_matrix = weights(tensor_product_matrix, multiplicative_entry_matrix, multiplicative_exit_matrix, fw)
        rows = jnp.stack([right, hops[2], hops[1], hops[0][0]])

        def rows_of(c):
            return [lax.dynamic_index_in_dim(rows, row ^ (c * m + t), 0, keepdims=False) for t in range(m)]

        got = shift(jnp.stack(rows_of(1 - col) + [hops[0][1]]), "col", 1)
        rights = jnp.stack([jnp.stack(rows_of(col)), got[:m]])
        lefts = jnp.stack([jnp.concatenate([left, left_x], axis=0), jnp.concatenate([hops[0][1], got[m]], axis=0)])
        far_edges = lax.ppermute(edge_activations, "row", [(0, nr - 1), (nr - 1, 0)])
        rights_other = shift(rights, "sub", 1)
        left_own = lax.dynamic_slice_in_dim(lefts, sub * span, span, 2)
        left_other = shift(lax.dynamic_slice_in_dim(lefts, (1 - sub) * span, span, 2), "sub", 1)
        right_t = prep(rights, rights_other, fw)
        mid, gate, lk, ls, rk, rs = pair(pos, left_own, left_other, 0, right_t, outer_weight, edge_activations, entry, tile_rows)
        outer = [(i, i ^ 1) for i in range(nr)]
        inner = [(1, 2), (2, 1)]
        outward = [(1, 0), (2, 3)]

        def along(x, pairs):
            return lax.ppermute(x, "row", pairs)

        near, mids = [along(rk, outer)], [along(rk, inner)]
        rr = shift(rs, "sub", 1)
        near, mids = near + [along(rr, outer)], mids + [along(rr, inner)]
        lr = shift(ls, "sub", 1)
        far_k, far_s = pair(pos, left_own, left_other, 1, right_t, outer_weight, far_edges, entry, tile_rows, nr - 1)
        last_in, last_out = [along(near[0], inner)], [along(mids[0], outward)]
        last_in, last_out = last_in + [along(near[1], inner)], last_out + [along(mids[1], outward)]
        far = [far_k, shift(far_s, "sub", 1)]
        rows, pairs = rk.shape[0], packing(width // 4, 4 * tile_rows)[1]
        shards = (3, 2, rows, tile_rows, LANES)
        acc = (3, pairs, 2 * tile_rows, LANES)
        send1, send1o, keep1, keep1o, rest, resto = products(early_kernel, shards, acc, (3, 2), 6, pos, lk, lr, [], [rk, rr, *near, *mids, *far], tile_cols, nr)
        got1, got1o, keep1o = shift(send1, "col", 1), across(send1o, 1), shift(keep1o, "sub", 1)
        group = (tile_rows, 2 * tile_rows, width)
        done1, mid2, gate2 = finish_group(finish_early_kernel, [group] * 3, width, tile_rows, pos, keep1, got1, keep1o, got1o, mid, gate, exit_matrix)
        own, other = [], []
        acc = (pairs // 2, 2 * tile_rows, LANES)
        for u in range(2):
            kernel = functools.partial(late_kernel, u)
            send, sendo, keep, keepo = products(kernel, rk.shape, acc, (1,), 4, pos, lk, lr, [rest, resto], [last_in[u], last_out[u]], tile_cols, nr)
            own += [keep, shift(send, "col", 1)]
            diagonal = across(sendo, 1)
            other += [shift(keepo, "sub", 1), diagonal]
        return finish_group(finish_late_kernel, [edge_activations.shape], width, tile_rows, pos, *own, *other, done1, mid2, gate2, exit_matrix)[0]

    outer_weight, entry, exit_matrix = weights(tensor_product_matrix, multiplicative_entry_matrix, multiplicative_exit_matrix, fw)
    rows = jnp.stack([right] + [shift(right, "row", d) for d in range(1, nr)])

    def rows_of(c):
        return jnp.stack([lax.dynamic_index_in_dim(rows, lax.rem(row - (c * m + t) + nr, nr), 0, keepdims=False) for t in range(m)])

    rights, lefts = [rows_of(col)], [left]
    for d in range(1, nc):
        rights.append(shift(rows_of(lax.rem(col + d, nc)), "col", d))
        lefts.append(shift(left, "col", d))
    rights = jnp.stack(rights)
    lefts = jnp.concatenate(lefts, axis=0)[None]
    rights_other = shift(rights, "sub", 1)
    left_own = lax.dynamic_slice_in_dim(lefts, sub * span, span, 2)
    left_other = shift(lax.dynamic_slice_in_dim(lefts, (1 - sub) * span, span, 2), "sub", 1)
    right_t = prep(rights, rights_other, fw)
    mid, gate, lk, ls, rk, rs = pair(pos, left_own, left_other, 0, right_t, outer_weight, edge_activations, entry, tile_rows)

    rr = shift(rs, "sub", 1)
    lr = shift(ls, "sub", 1)
    slots = [rk, rr]
    up, down = [rk, rr], [rk, rr]
    for t in range(1, nr):
        up = [step_along(x, "row", 1, t) for x in up]
        down = [step_along(x, "row", -1, t) for x in down]
        slots += up + down
    partial = triangle(pos, lk, lr, slots, nr, nc, m, tile_cols)

    own, other = [partial[0]], [shift(partial[1], "sub", 1)]
    for d in range(1, nc):
        own.append(shift(partial[2 * d], "col", d))
        other.append(across(partial[2 * d + 1], d))
    return final(sub_id, own, other, mid, gate, exit_matrix)


def solution(mesh):
    in_specs = (
        P(("grp", "col", "sub"), "row", None),
        P(("grp", "row", "sub"), "col", None),
        P(),
        P(),
        P(),
        P(),
        P(),
    )
    out_specs = P(("grp", "row", "sub"), "col", None)

    return jax.shard_map(per_device, mesh=mesh, in_specs=in_specs, out_specs=out_specs, check_vma=False)
```
